32 devices in a mesh: seq: 4 (over z), shard: 4 (over y, core), replica: 2 (over x).
Axes of the slice: x: 2, y: 2, z: 4, core: 2. Of those that a mesh axis runs over, the one named last changes fastest.
Arguments:
- tokens: bfloat16 [8, 2048, 768], P(('shard', 'replica'), 'seq'), may hold values from -6 to 6
- prefix_len: int32 [8], P(('shard', 'replica')), may hold values from 204 to 1024
- w_qkv: bfloat16 [768, 2304], P('shard'), may hold values from -0.3125 to 0.3125
- w_out: bfloat16 [768, 768], P('shard'), may hold values from -1.75 to 1.75
- w_up: bfloat16 [768, 3072], P('shard'), may hold values from -0.21875 to 0.21875
- w_down: bfloat16 [3072, 768], P('shard'), may hold values from -0.109375 to 0.109375
- conv_w: bfloat16 [3, 2304], P(None, 'shard'), may hold values from -3 to 3
- gain_attn: bfloat16 [768], P('shard'), may hold values from 0.25 to 1.75
- gain_ffn: bfloat16 [768], P('shard'), may hold values from 0.25 to 1.75
- cotangent: bfloat16 [8, 2048, 768], P(('shard', 'replica'), 'seq'), may hold values from -6 to 6
Outputs:
- output: bfloat16 [8, 2048, 768], P(('shard', 'replica'), 'seq')
- grad_input: bfloat16 [8, 2048, 768], P(('shard', 'replica'), 'seq')
- grad_qkv: float32 [768, 2304], P('shard')
- grad_out: float32 [768, 768], P('shard')
- grad_up: float32 [768, 3072], P('shard')
- grad_down: float32 [3072, 768], P('shard')
- grad_conv: float32 [3, 2304], P(None, 'shard')
- grad_gain_attn: float32 [768], P('shard')
- grad_gain_ffn: float32 [768], P('shard')
The draws below stay inside these ranges and needn't reach their ends.
All inputs are finite; a program needn't handle non-finite values.
Results may differ from the reference program's by a relative error of at most 0.019.
Values may be sent and summed in bfloat16 or wider, within the bound.
A program may use at most 192 MiB of HBM per device.

```python
import jax
import jax.numpy as jnp
from jax import lax

D = 768
HEADS = 12
HEAD_DIM = 64
FF = 3072
LEN = 2048
SEQS = 8


def with_ends(values, own_key, least, high):
    shape = values.shape
    spot = [jax.random.randint(jax.random.fold_in(own_key, axis), (), 0, shape[axis]) for axis in range(len(shape))]
    values = values.at[tuple(spot)].set(least)
    longest = shape.index(max(shape))
    spot[longest] = (spot[longest] + 1) % shape[longest]
    return values.at[tuple(spot)].set(high)


def steps_of(stream_key, shape, pieces, least, largest):
    def one(position, parts):
        heights = jax.random.uniform(jax.random.fold_in(jax.random.fold_in(stream_key, 6), position), (parts,), jnp.float32, least / len(pieces), largest / len(pieces))
        return jnp.repeat(jnp.exp(heights), shape[position] // parts).reshape((-1,) + (1,) * (len(shape) - position - 1))

    gain = one(*pieces[0])
    for cut in pieces[1:]:
        gain = gain * one(*cut)
    return gain


def bell_draw(key, dims, width, reach, pieces=(), held_as=jnp.bfloat16):
    array = width * jax.random.normal(key, dims, jnp.float32)
    if pieces:
        array = array * steps_of(key, dims, pieces, -0.22, 0.18)
    return jnp.clip(array, -reach, reach).astype(held_as)


def setup_inputs(seed: int = 0) -> dict:
    seeds = jax.random.split(jax.random.key(seed), 11)
    tokens = bell_draw(seeds[0], (SEQS, LEN, D), 1.0, 6.0, ((0, 8), (1, 4)))
    prefix_len = with_ends(jax.random.randint(seeds[1], (SEQS,), LEN // 10, LEN // 2 + 1), jax.random.fold_in(seeds[1], 1), LEN // 10, (LEN // 2 + 1) - 1).astype(jnp.int32)
    w_qkv = bell_draw(seeds[2], (D, 3 * D), (D // 2) ** -0.5, 0.3125, ((0, 4),))
    w_out = bell_draw(seeds[3], (D, D), (D // 64) ** -0.5, 1.75, ((0, 4),))
    w_up = bell_draw(seeds[4], (D, FF), D ** -0.5, 0.21875, ((0, 4),))
    w_down = bell_draw(seeds[5], (FF, D), FF ** -0.5, 0.109375, ((0, 4),))
    conv_w = bell_draw(seeds[6], (3, 3 * D), 0.5, 3.0, ((1, 4),))
    gain_attn = jnp.clip(1.0 + 0.15 * jax.random.normal(seeds[7], (D,), jnp.float32), 0.25, 1.75).astype(jnp.bfloat16)
    gain_ffn = jnp.clip(1.0 + 0.15 * jax.random.normal(seeds[8], (D,), jnp.float32), 0.25, 1.75).astype(jnp.bfloat16)
    cotangent = bell_draw(seeds[9], (SEQS, LEN, D), 1.0, 6.0, ((0, 8), (1, 4)))
    return dict(tokens=tokens, prefix_len=prefix_len, w_qkv=w_qkv, w_out=w_out, w_up=w_up, w_down=w_down, conv_w=conv_w, gain_attn=gain_attn, gain_ffn=gain_ffn, cotangent=cotangent)


@jax.custom_vjp
def low(v):
    return lax.optimization_barrier(v.astype(jnp.bfloat16)).astype(jnp.float32)

@jax.custom_vjp
def low_back(v):
    return v

def low_keep(v):
    return (low(v), None)

def low_pass(kept, grad):
    return (grad,)

def back_keep(v):
    return (v, None)

def back_low(kept, grad):
    return (low(grad),)
low.defvjp(low_keep, low_pass)
low_back.defvjp(back_keep, back_low)
highest = lax.Precision.HIGHEST

def rms_scale(values):
    return lax.rsqrt(lax.optimization_barrier(jnp.mean(values * values, axis=-1, keepdims=True)) + 1e-06)

def attend(queries, keys_all, values_all, prefix_end):
    block_rows = min(512, LEN)
    count = LEN // block_rows
    scale = HEAD_DIM ** (-0.5)
    key_pos = jnp.arange(LEN, dtype=jnp.int32)

    def block_fn(items):
        query_block, offset = items
        query_pos = offset + jnp.arange(block_rows, dtype=jnp.int32)
        scores = jnp.einsum('qhd,khd->hqk', query_block, keys_all, precision=highest) * scale
        scores = low_back(scores)
        allowed = (key_pos[None, :] <= query_pos[:, None]) | (key_pos[None, :] < prefix_end) & (query_pos[:, None] < prefix_end)
        scores = jnp.where(allowed[None], scores, -1e+30)
        weights = low(jax.nn.softmax(scores, axis=-1))
        return jnp.einsum('hqk,khd->qhd', weights, values_all, precision=highest)
    blocks = queries.reshape(count, block_rows, HEADS, HEAD_DIM)
    offsets = jnp.arange(count, dtype=jnp.int32) * block_rows
    result = lax.map(jax.checkpoint(block_fn), (blocks, offsets))
    return result.reshape(LEN, HEADS * HEAD_DIM)

def layer(x_seq, w_qkv, w_out, w_up, w_down, conv_w, gain_attn, gain_ffn, prefix_end):
    normed = low(x_seq * rms_scale(x_seq) * gain_attn)
    projected = low_back(low(jnp.dot(normed, w_qkv, precision=highest)))
    padded = jnp.concatenate([jnp.zeros((2, 3 * D), x_seq.dtype), projected], 0)
    mixed = conv_w[0] * projected + conv_w[1] * padded[1:LEN + 1] + conv_w[2] * padded[:LEN]
    mixed = low_back(low(mixed))
    queries = mixed[:, :D].reshape(LEN, HEADS, HEAD_DIM)
    keys_all = mixed[:, D:2 * D].reshape(LEN, HEADS, HEAD_DIM)
    values_all = mixed[:, 2 * D:].reshape(LEN, HEADS, HEAD_DIM)
    attended = low_back(low(attend(queries, keys_all, values_all, prefix_end)))
    branch = low_back(jnp.dot(attended, w_out, precision=highest))
    hidden = x_seq + branch
    normed_two = low(hidden * rms_scale(hidden) * gain_ffn)
    upper = low_back(jnp.dot(normed_two, w_up, precision=highest))
    active = low(jnp.square(jnp.maximum(upper, 0.0)))
    return hidden + jnp.dot(active, w_down, precision=highest)

def reference(tokens, prefix_len, w_qkv, w_out, w_up, w_down, conv_w, gain_attn, gain_ffn, cotangent):
    params = (w_qkv.astype(jnp.float32), w_out.astype(jnp.float32), w_up.astype(jnp.float32), w_down.astype(jnp.float32), conv_w.astype(jnp.float32), gain_attn.astype(jnp.float32), gain_ffn.astype(jnp.float32))

    def step(totals, items):
        x_seq, cot_seq, prefix_end = items

        def forward(x_in, weights):
            return layer(x_in, *weights, prefix_end)
        result, pullback = jax.vjp(forward, x_seq.astype(jnp.float32), params)
        grad_x, grad_w = pullback(cot_seq.astype(jnp.float32))
        totals = tuple((left + right for left, right in zip(totals, grad_w)))
        return (totals, (result.astype(jnp.bfloat16), grad_x.astype(jnp.bfloat16)))
    zeros = tuple((jnp.zeros_like(weight) for weight in params))
    totals, (outputs, grads) = lax.scan(step, zeros, (tokens, cotangent, prefix_len))
    return (outputs, grads, totals[0], totals[1], totals[2], totals[3], totals[4], totals[5], totals[6])
```

```python
import functools

import jax
import jax.numpy as jnp
from jax import lax
from jax.experimental import pallas as pl
from jax.experimental.pallas import tpu as pltpu
from jax.sharding import PartitionSpec as P

HEADS = 12
HEAD_DIM=64
NEG=-1e30
F32=jnp.float32
BF=jnp.bfloat16

def nt(a,b):
    return lax.dot_general(a,b,(((1,),(1,)),((),())),preferred_element_type=F32)
def tn(a,b):
    return lax.dot_general(a,b,(((0,),(0,)),((),())),preferred_element_type=F32)

def convolve(proj_ref, conv_ref, wide, heads, parts):
    length, width = proj_ref.shape
    rows = min(512, length)
    wide[0:8] = jnp.zeros((8, width), F32)
    taps = conv_ref[...].astype(F32)
    for c in range(length//rows):
        wide[8+c*rows:8+(c+1)*rows] = proj_ref[c*rows:(c+1)*rows].astype(F32)
    def body(c, _):
        base = pl.multiple_of(c*rows, rows)
        x = wide[pl.ds(base, rows+8)]
        mixed = taps[0:1]*x[8:] + taps[1:2]*x[7:7+rows] + taps[2:3]*x[6:6+rows]
        for p,ref in enumerate(parts):
            for h in range(heads):
                lo = (p*heads+h)*HEAD_DIM
                piece = mixed[:, lo:lo+HEAD_DIM].astype(BF)
                if p == 0:
                    piece = piece * jnp.asarray(HEAD_DIM**-0.5, BF)
                ref[h, pl.ds(base, rows)] = piece
        return 0
    lax.fori_loop(0, length//rows, body, 0)

def mask_t(i, j, rows, prefix):
    kpos = j*rows + lax.broadcasted_iota(jnp.int32, (rows, 1), 0)
    qpos = i*rows + lax.broadcasted_iota(jnp.int32, (1, rows), 1)
    return (kpos <= qpos) | ((kpos < prefix) & (qpos < prefix))

def mask_n(i, j, rows, prefix):
    qpos = i*rows + lax.broadcasted_iota(jnp.int32, (rows, 1), 0)
    kpos = j*rows + lax.broadcasted_iota(jnp.int32, (1, rows), 1)
    return (kpos <= qpos) | ((kpos < prefix) & (qpos < prefix))

def fwd_kernel(prefix_ref, proj_ref, conv_ref, out_ref, lse_ref, wide, qs, ks, vs, m_s, l_s, acc_s, o_s, *, rows):
    heads = qs.shape[0]
    length = proj_ref.shape[0]
    blocks = length//rows
    prefix = prefix_ref[0]
    convolve(proj_ref, conv_ref, wide, heads, (qs, ks, vs))
    def head(h, _):
        def qblock(i, _):
            q = qs[h, pl.ds(pl.multiple_of(i*rows, rows), rows)]
            m_s[...] = jnp.full((1, rows), NEG, F32)
            l_s[...] = jnp.zeros((1, rows), F32)
            acc_s[...] = jnp.zeros((HEAD_DIM, rows), F32)
            def step(j, masked):
                at = pl.ds(pl.multiple_of(j*rows, rows), rows)
                s = nt(ks[h, at], q)
                if masked:
                    s = jnp.where(mask_t(i, j, rows, prefix), s, NEG)
                m_old = m_s[...]
                m_new = jnp.maximum(m_old, jnp.max(s, axis=0, keepdims=True))
                p = jnp.exp(s - m_new)
                a = jnp.exp(m_old - m_new)
                m_s[...] = m_new
                l_s[...] = a*l_s[...] + jnp.sum(p, axis=0, keepdims=True)
                acc_s[...] = a*acc_s[...] + tn(vs[h, at], p.astype(BF))
                return 0
            lax.fori_loop(0, i, lambda j, _: step(j, False), 0)
            lax.fori_loop(i, jnp.maximum(i+1, blocks//2), lambda j, _: step(j, True), 0)
            l = l_s[...]
            o_s[h, pl.ds(pl.multiple_of(i*rows, rows), rows)] = jnp.transpose(acc_s[...]/l).astype(BF)
            lse = m_s[...] + jnp.log(l)
            lse_ref[h, :, pl.ds(pl.multiple_of(i*rows, rows), rows)] = jnp.broadcast_to(lse, (8, rows))
            return 0
        lax.fori_loop(0, blocks, qblock, 0)
        return 0
    lax.fori_loop(0, heads, head, 0)
    def out(c, _):
        at = pl.ds(pl.multiple_of(c*rows, rows), rows)
        out_ref[at] = jnp.concatenate([o_s[h, at] for h in range(heads)], axis=1)
        return 0
    lax.fori_loop(0, blocks, out, 0)

def attention_fwd(prefix, proj, conv, rows=512):
    length, width = proj.shape
    heads = width//(3*HEAD_DIM)
    vm = pl.BlockSpec(memory_space=pltpu.VMEM)
    return pl.pallas_call(
        functools.partial(fwd_kernel, rows=rows),
        out_shape=(jax.ShapeDtypeStruct((length, heads*HEAD_DIM), BF), jax.ShapeDtypeStruct((heads, 8, length), F32)),
        in_specs=[pl.BlockSpec(memory_space=pltpu.SMEM), vm, vm],
        out_specs=(vm, vm),
        scratch_shapes=[pltpu.VMEM((8+length, width), F32)] + [pltpu.VMEM((heads, length, HEAD_DIM), BF)]*3 + [
            pltpu.VMEM((1,rows),F32), pltpu.VMEM((1,rows),F32), pltpu.VMEM((HEAD_DIM,rows),F32), pltpu.VMEM((heads,length,HEAD_DIM),BF)],
        compiler_params=pltpu.CompilerParams(vmem_limit_bytes=60*1024*1024),
        cost_estimate=pl.CostEstimate(flops=4*heads*length*length*HEAD_DIM, bytes_accessed=length*width*2, transcendentals=heads*length*length),
        name="attention_fwd",
    )(prefix, proj, conv)

def bwd_kernel(prefix_ref, proj_ref, conv_ref, do_ref, o_ref, lse_ref, gp_ref, gconv_ref, wide, qs, ks, vs, dos, delta, dq, dk, dv, gq, gk, gv, gwide, *, rows):
    heads = qs.shape[0]
    length, width = proj_ref.shape
    blocks = length//rows
    prefix = prefix_ref[0]
    convolve(proj_ref, conv_ref, wide, heads, (qs, ks, vs))
    def prep(c, _):
        at = pl.ds(pl.multiple_of(c*rows, rows), rows)
        g = do_ref[at]
        prod = g.astype(F32)*o_ref[at].astype(F32)
        for h in range(heads):
            sl = slice(h*HEAD_DIM, (h+1)*HEAD_DIM)
            dos[h, at] = g[:, sl]
            d = jnp.sum(prod[:, sl], axis=1, keepdims=True)
            delta[h, :, at] = jnp.transpose(jnp.broadcast_to(d, (rows, 128)))[0:8]
        return 0
    lax.fori_loop(0, blocks, prep, 0)
    def head(h, _):
        dq[...] = jnp.zeros(dq.shape, F32)
        def kblock(j, _):
            kat = pl.ds(pl.multiple_of(j*rows, rows), rows)
            k = ks[h, kat]; v = vs[h, kat]
            dk[...] = jnp.zeros(dk.shape, F32)
            dv[...] = jnp.zeros(dv.shape, F32)
            def step(i, masked):
                qat = pl.ds(pl.multiple_of(i*rows, rows), rows)
                q = qs[h, qat]; do = dos[h, qat]
                s = nt(k, q)
                p = jnp.exp(s - lse_ref[h, 0:1, qat])
                if masked:
                    p = jnp.where(mask_t(i, j, rows, prefix), p, 0.0)
                dv[...] += jnp.dot(p.astype(BF), do, preferred_element_type=F32)
                dp = nt(v, do)
                ds = (p*(dp - delta[h, 0:1, qat])).astype(BF)
                dk[...] += jnp.dot(ds, q, preferred_element_type=F32)
                dq[qat] += tn(ds, k)
                return 0
            lax.fori_loop(j+1, blocks, lambda i, _: step(i, False), 0)
            lax.fori_loop(jnp.where(j < blocks//2, 0, j), j+1, lambda i, _: step(i, True), 0)
            gk[h, kat] = dk[...].astype(BF)
            gv[h, kat] = dv[...].astype(BF)
            return 0
        lax.fori_loop(0, blocks, kblock, 0)
        def qout(c, _):
            at = pl.ds(pl.multiple_of(c*rows, rows), rows)
            gq[h, at] = (dq[at]*(HEAD_DIM**-0.5)).astype(BF)
            return 0
        lax.fori_loop(0, blocks, qout, 0)
        return 0
    lax.fori_loop(0, heads, head, 0)
    taps = conv_ref[...].astype(F32)
    gwide[length:length+8] = jnp.zeros((8, width), F32)
    def fill(c, _):
        at = pl.ds(pl.multiple_of(c*rows, rows), rows)
        gwide[at] = jnp.concatenate([r[h, at] for r in (gq, gk, gv) for h in range(heads)], axis=1).astype(F32)
        return 0
    lax.fori_loop(0, blocks, fill, 0)
    def out(c, total):
        base = pl.multiple_of(c*rows, rows)
        g = gwide[pl.ds(base, rows+8)]
        x = wide[pl.ds(base, rows+8)]
        g0 = g[:rows]
        gp = taps[0:1]*g0 + taps[1:2]*g[1:rows+1] + taps[2:3]*g[2:rows+2]
        gp_ref[pl.ds(base, rows)] = gp.astype(BF)
        sums = [jnp.sum(g0*x[8-t:8-t+rows], axis=0, keepdims=True) for t in range(3)]
        return tuple(a+b for a, b in zip(total, sums))
    total = lax.fori_loop(0, blocks, out, tuple(jnp.zeros((1, width), F32) for _ in range(3)))
    gconv_ref[...] = jnp.concatenate(total, axis=0)

def attention_bwd(prefix, proj, conv, do, o, lse, rows=512):
    length, width = proj.shape
    heads = width//(3*HEAD_DIM)
    vm = pl.BlockSpec(memory_space=pltpu.VMEM)
    per = lambda dt: pltpu.VMEM((heads, length, HEAD_DIM), dt)
    return pl.pallas_call(
        functools.partial(bwd_kernel, rows=rows),
        out_shape=(jax.ShapeDtypeStruct((length, width), BF), jax.ShapeDtypeStruct((3, width), F32)),
        in_specs=[pl.BlockSpec(memory_space=pltpu.SMEM)] + [vm]*5,
        out_specs=(vm, vm),
        scratch_shapes=[pltpu.VMEM((8+length, width), F32), per(BF), per(BF), per(BF), per(BF), pltpu.VMEM((heads, 8, length), F32),
            pltpu.VMEM((length, HEAD_DIM), F32), pltpu.VMEM((rows, HEAD_DIM), F32), pltpu.VMEM((rows, HEAD_DIM), F32),
            per(BF), per(BF), per(BF), pltpu.VMEM((length+8, width), F32)],
        compiler_params=pltpu.CompilerParams(vmem_limit_bytes=60*1024*1024),
        cost_estimate=pl.CostEstimate(flops=10*heads*length*length*HEAD_DIM, bytes_accessed=length*width*4, transcendentals=heads*length*length),
        name="attention_bwd",
    )(prefix, proj, conv, do, o, lse)


def rms_scale(values):
    return lax.rsqrt(jnp.mean(values * values, axis=-1, keepdims=True) + 1e-06)


def norm_back(values, scale_rows, gain, upstream):
    weighted = upstream * gain
    grad_gain = jnp.sum(upstream * values * scale_rows, axis=0)
    grad_values = scale_rows * weighted - values * scale_rows**3 * jnp.mean(
        weighted * values, axis=-1, keepdims=True
    )
    return (grad_values, grad_gain)


def dot(a, b):
    return jnp.dot(a, b, preferred_element_type=F32)


def per_device(
    tokens, prefix_len, w_qkv, w_out, w_up, w_down, conv_w, gain_attn, gain_ffn, cotangent
):
    blocks = lax.axis_size("seq")
    me = lax.axis_index("seq")
    rows, width = tokens.shape[1:]
    own = HEADS // blocks * HEAD_DIM
    depth = w_qkv.shape[0]

    tokens_all = lax.all_gather(tokens[0], "seq", axis=0, tiled=True)
    columns = lax.dynamic_index_in_dim(w_qkv.reshape(depth, 3, blocks, own), me, 2, False)
    own_qkv = lax.all_gather(columns.reshape(depth, 3 * own), "shard", axis=0, tiled=True)
    small = jnp.concatenate([gain_attn, gain_ffn, conv_w.reshape(-1)])
    small = lax.all_gather(small, "shard", axis=0)
    full_gone = small[:, :depth].reshape(width).astype(F32)
    full_gtwo = small[:, depth : 2 * depth].reshape(width).astype(F32)
    full_conv = small[:, 2 * depth :].reshape(-1, 3, conv_w.shape[1]).transpose(1, 0, 2)
    own_conv = lax.dynamic_index_in_dim(full_conv.reshape(3, 3, blocks, own), me, 2, False)
    own_conv = own_conv.reshape(3, 3 * own)
    full_out = lax.all_gather(w_out, "shard", axis=0, tiled=True)
    full_up = lax.all_gather(w_up, "shard", axis=0, tiled=True)
    full_down = lax.all_gather(w_down, "shard", axis=0, tiled=True)

    whole = tokens_all.astype(F32)
    normed_all = (whole * rms_scale(whole) * full_gone).astype(BF)
    projected = dot(normed_all, own_qkv).astype(BF)
    attended_own, logsum = attention_fwd(prefix_len, projected, own_conv)

    def to_rows(array):
        array = lax.all_to_all(array.reshape(blocks, rows, own), "seq", 0, 0)
        return array.transpose(1, 0, 2).reshape(rows, width)

    def to_heads(array):
        array = array.reshape(rows, blocks, own).transpose(1, 0, 2)
        return lax.all_to_all(array, "seq", 0, 0).reshape(blocks * rows, own)

    inputs = tokens[0].astype(F32)
    scale_one = rms_scale(inputs)
    attended_b = to_rows(attended_own)
    hidden = inputs + dot(attended_b, full_out)
    scale_two = rms_scale(hidden)
    normed_two_b = (hidden * scale_two * full_gtwo).astype(BF)
    positive = jnp.maximum(dot(normed_two_b, full_up), 0.0)
    active_b = (positive * positive).astype(BF)
    output = hidden + dot(active_b, full_down)

    incoming = cotangent[0]
    grad_upper_b = (dot(incoming, full_down.T) * 2.0 * positive).astype(BF)
    grad_normed_two = dot(grad_upper_b, full_up.T)
    grad_hidden_norm, grad_gtwo = norm_back(hidden, scale_two, full_gtwo, grad_normed_two)
    grad_hidden = incoming.astype(F32) + grad_hidden_norm
    grad_hidden_b = grad_hidden.astype(BF)
    grad_attended_b = dot(grad_hidden_b, full_out.T).astype(BF)
    grad_own = to_heads(grad_attended_b)
    grad_down = dot(active_b.T, incoming)
    grad_up = dot(normed_two_b.T, grad_upper_b)
    grad_out = dot(attended_b.T, grad_hidden_b)

    grad_projected, grad_conv = attention_bwd(
        prefix_len, projected, own_conv, grad_own, attended_own, logsum
    )
    grad_normed = lax.psum_scatter(
        dot(grad_projected, own_qkv.T).astype(BF), "seq", scatter_dimension=0, tiled=True
    ).astype(F32)
    grad_qkv = dot(normed_all.T, grad_projected)
    grad_input_norm, grad_gone = norm_back(inputs, scale_one, full_gone, grad_normed)
    grad_input = (grad_hidden + grad_input_norm).astype(BF)

    def shared(grad):
        grad = lax.psum_scatter(grad.astype(BF), "shard", scatter_dimension=0, tiled=True)
        return lax.psum(grad, ("seq", "replica")).astype(F32)

    part = lax.psum_scatter(grad_qkv.astype(BF), "shard", scatter_dimension=0, tiled=True)
    part = lax.psum(part, "replica")
    part = lax.all_gather(part, "seq", axis=0)
    total_qkv = part.reshape(blocks, depth, 3, own).transpose(1, 2, 0, 3).reshape(depth, -1)

    spread = jnp.zeros((3, 3, blocks, own), F32)
    spread = lax.dynamic_update_slice(spread, grad_conv.reshape(3, 3, 1, own), (0, 0, me, 0))
    sums = lax.psum(
        jnp.concatenate([spread.reshape(-1), grad_gone, grad_gtwo]), ("seq", "shard", "replica")
    )
    at = lax.axis_index("shard")
    taps = spread.size
    conv_total = sums[:taps].reshape(3, -1)
    return (
        output[None].astype(BF),
        grad_input[None],
        total_qkv.astype(F32),
        shared(grad_out),
        shared(grad_up),
        shared(grad_down),
        lax.dynamic_slice_in_dim(conv_total, at * conv_w.shape[1], conv_w.shape[1], 1),
        lax.dynamic_slice_in_dim(sums[taps : taps + width], at * depth, depth),
        lax.dynamic_slice_in_dim(sums[taps + width :], at * depth, depth),
    )


def solution(mesh):
    placed = (
        P(("shard", "replica"), "seq", None),
        P(("shard", "replica")),
        P("shard", None),
        P("shard", None),
        P("shard", None),
        P("shard", None),
        P(None, "shard"),
        P("shard"),
        P("shard"),
        P(("shard", "replica"), "seq", None),
    )
    return jax.shard_map(
        per_device,
        mesh=mesh,
        in_specs=placed,
        out_specs=(
            P(("shard", "replica"), "seq", None),
            P(("shard", "replica"), "seq", None),
            P("shard", None),
            P("shard", None),
            P("shard", None),
            P("shard", None),
            P(None, "shard"),
            P("shard"),
            P("shard"),
        ),
        check_vma=False,
    )
```

```python
import functools

import jax
import jax.numpy as jnp
from jax import lax
from jax.experimental import pallas as pl
from jax.experimental.pallas import tpu as pltpu
from jax.sharding import PartitionSpec as P

HEADS = 12
HEAD_DIM=64
NEG=-1e30
F32=jnp.float32
BF=jnp.bfloat16

def nt(a,b):
    return lax.dot_general(a,b,(((1,),(1,)),((),())),preferred_element_type=F32)
def tn(a,b):
    return lax.dot_general(a,b,(((0,),(0,)),((),())),preferred_element_type=F32)

def convolve(proj_ref, conv_ref, wide, heads, parts):
    length, width = proj_ref.shape
    rows = min(512, length)
    wide[0:8] = jnp.zeros((8, width), F32)
    taps = conv_ref[...].astype(F32)
    for c in range(length//rows):
        wide[8+c*rows:8+(c+1)*rows] = proj_ref[c*rows:(c+1)*rows].astype(F32)
    def body(c, _):
        base = pl.multiple_of(c*rows, rows)
        x = wide[pl.ds(base, rows+8)]
        mixed = taps[0:1]*x[8:] + taps[1:2]*x[7:7+rows] + taps[2:3]*x[6:6+rows]
        for p,ref in enumerate(parts):
            for h in range(heads):
                lo = (p*heads+h)*HEAD_DIM
                piece = mixed[:, lo:lo+HEAD_DIM].astype(BF)
                if p == 0:
                    piece = piece * jnp.asarray(HEAD_DIM**-0.5, BF)
                ref[h, pl.ds(base, rows)] = piece
        return 0
    lax.fori_loop(0, length//rows, body, 0)

def mask_t(i, j, rows, prefix):
    kpos = j*rows + lax.broadcasted_iota(jnp.int32, (rows, 1), 0)
    qpos = i*rows + lax.broadcasted_iota(jnp.int32, (1, rows), 1)
    return (kpos <= qpos) | ((kpos < prefix) & (qpos < prefix))

def mask_n(i, j, rows, prefix):
    qpos = i*rows + lax.broadcasted_iota(jnp.int32, (rows, 1), 0)
    kpos = j*rows + lax.broadcasted_iota(jnp.int32, (1, rows), 1)
    return (kpos <= qpos) | ((kpos < prefix) & (qpos < prefix))

def fwd_kernel(prefix_ref, proj_ref, conv_ref, out_ref, lse_ref, wide, qs, ks, vs, m_s, l_s, acc_s, o_s, *, rows):
    heads = qs.shape[0]
    length = proj_ref.shape[0]
    blocks = length//rows
    prefix = prefix_ref[0]
    convolve(proj_ref, conv_ref, wide, heads, (qs, ks, vs))
    def head(h, _):
        def qblock(i, _):
            q = qs[h, pl.ds(pl.multiple_of(i*rows, rows), rows)]
            m_s[...] = jnp.full((1, rows), NEG, F32)
            l_s[...] = jnp.zeros((1, rows), F32)
            acc_s[...] = jnp.zeros((HEAD_DIM, rows), F32)
            def step(j, masked):
                at = pl.ds(pl.multiple_of(j*rows, rows), rows)
                s = nt(ks[h, at], q)
                if masked:
                    s = jnp.where(mask_t(i, j, rows, prefix), s, NEG)
                m_old = m_s[...]
                m_new = jnp.maximum(m_old, jnp.max(s, axis=0, keepdims=True))
                p = jnp.exp(s - m_new)
                a = jnp.exp(m_old - m_new)
                m_s[...] = m_new
                l_s[...] = a*l_s[...] + jnp.sum(p, axis=0, keepdims=True)
                acc_s[...] = a*acc_s[...] + tn(vs[h, at], p.astype(BF))
                return 0
            lax.fori_loop(0, i, lambda j, _: step(j, False), 0)
            lax.fori_loop(i, jnp.maximum(i+1, blocks//2), lambda j, _: step(j, True), 0)
            l = l_s[...]
            o_s[h, pl.ds(pl.multiple_of(i*rows, rows), rows)] = jnp.transpose(acc_s[...]/l).astype(BF)
            lse = m_s[...] + jnp.log(l)
            lse_ref[h, :, pl.ds(pl.multiple_of(i*rows, rows), rows)] = jnp.broadcast_to(lse, (8, rows))
            return 0
        lax.fori_loop(0, blocks, qblock, 0)
        return 0
    lax.fori_loop(0, heads, head, 0)
    def out(c, _):
        at = pl.ds(pl.multiple_of(c*rows, rows), rows)
        out_ref[at] = jnp.concatenate([o_s[h, at] for h in range(heads)], axis=1)
        return 0
    lax.fori_loop(0, blocks, out, 0)

def attention_fwd(prefix, proj, conv, rows=512):
    length, width = proj.shape
    heads = width//(3*HEAD_DIM)
    vm = pl.BlockSpec(memory_space=pltpu.VMEM)
    return pl.pallas_call(
        functools.partial(fwd_kernel, rows=rows),
        out_shape=(jax.ShapeDtypeStruct((length, heads*HEAD_DIM), BF), jax.ShapeDtypeStruct((heads, 8, length), F32)),
        in_specs=[pl.BlockSpec(memory_space=pltpu.SMEM), vm, vm],
        out_specs=(vm, vm),
        scratch_shapes=[pltpu.VMEM((8+length, width), F32)] + [pltpu.VMEM((heads, length, HEAD_DIM), BF)]*3 + [
            pltpu.VMEM((1,rows),F32), pltpu.VMEM((1,rows),F32), pltpu.VMEM((HEAD_DIM,rows),F32), pltpu.VMEM((heads,length,HEAD_DIM),BF)],
        compiler_params=pltpu.CompilerParams(vmem_limit_bytes=60*1024*1024),
        cost_estimate=pl.CostEstimate(flops=4*heads*length*length*HEAD_DIM, bytes_accessed=length*width*2, transcendentals=heads*length*length),
        name="attention_fwd",
    )(prefix, proj, conv)

def bwd_kernel(prefix_ref, proj_ref, conv_ref, do_ref, o_ref, lse_ref, gp_ref, gconv_ref, wide, qs, ks, vs, dos, delta, dq, dk, dv, gq, gk, gv, gwide, *, rows):
    heads = qs.shape[0]
    length, width = proj_ref.shape
    blocks = length//rows
    prefix = prefix_ref[0]
    convolve(proj_ref, conv_ref, wide, heads, (qs, ks, vs))
    def prep(c, _):
        at = pl.ds(pl.multiple_of(c*rows, rows), rows)
        g = do_ref[at]
        prod = g.astype(F32)*o_ref[at].astype(F32)
        for h in range(heads):
            sl = slice(h*HEAD_DIM, (h+1)*HEAD_DIM)
            dos[h, at] = g[:, sl]
            d = jnp.sum(prod[:, sl], axis=1, keepdims=True)
            delta[h, :, at] = jnp.transpose(jnp.broadcast_to(d, (rows, 128)))[0:8]
        return 0
    lax.fori_loop(0, blocks, prep, 0)
    def head(h, _):
        dq[...] = jnp.zeros(dq.shape, F32)
        def kblock(j, _):
            kat = pl.ds(pl.multiple_of(j*rows, rows), rows)
            k = ks[h, kat]; v = vs[h, kat]
            dk[...] = jnp.zeros(dk.shape, F32)
            dv[...] = jnp.zeros(dv.shape, F32)
            def step(i, masked):
                qat = pl.ds(pl.multiple_of(i*rows, rows), rows)
                q = qs[h, qat]; do = dos[h, qat]
                s = nt(k, q)
                p = jnp.exp(s - lse_ref[h, 0:1, qat])
                if masked:
                    p = jnp.where(mask_t(i, j, rows, prefix), p, 0.0)
                dv[...] += jnp.dot(p.astype(BF), do, preferred_element_type=F32)
                dp = nt(v, do)
                ds = (p*(dp - delta[h, 0:1, qat])).astype(BF)
                dk[...] += jnp.dot(ds, q, preferred_element_type=F32)
                dq[qat] += tn(ds, k)
                return 0
            lax.fori_loop(j+1, blocks, lambda i, _: step(i, False), 0)
            lax.fori_loop(jnp.where(j < blocks//2, 0, j), j+1, lambda i, _: step(i, True), 0)
            gk[h, kat] = dk[...].astype(BF)
            gv[h, kat] = dv[...].astype(BF)
            return 0
        lax.fori_loop(0, blocks, kblock, 0)
        def qout(c, _):
            at = pl.ds(pl.multiple_of(c*rows, rows), rows)
            gq[h, at] = (dq[at]*(HEAD_DIM**-0.5)).astype(BF)
            return 0
        lax.fori_loop(0, blocks, qout, 0)
        return 0
    lax.fori_loop(0, heads, head, 0)
    taps = conv_ref[...].astype(F32)
    gwide[length:length+8] = jnp.zeros((8, width), F32)
    def fill(c, _):
        at = pl.ds(pl.multiple_of(c*rows, rows), rows)
        gwide[at] = jnp.concatenate([r[h, at] for r in (gq, gk, gv) for h in range(heads)], axis=1).astype(F32)
        return 0
    lax.fori_loop(0, blocks, fill, 0)
    def out(c, total):
        base = pl.multiple_of(c*rows, rows)
        g = gwide[pl.ds(base, rows+8)]
        x = wide[pl.ds(base, rows+8)]
        g0 = g[:rows]
        gp = taps[0:1]*g0 + taps[1:2]*g[1:rows+1] + taps[2:3]*g[2:rows+2]
        gp_ref[pl.ds(base, rows)] = gp.astype(BF)
        sums = [jnp.sum(g0*x[8-t:8-t+rows], axis=0, keepdims=True) for t in range(3)]
        return tuple(a+b for a, b in zip(total, sums))
    total = lax.fori_loop(0, blocks, out, tuple(jnp.zeros((1, width), F32) for _ in range(3)))
    gconv_ref[...] = jnp.concatenate(total, axis=0)

def attention_bwd(prefix, proj, conv, do, o, lse, rows=512):
    length, width = proj.shape
    heads = width//(3*HEAD_DIM)
    vm = pl.BlockSpec(memory_space=pltpu.VMEM)
    per = lambda dt: pltpu.VMEM((heads, length, HEAD_DIM), dt)
    return pl.pallas_call(
        functools.partial(bwd_kernel, rows=rows),
        out_shape=(jax.ShapeDtypeStruct((length, width), BF), jax.ShapeDtypeStruct((3, width), F32)),
        in_specs=[pl.BlockSpec(memory_space=pltpu.SMEM)] + [vm]*5,
        out_specs=(vm, vm),
        scratch_shapes=[pltpu.VMEM((8+length, width), F32), per(BF), per(BF), per(BF), per(BF), pltpu.VMEM((heads, 8, length), F32),
            pltpu.VMEM((length, HEAD_DIM), F32), pltpu.VMEM((rows, HEAD_DIM), F32), pltpu.VMEM((rows, HEAD_DIM), F32),
            per(BF), per(BF), per(BF), pltpu.VMEM((length+8, width), F32)],
        compiler_params=pltpu.CompilerParams(vmem_limit_bytes=60*1024*1024),
        cost_estimate=pl.CostEstimate(flops=10*heads*length*length*HEAD_DIM, bytes_accessed=length*width*4, transcendentals=heads*length*length),
        name="attention_bwd",
    )(prefix, proj, conv, do, o, lse)


MESH = pl.DeviceIdType.MESH


def reduce_kernel(
    big_ref, qkv_ref, out_ref, qout_ref, a_buf, b_buf, c_buf, d_buf, qa, qb, qc,
    a_s, a_r, b_s, b_r, c_s, c_r, d_s, d_r, e_s, e_r, f_s, f_r,
    *, nx, nz,
):
    ny, _, chunks, units = big_ref.shape[:4]
    half = units // nx
    piece = half // nz
    qhalf = qkv_ref.shape[2] // nx
    z, s, x = lax.axis_index("seq"), lax.axis_index("shard"), lax.axis_index("replica")
    y, c = s // 2, s % 2
    core = (z, 2 * y + 1 - c, x)

    def at_y(i):
        return (y + i) % ny

    def at_x(i):
        return (x + i) % nx

    def at_z(i):
        return (z + i) % nz

    def dev_y(i):
        return (z, 2 * at_y(i) + c, x)

    def dev_x(i):
        return (z, s, at_x(i))

    def dev_z(i):
        return (at_z(i), s, x)

    peers = [core] + [dev_y(i) for i in range(1, ny)] + [dev_x(i) for i in range(1, nx)]
    peers += [dev_z(i) for i in range(1, nz)]
    barrier = pltpu.get_barrier_semaphore()
    for peer in peers:
        pl.semaphore_signal(barrier, inc=1, device_id=peer, device_id_type=MESH)
    pl.semaphore_wait(barrier, len(peers))

    def copy(src, dst, ss, rs, peer):
        return pltpu.make_async_remote_copy(
            src_ref=src, dst_ref=dst, send_sem=ss, recv_sem=rs, device_id=peer, device_id_type=MESH
        )

    def stage_a(k, _):
        copy(big_ref.at[:, 1 - c, k], a_buf.at[k], a_s.at[k], a_r.at[k], core).start()
        return 0

    def wait_a(k):
        return copy(a_buf.at[k], a_buf.at[k], a_s.at[k], a_r.at[k], core)

    def copy_b(k, i, there):
        slot = y if there else at_y(i)
        return copy(a_buf.at[k, at_y(i)], b_buf.at[k, slot], b_s.at[k, at_y(i)], b_r.at[k, slot], dev_y(i))

    def stage_b(k, _):
        wait_a(k).wait_recv()
        for i in list(range(1, ny)) + [0]:
            p = at_y(i)
            a_buf[k, p] = (a_buf[k, p].astype(F32) + big_ref[p, c, k].astype(F32)).astype(BF)
            if i:
                copy_b(k, i, True).start()
        return 0

    def copy_c(k, i, there):
        slot = x if there else at_x(i)
        src = a_buf.at[k, y, pl.ds(at_x(i) * half, half)]
        return copy(src, c_buf.at[k, slot], c_s.at[k, at_x(i)], c_r.at[k, slot], dev_x(i))

    def stage_c(k):
        total = a_buf[k, y].astype(F32)
        for i in range(1, ny):
            copy_b(k, i, False).wait_recv()
            total = total + b_buf[k, at_y(i)].astype(F32)
        a_buf[k, y] = total.astype(BF)
        for i in range(1, nx):
            copy_c(k, i, True).start()

    def copy_d(k, i, there):
        slot = z if there else at_z(i)
        src = a_buf.at[k, y, pl.ds(x * half + at_z(i) * piece, piece)]
        return copy(src, d_buf.at[k, slot], d_s.at[k, at_z(i)], d_r.at[k, slot], dev_z(i))

    def stage_d(k):
        mine = pl.ds(x * half, half)
        total = a_buf[k, y, mine].astype(F32)
        for i in range(1, nx):
            copy_c(k, i, False).wait_recv()
            total = total + c_buf[k, at_x(i)].astype(F32)
        a_buf[k, y, mine] = total.astype(BF)
        for i in range(1, nz):
            copy_d(k, i, True).start()

    def copy_e(k, i, there):
        slot = z if there else at_z(i)
        ref = out_ref.at[k, pl.ds(x * half + slot * piece, piece)]
        return copy(ref, ref, e_s.at[k, at_z(i)], e_r.at[k, slot], dev_z(i))

    def stage_e(k):
        mine = pl.ds(x * half + z * piece, piece)
        total = a_buf[k, y, mine].astype(F32)
        for i in range(1, nz):
            copy_d(k, i, False).wait_recv()
            total = total + d_buf[k, at_z(i)].astype(F32)
        out_ref[k, mine] = total.astype(BF)
        for i in range(1, nz):
            copy_e(k, i, True).start()

    def copy_f(k, i, there):
        slot = x if there else at_x(i)
        ref = out_ref.at[k, pl.ds(slot * half, half)]
        return copy(ref, ref, f_s.at[k, at_x(i)], f_r.at[k, slot], dev_x(i))

    def stage_f(k):
        for i in range(1, nz):
            copy_e(k, i, False).wait_recv()
        for i in range(1, nx):
            copy_f(k, i, True).start()

    last = chunks

    def q_a():
        return copy(qkv_ref.at[:, 1 - c], qa, a_s.at[last], a_r.at[last], core)

    def q_b(i, there):
        slot = y if there else at_y(i)
        return copy(qa.at[at_y(i)], qb.at[slot], b_s.at[last, at_y(i)], b_r.at[last, slot], dev_y(i))

    def q_c(i, there):
        slot = x if there else at_x(i)
        src = qa.at[y, pl.ds(at_x(i) * qhalf, qhalf)]
        return copy(src, qc.at[slot], c_s.at[last, at_x(i)], c_r.at[last, slot], dev_x(i))

    def q_e(i, there):
        ref = qout_ref.at[z if there else at_z(i), pl.ds(x * qhalf, qhalf)]
        return copy(ref, ref, e_s.at[last, at_z(i)], e_r.at[last, z if there else at_z(i)], dev_z(i))

    def q_f(i, there):
        slot = x if there else at_x(i)
        ref = qout_ref.at[:, pl.ds(slot * qhalf, qhalf)]
        return copy(ref, ref, f_s.at[last, at_x(i)], f_r.at[last, slot], dev_x(i))

    q_a().start()
    lax.fori_loop(0, chunks, stage_a, 0)
    q_a().wait_recv()
    for i in list(range(1, ny)) + [0]:
        p = at_y(i)
        qa[p] = (qa[p].astype(F32) + qkv_ref[p, c].astype(F32)).astype(BF)
        if i:
            q_b(i, True).start()
    lax.fori_loop(0, chunks, stage_b, 0)
    total = qa[y].astype(F32)
    for i in range(1, ny):
        q_b(i, False).wait_recv()
        total = total + qb[at_y(i)].astype(F32)
    qa[y] = total.astype(BF)
    for i in range(1, nx):
        q_c(i, True).start()

    def step(t, _):
        for lag, stage in enumerate((stage_c, stage_d, stage_e, stage_f)):
            @pl.when((t >= lag) & (t < chunks + lag))
            def _():
                stage(t - lag)
        return 0

    lax.fori_loop(0, 1, step, 0)
    mine = pl.ds(x * qhalf, qhalf)
    total = qa[y, mine].astype(F32)
    for i in range(1, nx):
        q_c(i, False).wait_recv()
        total = total + qc[at_x(i)].astype(F32)
    qout_ref[z, mine] = total.astype(BF)
    for i in range(1, nz):
        q_e(i, True).start()
    lax.fori_loop(1, 3, step, 0)
    for i in range(1, nz):
        q_e(i, False).wait_recv()
    for i in range(1, nx):
        q_f(i, True).start()
    lax.fori_loop(3, chunks + 3, step, 0)

    def finish(k, _):
        for i in range(1, nx):
            copy_f(k, i, False).wait_recv()
        wait_a(k).wait_send()
        for i in range(1, ny):
            copy_b(k, i, True).wait_send()
        for i in range(1, nx):
            copy_c(k, i, True).wait_send()
            copy_f(k, i, True).wait_send()
        for i in range(1, nz):
            copy_d(k, i, True).wait_send()
            copy_e(k, i, True).wait_send()
        return 0

    lax.fori_loop(0, chunks, finish, 0)
    for i in range(1, nx):
        q_f(i, False).wait_recv()
    q_a().wait_send()
    for i in range(1, ny):
        q_b(i, True).wait_send()
    for i in range(1, nx):
        q_c(i, True).wait_send()
        q_f(i, True).wait_send()
    for i in range(1, nz):
        q_e(i, True).wait_send()


def reduce_grads(big, qkv, nx, nz):
    ny, _, chunks, units = big.shape[:4]
    tail = big.shape[4:]
    uq = qkv.shape[2]
    qtail = qkv.shape[3:]
    half, qhalf = units // nx, uq // nx
    vm = pl.BlockSpec(memory_space=pltpu.VMEM)
    sems = []
    for n in (ny, nx, nz, nz, nx):
        sems += [pltpu.SemaphoreType.DMA((chunks + 1, n))] * 2
    return pl.pallas_call(
        functools.partial(reduce_kernel, nx=nx, nz=nz),
        out_shape=(
            jax.ShapeDtypeStruct((chunks, units) + tail, BF),
            jax.ShapeDtypeStruct((nz, uq) + qtail, BF),
        ),
        in_specs=[vm, vm],
        out_specs=(vm, vm),
        scratch_shapes=[
            pltpu.VMEM((chunks, ny, units) + tail, BF),
            pltpu.VMEM((chunks, ny, units) + tail, BF),
            pltpu.VMEM((chunks, nx, half) + tail, BF),
            pltpu.VMEM((chunks, nz, half // nz) + tail, BF),
            pltpu.VMEM((ny, uq) + qtail, BF),
            pltpu.VMEM((ny, uq) + qtail, BF),
            pltpu.VMEM((nx, qhalf) + qtail, BF),
            pltpu.SemaphoreType.DMA((chunks + 1,)),
            pltpu.SemaphoreType.DMA((chunks + 1,)),
        ]
        + sems,
        compiler_params=pltpu.CompilerParams(
            collective_id=1, has_side_effects=True, vmem_limit_bytes=60 * 1024 * 1024
        ),
        name="reduce_grads",
    )(big, qkv)


def rms_scale(values):
    return lax.rsqrt(jnp.mean(values * values, axis=-1, keepdims=True) + 1e-06)


def norm_back(values, scale_rows, gain, upstream):
    weighted = upstream * gain
    grad_values = scale_rows * weighted - values * scale_rows**3 * jnp.mean(
        weighted * values, axis=-1, keepdims=True
    )
    return grad_values


def dot(a, b):
    return jnp.dot(a, b, preferred_element_type=F32)


def per_device(
    tokens, prefix_len, w_qkv, w_out, w_up, w_down, conv_w, gain_attn, gain_ffn, cotangent
):
    blocks = lax.axis_size("seq")
    me = lax.axis_index("seq")
    rows, width = tokens.shape[1:]
    own = HEADS // blocks * HEAD_DIM
    depth = w_qkv.shape[0]

    tokens_all = lax.all_gather(tokens[0], "seq", axis=0, tiled=True)
    columns = lax.dynamic_index_in_dim(w_qkv.reshape(depth, 3, blocks, own), me, 2, False)
    own_qkv = lax.all_gather(columns.reshape(depth, 3 * own), "shard", axis=0, tiled=True)
    small = jnp.concatenate([gain_attn, gain_ffn, conv_w.reshape(-1)])
    small = lax.all_gather(small, "shard", axis=0)
    full_gone = small[:, :depth].reshape(width).astype(F32)
    full_gtwo = small[:, depth : 2 * depth].reshape(width).astype(F32)
    full_conv = small[:, 2 * depth :].reshape(-1, 3, conv_w.shape[1]).transpose(1, 0, 2)
    own_conv = lax.dynamic_index_in_dim(full_conv.reshape(3, 3, blocks, own), me, 2, False)
    own_conv = own_conv.reshape(3, 3 * own)
    full_out = lax.all_gather(w_out, "shard", axis=0, tiled=True)
    full_up = lax.all_gather(w_up, "shard", axis=0, tiled=True)
    full_down = lax.all_gather(w_down, "shard", axis=0, tiled=True)

    whole = tokens_all.astype(F32)
    normed_all = (whole * rms_scale(whole) * full_gone).astype(BF)
    projected = dot(normed_all, own_qkv).astype(BF)
    attended_own, logsum = attention_fwd(prefix_len, projected, own_conv)

    def to_rows(array):
        array = lax.all_to_all(array.reshape(blocks, rows, own), "seq", 0, 0)
        return array.transpose(1, 0, 2).reshape(rows, width)

    def to_heads(array):
        array = array.reshape(rows, blocks, own).transpose(1, 0, 2)
        return lax.all_to_all(array, "seq", 0, 0).reshape(blocks * rows, own)

    inputs = tokens[0].astype(F32)
    scale_one = rms_scale(inputs)
    attended_b = to_rows(attended_own)
    hidden = inputs + dot(attended_b, full_out)
    scale_two = rms_scale(hidden)
    normed_two_b = (hidden * scale_two * full_gtwo).astype(BF)
    positive = jnp.maximum(dot(normed_two_b, full_up), 0.0)
    active_b = (positive * positive).astype(BF)
    output = hidden + dot(active_b, full_down)

    incoming = cotangent[0]
    grad_upper_b = (dot(incoming, full_down.T) * 2.0 * positive).astype(BF)
    grad_normed_two = dot(grad_upper_b, full_up.T)
    grad_hidden = incoming.astype(F32) + norm_back(hidden, scale_two, full_gtwo, grad_normed_two)
    grad_hidden_b = grad_hidden.astype(BF)
    grad_attended_b = dot(grad_hidden_b, full_out.T).astype(BF)
    grad_own = to_heads(grad_attended_b)
    grad_projected, grad_conv = attention_bwd(
        prefix_len, projected, own_conv, grad_own, attended_own, logsum
    )
    grad_normed = lax.psum_scatter(
        dot(grad_projected, own_qkv.T).astype(BF), "seq", scatter_dimension=0, tiled=True
    ).astype(F32)
    grad_qkv = dot(normed_all.T, grad_projected)
    grad_input = (grad_hidden + norm_back(inputs, scale_one, full_gone, grad_normed)).astype(BF)

    shards, copies = lax.axis_size("shard"), lax.axis_size("replica")
    cut = lambda grad: grad.astype(BF).reshape(shards, -1, 8, width)
    parts = [
        cut(dot(normed_two_b.T, grad_upper_b[:, i * width : (i + 1) * width]))
        for i in range(grad_upper_b.shape[1] // width)
    ]
    parts += [cut(dot(active_b.T, incoming)), cut(dot(attended_b.T, grad_hidden_b))]
    sizes = [part.shape[1] for part in parts]
    groups = -(-sum(sizes) // (copies * blocks))
    chunks = -(-groups // max(1, groups // 9))
    per = max(1, groups // 9) * copies * blocks
    spare = chunks * per - sum(sizes)
    if spare:
        parts.append(jnp.zeros((shards, spare, 8, width), BF))
    big = jnp.concatenate(parts, axis=1).reshape(shards // 2, 2, chunks, per, 8, width)
    taps = grad_conv.shape[0]
    extra = jnp.pad(grad_conv.astype(BF), ((0, 8 - taps), (0, 0)))
    mine = depth // 8
    uq = -(-(mine + 1) // copies) * copies
    qkv = jnp.concatenate(
        [
            grad_qkv.astype(BF).reshape(shards, mine, 8, 3 * own),
            jnp.broadcast_to(extra, (shards, 1, 8, 3 * own)),
            jnp.zeros((shards, uq - mine - 1, 8, 3 * own), BF),
        ],
        axis=1,
    ).reshape(shards // 2, 2, uq, 8, 3 * own)
    sums, own_sums = reduce_grads(big, qkv, copies, blocks)
    sums = sums.reshape(-1, 8, width)
    cuts = [sum(sizes[:i]) for i in range(len(sizes) + 1)]
    pieces = [sums[lo:hi].reshape(-1, width).astype(F32) for lo, hi in zip(cuts, cuts[1:])]
    total_up = jnp.concatenate(pieces[:-2], axis=1)

    def merge(array):
        return jnp.concatenate(
            [array[j, :, p * own : (p + 1) * own] for p in range(3) for j in range(blocks)], axis=1
        ).astype(F32)

    total_qkv = merge(own_sums[:, :mine].reshape(blocks, depth, 3 * own))
    total_conv = merge(own_sums[:, mine, :taps])
    at = lax.axis_index("shard")

    def gain_grad(grad, weight, gain):
        return jnp.sum(grad * weight.astype(F32), axis=1) / gain.astype(F32)

    return (
        output[None].astype(BF),
        grad_input[None],
        total_qkv,
        pieces[-1],
        total_up,
        pieces[-2],
        lax.dynamic_slice_in_dim(total_conv, at * conv_w.shape[1], conv_w.shape[1], 1),
        gain_grad(total_qkv, w_qkv, gain_attn),
        gain_grad(total_up, w_up, gain_ffn),
    )


def solution(mesh):
    placed = (
        P(("shard", "replica"), "seq", None),
        P(("shard", "replica")),
        P("shard", None),
        P("shard", None),
        P("shard", None),
        P("shard", None),
        P(None, "shard"),
        P("shard"),
        P("shard"),
        P(("shard", "replica"), "seq", None),
    )
    return jax.shard_map(
        per_device,
        mesh=mesh,
        in_specs=placed,
        out_specs=(
            P(("shard", "replica"), "seq", None),
            P(("shard", "replica"), "seq", None),
            P("shard", None),
            P("shard", None),
            P("shard", None),
            P("shard", None),
            P(None, "shard"),
            P("shard"),
            P("shard"),
        ),
        check_vma=False,
    )
```

```python
import functools

import jax
import jax.numpy as jnp
from jax import lax
from jax.experimental import pallas as pl
from jax.experimental.pallas import tpu as pltpu
from jax.sharding import PartitionSpec as P

HEADS = 12
HEAD_DIM=64
NEG=-1e30
F32=jnp.float32
BF=jnp.bfloat16

def nt(a,b):
    return lax.dot_general(a,b,(((1,),(1,)),((),())),preferred_element_type=F32)
def tn(a,b):
    return lax.dot_general(a,b,(((0,),(0,)),((),())),preferred_element_type=F32)

def convolve(proj_ref, conv_ref, wide, heads, parts):
    length, width = proj_ref.shape
    rows = min(512, length)
    wide[0:8] = jnp.zeros((8, width), F32)
    taps = conv_ref[...].astype(F32)
    for c in range(length//rows):
        wide[8+c*rows:8+(c+1)*rows] = proj_ref[c*rows:(c+1)*rows].astype(F32)
    def body(c, _):
        base = pl.multiple_of(c*rows, rows)
        x = wide[pl.ds(base, rows+8)]
        mixed = taps[0:1]*x[8:] + taps[1:2]*x[7:7+rows] + taps[2:3]*x[6:6+rows]
        for p,ref in enumerate(parts):
            for h in range(heads):
                lo = (p*heads+h)*HEAD_DIM
                piece = mixed[:, lo:lo+HEAD_DIM].astype(BF)
                if p == 0:
                    piece = piece * jnp.asarray(HEAD_DIM**-0.5, BF)
                ref[h, pl.ds(base, rows)] = piece
        return 0
    lax.fori_loop(0, length//rows, body, 0)

def mask_t(i, j, rows, prefix):
    kpos = j*rows + lax.broadcasted_iota(jnp.int32, (rows, 1), 0)
    qpos = i*rows + lax.broadcasted_iota(jnp.int32, (1, rows), 1)
    return (kpos <= qpos) | ((kpos < prefix) & (qpos < prefix))

def mask_n(i, j, rows, prefix):
    qpos = i*rows + lax.broadcasted_iota(jnp.int32, (rows, 1), 0)
    kpos = j*rows + lax.broadcasted_iota(jnp.int32, (1, rows), 1)
    return (kpos <= qpos) | ((kpos < prefix) & (qpos < prefix))

MESH = pl.DeviceIdType.MESH


def remote(src, dst, send, recv, peer):
    return pltpu.make_async_remote_copy(
        src_ref=src, dst_ref=dst, send_sem=send, recv_sem=recv, device_id=peer, device_id_type=MESH
    )


def greet(peers):
    barrier = pltpu.get_barrier_semaphore()
    for peer in peers:
        pl.semaphore_signal(barrier, inc=1, device_id=peer, device_id_type=MESH)
    pl.semaphore_wait(barrier, len(peers))


def fwd_kernel(prefix_ref, proj_ref, conv_ref, own_ref, lse_ref, rows_ref, wide, qs, ks, vs, m_s, l_s, acc_s, o_s, r_s, send, recv):
    heads = qs.shape[0]
    length = proj_ref.shape[0]
    blocks = own_ref.shape[1]
    rows = length // blocks
    prefix = prefix_ref[0]
    z, s_at, x = lax.axis_index("seq"), lax.axis_index("shard"), lax.axis_index("replica")

    def block_copy(h, i, at):
        return remote(o_s.at[h, i], r_s.at[at * heads + h], send.at[h, i], recv.at[h, at], (i, s_at, x))

    greet([((z + i) % blocks, s_at, x) for i in range(1, blocks)])
    convolve(proj_ref, conv_ref, wide, heads, (qs, ks, vs))
    def head(h, _):
        def qblock(i, _):
            q = qs[h, pl.ds(pl.multiple_of(i*rows, rows), rows)]
            m_s[...] = jnp.full((1, rows), NEG, F32)
            l_s[...] = jnp.zeros((1, rows), F32)
            acc_s[...] = jnp.zeros((HEAD_DIM, rows), F32)
            def step(j, masked):
                at = pl.ds(pl.multiple_of(j*rows, rows), rows)
                s = nt(ks[h, at], q)
                if masked:
                    s = jnp.where(mask_t(i, j, rows, prefix), s, NEG)
                m_old = m_s[...]
                m_new = jnp.maximum(m_old, jnp.max(s, axis=0, keepdims=True))
                p = jnp.exp(s - m_new)
                a = jnp.exp(m_old - m_new)
                m_s[...] = m_new
                l_s[...] = a*l_s[...] + jnp.sum(p, axis=0, keepdims=True)
                acc_s[...] = a*acc_s[...] + tn(vs[h, at], p.astype(BF))
                return 0
            lax.fori_loop(0, i, lambda j, _: step(j, False), 0)
            lax.fori_loop(i, jnp.maximum(i+1, blocks//2), lambda j, _: step(j, True), 0)
            l = l_s[...]
            done = (acc_s[...]/l).astype(BF)
            o_s[h, i] = done
            own_ref[h, i] = done
            @pl.when(i != z)
            def _():
                block_copy(h, i, z).start()
            lse = m_s[...] + jnp.log(l)
            lse_ref[h, :, pl.ds(pl.multiple_of(i*rows, rows), rows)] = jnp.broadcast_to(lse, (8, rows))
            return 0
        lax.fori_loop(0, blocks, qblock, 0)
        r_s[z * heads + h] = o_s[h, z]
        return 0
    lax.fori_loop(0, heads, head, 0)
    def finish(h, _):
        for i in range(1, blocks):
            there = (z + i) % blocks
            block_copy(h, there, there).wait_recv()
            block_copy(h, there, z).wait_send()
        return 0
    lax.fori_loop(0, heads, finish, 0)
    rows_ref[...] = r_s[...]

def attention_fwd(prefix, proj, conv, blocks):
    length, width = proj.shape
    heads = width//(3*HEAD_DIM)
    rows = length // blocks
    vm = pl.BlockSpec(memory_space=pltpu.VMEM)
    own = (heads, blocks, HEAD_DIM, rows)
    every = (heads * blocks, HEAD_DIM, rows)
    return pl.pallas_call(
        fwd_kernel,
        out_shape=(jax.ShapeDtypeStruct(own, BF), jax.ShapeDtypeStruct((heads, 8, length), F32), jax.ShapeDtypeStruct(every, BF)),
        in_specs=[pl.BlockSpec(memory_space=pltpu.SMEM), vm, vm],
        out_specs=(vm, vm, vm),
        scratch_shapes=[pltpu.VMEM((8+length, width), F32)] + [pltpu.VMEM((heads, length, HEAD_DIM), BF)]*3 + [
            pltpu.VMEM((1,rows),F32), pltpu.VMEM((1,rows),F32), pltpu.VMEM((HEAD_DIM,rows),F32), pltpu.VMEM(own,BF), pltpu.VMEM(every,BF),
            pltpu.SemaphoreType.DMA((heads, blocks)), pltpu.SemaphoreType.DMA((heads, blocks))],
        compiler_params=pltpu.CompilerParams(vmem_limit_bytes=60*1024*1024, collective_id=2, has_side_effects=True),
        cost_estimate=pl.CostEstimate(flops=4*heads*length*length*HEAD_DIM, bytes_accessed=length*width*2, transcendentals=heads*length*length),
        name="attention_fwd",
    )(prefix, proj, conv)

def split_shard():
    s = lax.axis_index("shard")
    return lax.axis_index("seq"), s // 2, s % 2, lax.axis_index("replica")


class Sums:
    def __init__(self, parts, out_ref, bufs, sems, nz):
        self.parts, self.out = parts, out_ref
        self.a, self.b, self.c, self.d = bufs
        self.sa, self.ra, self.sb, self.rb, self.sc, self.rc, self.sd, self.rd, self.se, self.re, self.sf, self.rf = sems
        self.chunks, self.ny = self.a.shape[:2]
        self.nx = self.c.shape[1]
        self.nz = nz
        self.half = self.c.shape[2]
        self.piece = self.half // nz
        self.me = split_shard()
        z, y, c, x = self.me
        self.core = (z, 2 * y + 1 - c, x)

    def py(self, i):
        return (self.me[1] + i) % self.ny

    def px(self, i):
        return (self.me[3] + i) % self.nx

    def pz(self, i):
        return (self.me[0] + i) % self.nz

    def dy(self, i):
        z, y, c, x = self.me
        return (z, 2 * self.py(i) + c, x)

    def dx(self, i):
        z, y, c, x = self.me
        return (z, 2 * y + c, self.px(i))

    def dz(self, i):
        z, y, c, x = self.me
        return (self.pz(i), 2 * y + c, x)

    def peers(self):
        out = [self.core] + [self.dy(i) for i in range(1, self.ny)]
        out += [self.dx(i) for i in range(1, self.nx)]
        return out + [self.dz(i) for i in range(1, self.nz)]

    def copy_a(self, k, src):
        return remote(src, self.a.at[k], self.sa.at[k], self.ra.at[k], self.core)

    def start(self):
        c = self.me[2]
        for ref, first, count in self.parts:
            for j in range(count):
                src = ref.at[:, 1 - c, j]
                self.copy_a(first + j, src).start()

    def copy_b(self, k, i, there):
        slot = self.me[1] if there else self.py(i)
        return remote(self.a.at[k, self.py(i)], self.b.at[k, slot], self.sb.at[k, self.py(i)], self.rb.at[k, slot], self.dy(i))

    def stage_b(self, k):
        c = self.me[2]
        self.copy_a(k, self.a.at[k]).wait_recv()
        for i in list(range(1, self.ny)) + [0]:
            p = self.py(i)
            for ref, first, count in self.parts:
                @pl.when((k >= first) & (k < first + count))
                def _():
                    j = jnp.clip(k - first, 0, count - 1)
                    self.a[k, p] = (self.a[k, p].astype(F32) + ref[p, c, j].astype(F32)).astype(BF)
            if i:
                self.copy_b(k, i, True).start()

    def copy_c(self, k, i, there):
        slot = self.me[3] if there else self.px(i)
        src = self.a.at[k, self.me[1], pl.ds(self.px(i) * self.half, self.half)]
        return remote(src, self.c.at[k, slot], self.sc.at[k, self.px(i)], self.rc.at[k, slot], self.dx(i))

    def stage_c(self, k):
        y = self.me[1]
        total = self.a[k, y].astype(F32)
        for i in range(1, self.ny):
            self.copy_b(k, i, False).wait_recv()
            total = total + self.b[k, self.py(i)].astype(F32)
        for i in range(1, self.ny):
            self.copy_b(k, i, True).wait_send()
        self.a[k, y] = total.astype(BF)
        for i in range(1, self.nx):
            self.copy_c(k, i, True).start()

    def copy_d(self, k, i, there):
        z, y, c, x = self.me
        slot = z if there else self.pz(i)
        src = self.a.at[k, y, pl.ds(x * self.half + self.pz(i) * self.piece, self.piece)]
        return remote(src, self.d.at[k, slot], self.sd.at[k, self.pz(i)], self.rd.at[k, slot], self.dz(i))

    def stage_d(self, k):
        z, y, c, x = self.me
        mine = pl.ds(x * self.half, self.half)
        total = self.a[k, y, mine].astype(F32)
        for i in range(1, self.nx):
            self.copy_c(k, i, False).wait_recv()
            total = total + self.c[k, self.px(i)].astype(F32)
        for i in range(1, self.nx):
            self.copy_c(k, i, True).wait_send()
        self.a[k, y, mine] = total.astype(BF)
        for i in range(1, self.nz):
            self.copy_d(k, i, True).start()

    def copy_e(self, k, i, there):
        slot = self.me[0] if there else self.pz(i)
        ref = self.out.at[k, pl.ds(self.me[3] * self.half + slot * self.piece, self.piece)]
        return remote(ref, ref, self.se.at[k, self.pz(i)], self.re.at[k, slot], self.dz(i))

    def stage_e(self, k):
        z, y, c, x = self.me
        mine = pl.ds(x * self.half + z * self.piece, self.piece)
        total = self.a[k, y, mine].astype(F32)
        for i in range(1, self.nz):
            self.copy_d(k, i, False).wait_recv()
            total = total + self.d[k, self.pz(i)].astype(F32)
        self.out[k, mine] = total.astype(BF)
        for i in range(1, self.nz):
            self.copy_e(k, i, True).start()

    def copy_f(self, k, i, there):
        slot = self.me[3] if there else self.px(i)
        ref = self.out.at[k, pl.ds(slot * self.half, self.half)]
        return remote(ref, ref, self.sf.at[k, self.px(i)], self.rf.at[k, slot], self.dx(i))

    def stage_f(self, k):
        for i in range(1, self.nz):
            self.copy_e(k, i, False).wait_recv()
        for i in range(1, self.nx):
            self.copy_f(k, i, True).start()

    def step(self, t):
        for lag, stage in enumerate((self.stage_c, self.stage_d, self.stage_e, self.stage_f)):
            @pl.when((t >= lag) & (t < self.chunks + lag))
            def _():
                stage(t - lag)

    def finish(self):
        def body(k, _):
            for i in range(1, self.nx):
                self.copy_f(k, i, False).wait_recv()
            self.copy_a(k, self.a.at[k]).wait_send()
            for i in range(1, self.nx):
                self.copy_f(k, i, True).wait_send()
            for i in range(1, self.nz):
                self.copy_d(k, i, True).wait_send()
                self.copy_e(k, i, True).wait_send()
            return 0

        lax.fori_loop(0, self.chunks, body, 0)

    @staticmethod
    def sems(chunks, ny, nx, nz):
        out = [pltpu.SemaphoreType.DMA((chunks,))] * 2
        for n in (ny, nx, nz, nz, nx):
            out += [pltpu.SemaphoreType.DMA((chunks, n))] * 2
        return out


def bwd_kernel(counts, *refs):
    parts_n = len(counts)
    prefix_ref, proj_ref, conv_ref, do_ref, o_ref, lse_ref = refs[:6]
    part_refs = refs[6:6 + parts_n]
    gp_ref, gconv_ref, sum_ref = refs[6 + parts_n:9 + parts_n]
    wide, qs, ks, vs, dos, delta, dq, dk, dv, gq, gk, gv, gwide, send, recv = refs[9 + parts_n:24 + parts_n]
    bufs = refs[24 + parts_n:28 + parts_n]
    sems = refs[28 + parts_n:]
    heads = qs.shape[0]
    length, width = proj_ref.shape
    blocks = dos.shape[1]
    rows = length//blocks
    prefix = prefix_ref[0]
    parts = []
    first = 0
    for ref, count in zip(part_refs, counts):
        parts.append((ref, first, count))
        first += count
    sums = Sums(parts, sum_ref, bufs, sems, blocks)
    z, y, c, x = sums.me
    greet(sums.peers())
    sums.start()

    def block_copy(h, i, at):
        return remote(do_ref.at[i * heads + h], dos.at[h, at], send.at[h, i], recv.at[h, at], (i, 2 * y + c, x))

    for h in range(heads):
        for i in range(1, blocks):
            block_copy(h, (z + i) % blocks, z).start()
        dos[h, z] = do_ref[z * heads + h]
    convolve(proj_ref, conv_ref, wide, heads, (qs, ks, vs))

    def head(h, _):
        for i in range(1, blocks):
            there = (z + i) % blocks
            block_copy(h, there, there).wait_recv()
        for i in range(blocks):
            prod = dos[h, i].astype(F32) * o_ref[h, i].astype(F32)
            delta[i] = jnp.broadcast_to(jnp.sum(prod, axis=0, keepdims=True), (8, rows))
        dq[...] = jnp.zeros(dq.shape, F32)
        def kblock(j, _):
            t = h*blocks + j
            @pl.when(t < sums.chunks)
            def _():
                sums.stage_b(t)
            turn = (2*t)//3
            @pl.when((turn > 0) & ((2*t)%3 != 2))
            def _():
                sums.step(turn - 1)
            kat = pl.ds(pl.multiple_of(j*rows, rows), rows)
            k = ks[h, kat]; v = vs[h, kat]
            dk[...] = jnp.zeros(dk.shape, F32)
            dv[...] = jnp.zeros(dv.shape, F32)
            def step(i, masked):
                qat = pl.ds(pl.multiple_of(i*rows, rows), rows)
                q = qs[h, qat]; do = dos[h, i]
                s = nt(k, q)
                p = jnp.exp(s - lse_ref[h, 0:1, qat])
                if masked:
                    p = jnp.where(mask_t(i, j, rows, prefix), p, 0.0)
                dv[...] += nt(p.astype(BF), do)
                dp = jnp.dot(v, do, preferred_element_type=F32)
                ds = (p*(dp - delta[i, 0:1])).astype(BF)
                dk[...] += jnp.dot(ds, q, preferred_element_type=F32)
                dq[qat] += tn(ds, k)
                return 0
            lax.fori_loop(j+1, blocks, lambda i, _: step(i, False), 0)
            lax.fori_loop(jnp.where(j < blocks//2, 0, j), j+1, lambda i, _: step(i, True), 0)
            gk[h, kat] = dk[...].astype(BF)
            gv[h, kat] = dv[...].astype(BF)
            return 0
        lax.fori_loop(0, blocks, kblock, 0)
        def qout(c, _):
            at = pl.ds(pl.multiple_of(c*rows, rows), rows)
            gq[h, at] = (dq[at]*(HEAD_DIM**-0.5)).astype(BF)
            return 0
        lax.fori_loop(0, blocks, qout, 0)
        return 0
    lax.fori_loop(0, heads, head, 0)
    steps = heads*blocks
    turns = (2*(steps - 1))//3
    def rest(t, _):
        sums.stage_b(t)
        return 0
    lax.fori_loop(steps, sums.chunks, rest, 0)
    taps = conv_ref[...].astype(F32)
    gwide[length:length+8] = jnp.zeros((8, width), F32)
    def fill(c, _):
        at = pl.ds(pl.multiple_of(c*rows, rows), rows)
        gwide[at] = jnp.concatenate([r[h, at] for r in (gq, gk, gv) for h in range(heads)], axis=1).astype(F32)
        return 0
    lax.fori_loop(0, blocks, fill, 0)
    def out(c, total):
        sums.step(turns + c)
        base = pl.multiple_of(c*rows, rows)
        g = gwide[pl.ds(base, rows+8)]
        x = wide[pl.ds(base, rows+8)]
        g0 = g[:rows]
        gp = taps[0:1]*g0 + taps[1:2]*g[1:rows+1] + taps[2:3]*g[2:rows+2]
        gp_ref[pl.ds(base, rows)] = gp.astype(BF)
        add = [jnp.sum(g0*x[8-t:8-t+rows], axis=0, keepdims=True) for t in range(3)]
        return tuple(a+b for a, b in zip(total, add))
    total = lax.fori_loop(0, blocks, out, tuple(jnp.zeros((1, width), F32) for _ in range(3)))
    gconv_ref[...] = jnp.concatenate(total, axis=0)
    def tail(t, _):
        sums.step(t)
        return 0
    lax.fori_loop(turns + blocks, max(sums.chunks + 3, turns + blocks), tail, 0)
    sums.finish()
    def sent(h, _):
        for i in range(1, blocks):
            block_copy(h, (z + i) % blocks, z).wait_send()
        return 0
    lax.fori_loop(0, heads, sent, 0)

def attention_bwd(prefix, proj, conv, do, o, lse, parts, nx):
    length, width = proj.shape
    heads, blocks = o.shape[:2]
    rows = length // blocks
    counts = tuple(part.shape[2] for part in parts)
    ny, _, _, units = parts[0].shape[:4]
    unit = parts[0].shape[4:]
    chunks = sum(counts)
    half = units // nx
    vm = pl.BlockSpec(memory_space=pltpu.VMEM)
    per = lambda dt: pltpu.VMEM((heads, length, HEAD_DIM), dt)
    return pl.pallas_call(
        functools.partial(bwd_kernel, counts),
        out_shape=(jax.ShapeDtypeStruct((length, width), BF), jax.ShapeDtypeStruct((3, width), F32), jax.ShapeDtypeStruct((chunks, units) + unit, BF)),
        in_specs=[pl.BlockSpec(memory_space=pltpu.SMEM)] + [vm]*(5 + len(parts)),
        out_specs=(vm, vm, vm),
        scratch_shapes=[pltpu.VMEM((8+length, width), F32), per(BF), per(BF), per(BF), pltpu.VMEM(o.shape, BF), pltpu.VMEM((blocks, 8, rows), F32),
            pltpu.VMEM((length, HEAD_DIM), F32), pltpu.VMEM((rows, HEAD_DIM), F32), pltpu.VMEM((rows, HEAD_DIM), F32),
            per(BF), per(BF), per(BF), pltpu.VMEM((length+8, width), F32),
            pltpu.SemaphoreType.DMA((heads, blocks)), pltpu.SemaphoreType.DMA((heads, blocks)),
            pltpu.VMEM((chunks, ny, units) + unit, BF), pltpu.VMEM((chunks, ny, units) + unit, BF),
            pltpu.VMEM((chunks, nx, half) + unit, BF), pltpu.VMEM((chunks, blocks, half // blocks) + unit, BF)]
            + Sums.sems(chunks, ny, nx, blocks),
        compiler_params=pltpu.CompilerParams(vmem_limit_bytes=67043328, collective_id=3, has_side_effects=True),
        cost_estimate=pl.CostEstimate(flops=10*heads*length*length*HEAD_DIM, bytes_accessed=length*width*4, transcendentals=heads*length*length),
        name="attention_bwd",
    )(prefix, proj, conv, do, o, lse, *parts)


def qkv_kernel(part_ref, out_ref, qa, qb, qc, sa, ra, sb, rb, sc, rc, se, re, sf, rf, *, nx, nz):
    ny = part_ref.shape[0]
    half = part_ref.shape[2] // nx
    z, y, c, x = split_shard()
    core = (z, 2 * y + 1 - c, x)

    def py(i):
        return (y + i) % ny

    def px(i):
        return (x + i) % nx

    def pz(i):
        return (z + i) % nz

    def dy(i):
        return (z, 2 * py(i) + c, x)

    def dx(i):
        return (z, 2 * y + c, px(i))

    def dz(i):
        return (pz(i), 2 * y + c, x)

    def to_y(i, there):
        slot = y if there else py(i)
        return remote(qa.at[py(i)], qb.at[slot], sb.at[py(i)], rb.at[slot], dy(i))

    def to_x(i, there):
        slot = x if there else px(i)
        return remote(qa.at[y, pl.ds(px(i) * half, half)], qc.at[slot], sc.at[px(i)], rc.at[slot], dx(i))

    def on_z(i, there):
        slot = z if there else pz(i)
        ref = out_ref.at[slot, pl.ds(x * half, half)]
        return remote(ref, ref, se.at[pz(i)], re.at[slot], dz(i))

    def on_x(i, j, there):
        slot = x if there else px(j)
        ref = out_ref.at[pz(i), pl.ds(slot * half, half)]
        return remote(ref, ref, sf.at[pz(i), px(j)], rf.at[pz(i), slot], dx(j))

    greet([core] + [dy(i) for i in range(1, ny)] + [dx(i) for i in range(1, nx)] + [dz(i) for i in range(1, nz)])
    first = remote(part_ref.at[:, 1 - c], qa, sa.at[0], ra.at[0], core)
    first.start()
    first.wait_recv()
    for i in list(range(1, ny)) + [0]:
        qa[py(i)] = (qa[py(i)].astype(F32) + part_ref[py(i), c].astype(F32)).astype(BF)
        if i:
            to_y(i, True).start()
    total = qa[y].astype(F32)
    for i in range(1, ny):
        to_y(i, False).wait_recv()
        total = total + qb[py(i)].astype(F32)
    qa[y] = total.astype(BF)
    for i in range(1, nx):
        to_x(i, True).start()
    mine = pl.ds(x * half, half)
    total = qa[y, mine].astype(F32)
    for i in range(1, nx):
        to_x(i, False).wait_recv()
        total = total + qc[px(i)].astype(F32)
    out_ref[z, mine] = total.astype(BF)
    for i in range(1, nz):
        on_z(i, True).start()
    for i in range(nz):
        if i:
            on_z(i, False).wait_recv()
        for j in range(1, nx):
            on_x(i, j, True).start()
    for i in range(nz):
        for j in range(1, nx):
            on_x(i, j, False).wait_recv()
            on_x(i, j, True).wait_send()
    first.wait_send()
    for i in range(1, ny):
        to_y(i, True).wait_send()
    for i in range(1, nx):
        to_x(i, True).wait_send()
    for i in range(1, nz):
        on_z(i, True).wait_send()


def reduce_qkv(part, nx, nz):
    ny, _, units = part.shape[:3]
    unit = part.shape[3:]
    vm = pl.BlockSpec(memory_space=pltpu.VMEM)
    dma = pltpu.SemaphoreType.DMA
    return pl.pallas_call(
        functools.partial(qkv_kernel, nx=nx, nz=nz),
        out_shape=jax.ShapeDtypeStruct((nz, units) + unit, BF),
        in_specs=[vm],
        out_specs=vm,
        scratch_shapes=[
            pltpu.VMEM((ny, units) + unit, BF),
            pltpu.VMEM((ny, units) + unit, BF),
            pltpu.VMEM((nx, units // nx) + unit, BF),
        ]
        + [dma((1,))] * 2
        + [dma((ny,))] * 2
        + [dma((nx,))] * 2
        + [dma((nz,))] * 2
        + [dma((nz, nx))] * 2,
        compiler_params=pltpu.CompilerParams(
            collective_id=1, has_side_effects=True, vmem_limit_bytes=60 * 1024 * 1024
        ),
        name="reduce_qkv",
    )(part)


def rms_scale(values):
    return lax.rsqrt(jnp.mean(values * values, axis=-1, keepdims=True) + 1e-06)


def norm_back(values, scale_rows, gain, upstream):
    weighted = upstream * gain
    grad_values = scale_rows * weighted - values * scale_rows**3 * jnp.mean(
        weighted * values, axis=-1, keepdims=True
    )
    return grad_values


def dot(a, b):
    return jnp.dot(a, b, preferred_element_type=F32)


def per_device(
    tokens, prefix_len, w_qkv, w_out, w_up, w_down, conv_w, gain_attn, gain_ffn, cotangent
):
    blocks = lax.axis_size("seq")
    me = lax.axis_index("seq")
    rows, width = tokens.shape[1:]
    own = HEADS // blocks * HEAD_DIM
    depth = w_qkv.shape[0]

    tokens_all = lax.all_gather(tokens[0], "seq", axis=0, tiled=True)
    columns = lax.dynamic_index_in_dim(w_qkv.reshape(depth, 3, blocks, own), me, 2, False)
    own_qkv = lax.all_gather(columns.reshape(depth, 3 * own), "shard", axis=0, tiled=True)
    small = jnp.concatenate([gain_attn, gain_ffn, conv_w.reshape(-1)])
    small = lax.all_gather(small, "shard", axis=0)
    full_gone = small[:, :depth].reshape(width).astype(F32)
    full_gtwo = small[:, depth : 2 * depth].reshape(width).astype(F32)
    full_conv = small[:, 2 * depth :].reshape(-1, 3, conv_w.shape[1]).transpose(1, 0, 2)
    own_conv = lax.dynamic_index_in_dim(full_conv.reshape(3, 3, blocks, own), me, 2, False)
    own_conv = own_conv.reshape(3, 3 * own)
    full_out = lax.all_gather(w_out, "shard", axis=0, tiled=True)
    full_up = lax.all_gather(w_up, "shard", axis=0, tiled=True)
    full_down = lax.all_gather(w_down, "shard", axis=0, tiled=True)

    whole = tokens_all.astype(F32)
    normed_all = (whole * rms_scale(whole) * full_gone).astype(BF)
    projected = dot(normed_all, own_qkv).astype(BF)
    attended_own, logsum, attended = attention_fwd(prefix_len, projected, own_conv, blocks)
    attended = attended.reshape(width, rows)

    inputs = tokens[0].astype(F32)
    scale_one = rms_scale(inputs)
    hidden = inputs + tn(attended, full_out)
    scale_two = rms_scale(hidden)
    normed_two_b = (hidden * scale_two * full_gtwo).astype(BF)
    positive = jnp.maximum(dot(normed_two_b, full_up), 0.0)
    active_b = (positive * positive).astype(BF)
    output = hidden + dot(active_b, full_down)

    incoming = cotangent[0]
    grad_upper_b = (dot(incoming, full_down.T) * 2.0 * positive).astype(BF)
    grad_normed_two = dot(grad_upper_b, full_up.T)
    grad_hidden = incoming.astype(F32) + norm_back(hidden, scale_two, full_gtwo, grad_normed_two)
    grad_hidden_b = grad_hidden.astype(BF)
    grad_attended = nt(full_out, grad_hidden_b).astype(BF)

    shards, copies = lax.axis_size("shard"), lax.axis_size("replica")
    mine = depth // 8

    def cut(grad):
        return grad.astype(BF).reshape(shards // 2, 2, -1, mine, 8, width)

    parts = [
        cut(dot(normed_two_b.T, grad_upper_b[:, i * width : (i + 1) * width]))
        for i in range(grad_upper_b.shape[1] // width)
    ]
    parts += [cut(dot(active_b.T, incoming)), cut(dot(attended, grad_hidden_b))]
    pieces = sum(part.shape[2] for part in parts)
    if mine % (copies * blocks):
        units = -(-pieces * mine // (copies * blocks)) * copies * blocks
        joined = [part.reshape(shards // 2, 2, -1, 8, width) for part in parts]
        joined.append(jnp.zeros((shards // 2, 2, units - pieces * mine, 8, width), BF))
        joined = jnp.concatenate(joined, axis=2)
        parts = [joined.reshape(shards // 2, 2, -1, copies * blocks, 8, width)]

    grad_projected, grad_conv, sums = attention_bwd(
        prefix_len, projected, own_conv, grad_attended.reshape(HEADS, HEAD_DIM, rows),
        attended_own, logsum, parts, copies,
    )
    grad_normed = lax.psum_scatter(
        dot(grad_projected, own_qkv.T).astype(BF), "seq", scatter_dimension=0, tiled=True
    ).astype(F32)
    grad_qkv = dot(normed_all.T, grad_projected)
    grad_input = (grad_hidden + norm_back(inputs, scale_one, full_gone, grad_normed)).astype(BF)

    taps = grad_conv.shape[0]
    extra = jnp.pad(grad_conv.astype(BF), ((0, 8 - taps), (0, 0)))
    uq = -(-(mine + 1) // copies) * copies
    qkv = jnp.concatenate(
        [
            grad_qkv.astype(BF).reshape(shards, mine, 8, 3 * own),
            jnp.broadcast_to(extra, (shards, 1, 8, 3 * own)),
            jnp.zeros((shards, uq - mine - 1, 8, 3 * own), BF),
        ],
        axis=1,
    ).reshape(shards // 2, 2, uq, 8, 3 * own)
    own_sums = reduce_qkv(qkv, copies, blocks)
    sums = sums.reshape(-1, 8, width)[: pieces * mine].reshape(pieces, depth, width)
    ups = w_up.shape[1] // width
    total_up = jnp.concatenate(list(sums[:ups]), axis=1).astype(F32)
    total_down = sums[ups:-1].reshape(-1, width).astype(F32)
    total_out = sums[-1].astype(F32)

    def merge(array):
        return jnp.concatenate(
            [array[j, :, p * own : (p + 1) * own] for p in range(3) for j in range(blocks)], axis=1
        ).astype(F32)

    total_qkv = merge(own_sums[:, :mine].reshape(blocks, depth, 3 * own))
    total_conv = merge(own_sums[:, mine, :taps])
    at = lax.axis_index("shard")

    def gain_grad(grad, weight, gain):
        return jnp.sum(grad * weight.astype(F32), axis=1) / gain.astype(F32)

    return (
        output[None].astype(BF),
        grad_input[None],
        total_qkv,
        total_out,
        total_up,
        total_down,
        lax.dynamic_slice_in_dim(total_conv, at * conv_w.shape[1], conv_w.shape[1], 1),
        gain_grad(total_qkv, w_qkv, gain_attn),
        gain_grad(total_up, w_up, gain_ffn),
    )


def solution(mesh):
    placed = (
        P(("shard", "replica"), "seq", None),
        P(("shard", "replica")),
        P("shard", None),
        P("shard", None),
        P("shard", None),
        P("shard", None),
        P(None, "shard"),
        P("shard"),
        P("shard"),
        P(("shard", "replica"), "seq", None),
    )
    return jax.shard_map(
        per_device,
        mesh=mesh,
        in_specs=placed,
        out_specs=(
            P(("shard", "replica"), "seq", None),
            P(("shard", "replica"), "seq", None),
            P("shard", None),
            P("shard", None),
            P("shard", None),
            P("shard", None),
            P(None, "shard"),
            P("shard"),
            P("shard"),
        ),
        check_vma=False,
    )
```

```python
import functools

import jax
import jax.numpy as jnp
from jax import lax
from jax.experimental import pallas as pl
from jax.experimental.pallas import tpu as pltpu
from jax.sharding import PartitionSpec as P

HEADS = 12
HEAD_DIM=64
NEG=-1e30
F32=jnp.float32
BF=jnp.bfloat16

def nt(a,b):
    return lax.dot_general(a,b,(((1,),(1,)),((),())),preferred_element_type=F32)
def tn(a,b):
    return lax.dot_general(a,b,(((0,),(0,)),((),())),preferred_element_type=F32)

def convolve(proj_ref, conv_ref, wide, heads, parts):
    length, width = proj_ref.shape
    rows = min(512, length)
    wide[0:8] = jnp.zeros((8, width), F32)
    taps = conv_ref[...].astype(F32)
    for c in range(length//rows):
        wide[8+c*rows:8+(c+1)*rows] = proj_ref[c*rows:(c+1)*rows].astype(F32)
    def body(c, _):
        base = pl.multiple_of(c*rows, rows)
        x = wide[pl.ds(base, rows+8)]
        mixed = taps[0:1]*x[8:] + taps[1:2]*x[7:7+rows] + taps[2:3]*x[6:6+rows]
        for p,ref in enumerate(parts):
            for h in range(heads):
                lo = (p*heads+h)*HEAD_DIM
                piece = mixed[:, lo:lo+HEAD_DIM].astype(BF)
                if p == 0:
                    piece = piece * jnp.asarray(HEAD_DIM**-0.5, BF)
                ref[h, pl.ds(base, rows)] = piece
        return 0
    lax.fori_loop(0, length//rows, body, 0)

def mask_t(i, j, rows, prefix):
    kpos = j*rows + lax.broadcasted_iota(jnp.int32, (rows, 1), 0)
    qpos = i*rows + lax.broadcasted_iota(jnp.int32, (1, rows), 1)
    return (kpos <= qpos) | ((kpos < prefix) & (qpos < prefix))

def mask_n(i, j, rows, prefix):
    qpos = i*rows + lax.broadcasted_iota(jnp.int32, (rows, 1), 0)
    kpos = j*rows + lax.broadcasted_iota(jnp.int32, (1, rows), 1)
    return (kpos <= qpos) | ((kpos < prefix) & (qpos < prefix))

MESH = pl.DeviceIdType.MESH


def remote(src, dst, send, recv, peer):
    return pltpu.make_async_remote_copy(
        src_ref=src, dst_ref=dst, send_sem=send, recv_sem=recv, device_id=peer, device_id_type=MESH
    )


def greet(peers):
    barrier = pltpu.get_barrier_semaphore()
    for peer in peers:
        pl.semaphore_signal(barrier, inc=1, device_id=peer, device_id_type=MESH)
    pl.semaphore_wait(barrier, len(peers))


def split_shard():
    s = lax.axis_index("shard")
    return lax.axis_index("seq"), s // 2, s % 2, lax.axis_index("replica")


class Gather:
    def __init__(self, src, dst, sems):
        self.src, self.dst = src, dst
        self.sy, self.ry, self.sk, self.rk, self.local = sems
        self.ny = dst.shape[0] // 2
        self.chunks = dst.shape[1]
        self.z, self.y, self.c, self.x = split_shard()
        self.core = (self.z, 2 * self.y + 1 - self.c, self.x)

    def py(self, i):
        return (self.y + i) % self.ny

    def dy(self, i):
        return (self.z, 2 * self.py(i) + self.c, self.x)

    def peers(self):
        return [self.core] + [self.dy(i) for i in range(1, self.ny)]

    def own(self):
        return pltpu.make_async_copy(self.src, self.dst.at[2 * self.y + self.c], self.local.at[0])

    def over_y(self, j, i):
        slot = self.dst.at[2 * self.y + self.c, j]
        return remote(self.src.at[j], slot, self.sy.at[j, self.py(i)], self.ry.at[j, self.y], self.dy(i))

    def to_core(self, j):
        slot = self.dst.at[2 * self.y + self.c, j]
        return remote(self.src.at[j], slot, self.sk.at[j, self.y], self.rk.at[j, self.y], self.core)

    def pass_on(self, j, i):
        ref = self.dst.at[2 * self.py(i) + self.c, j]
        return remote(ref, ref, self.sk.at[j, self.py(i)], self.rk.at[j, self.py(i)], self.core)

    def start(self):
        for j in range(self.chunks):
            for i in range(1, self.ny):
                self.over_y(j, i).start()
            self.to_core(j).start()
        self.own().start()

    def relay(self, j):
        for i in range(1, self.ny):
            ref = self.dst.at[2 * self.py(i) + self.c, j]
            remote(ref, ref, self.sy.at[j, self.py(i)], self.ry.at[j, self.py(i)], self.dy(i)).wait_recv()
            self.pass_on(j, i).start()

    def finish(self):
        self.own().wait()
        for j in range(self.chunks):
            for i in range(self.ny):
                ref = self.dst.at[2 * self.py(i) + 1 - self.c, j]
                remote(ref, ref, self.sk.at[j, self.py(i)], self.rk.at[j, self.py(i)], self.core).wait_recv()
                if i:
                    self.over_y(j, i).wait_send()
                    self.pass_on(j, i).wait_send()
                else:
                    self.to_core(j).wait_send()

    @staticmethod
    def sems(shards, chunks):
        return [pltpu.SemaphoreType.DMA((chunks, shards // 2))] * 4 + [pltpu.SemaphoreType.DMA((1,))]


def gather_kernel(
    tok_ref, small_ref, qkv_ref, out_ref, up_ref,
    normed_ref, proj_ref, small_all, qkv_all, out_all, up_all,
    toks, sl, sr, rl, rr, *sems,
):
    blocks, rows, width = toks.shape
    shards, _, depth = qkv_all.shape[:3]
    small, qkv, out, up = (
        Gather(src, dst, sems[5 * i : 5 * i + 5])
        for i, (src, dst) in enumerate(
            ((small_ref, small_all), (qkv_ref, qkv_all), (out_ref, out_all), (up_ref, up_all))
        )
    )
    z, y, c, x = split_shard()
    shard = 2 * y + c
    left, right = (z - 1, shard, x), (z + 1, shard, x)
    has_left, has_right = z > 0, z < blocks - 1
    greet(small.peers() + [((z + i) % blocks, shard, x) for i in range(1, blocks)])

    def go_left(b, src):
        return remote(src, toks.at[b], sl.at[b], rr.at[b], left)

    def go_right(b, src):
        return remote(src, toks.at[b], sr.at[b], rl.at[b], right)

    small.start()
    qkv.start()

    @pl.when(has_left)
    def _():
        go_left(z, tok_ref).start()

    @pl.when(has_right)
    def _():
        go_right(z, tok_ref).start()

    out.start()
    up.start()
    small.relay(0)
    qkv.relay(0)
    small.finish()
    qkv.finish()
    gain = jnp.concatenate([small_all[s, 0, 0:1, :depth] for s in range(shards)], axis=1).astype(F32)
    weight = qkv_all[...].reshape(shards * depth, qkv_all.shape[3])

    def project(b, values):
        at = pl.ds(pl.multiple_of(b * rows, rows), rows)
        values = values.astype(F32)
        scale = lax.rsqrt(jnp.mean(values * values, axis=-1, keepdims=True) + 1e-06)
        normed = (values * scale * gain).astype(BF)
        normed_ref[at] = normed
        proj_ref[at] = jnp.dot(normed, weight, preferred_element_type=F32).astype(BF)

    project(z, tok_ref[...])
    for d in range(1, blocks):
        before, after = z - d, z + d

        @pl.when(before >= 0)
        def _():
            go_right(before, toks.at[before]).wait_recv()

            @pl.when(has_right)
            def _():
                go_right(before, toks.at[before]).start()

        @pl.when(after < blocks)
        def _():
            go_left(after, toks.at[after]).wait_recv()

            @pl.when(has_left)
            def _():
                go_left(after, toks.at[after]).start()

        @pl.when(before >= 0)
        def _():
            project(before, toks[before])

        @pl.when(after < blocks)
        def _():
            project(after, toks[after])

        if d == 1:
            out.relay(0)
        last = up.chunks * d // (blocks - 1)
        for j in range(up.chunks * (d - 1) // (blocks - 1), last):
            up.relay(j)

    out.finish()
    up.finish()

    def sent(b, _):
        @pl.when((b <= z) & has_right)
        def _():
            go_right(b, toks.at[b]).wait_send()

        @pl.when((b >= z) & has_left)
        def _():
            go_left(b, toks.at[b]).wait_send()

        return 0

    lax.fori_loop(0, blocks, sent, 0)


def gather_all(tokens, small, qkv, out, up, blocks, shards):
    rows, width = tokens.shape
    vm = pl.BlockSpec(memory_space=pltpu.VMEM)
    hbm = pl.BlockSpec(memory_space=pl.ANY)
    cut = 4
    arrays = [
        small[None],
        qkv[None],
        out[None],
        up.reshape(cut, up.shape[0] // cut, up.shape[1]),
    ]
    dma = pltpu.SemaphoreType.DMA
    sems = [dma((blocks,))] * 4
    for array in arrays:
        sems += Gather.sems(shards, array.shape[0])
    return pl.pallas_call(
        gather_kernel,
        out_shape=[
            jax.ShapeDtypeStruct((blocks * rows, width), BF),
            jax.ShapeDtypeStruct((blocks * rows, qkv.shape[1]), BF),
        ]
        + [jax.ShapeDtypeStruct((shards,) + array.shape, BF) for array in arrays],
        in_specs=[vm] * 5,
        out_specs=[vm] * 4 + [hbm] * 2,
        scratch_shapes=[pltpu.VMEM((blocks, rows, width), BF)] + sems,
        compiler_params=pltpu.CompilerParams(
            vmem_limit_bytes=60 * 1024 * 1024, collective_id=4, has_side_effects=True
        ),
        name="gather_all",
    )(tokens, *arrays)


def fwd_kernel(prefix_ref, proj_ref, conv_ref, down_ref, own_ref, lse_ref, rows_ref, down_all, wide, qs, ks, vs, m_s, l_s, acc_s, o_s, r_s, send, recv, *sems):
    heads = qs.shape[0]
    length = proj_ref.shape[0]
    blocks = own_ref.shape[1]
    rows = length // blocks
    prefix = prefix_ref[0]
    z, s_at, x = lax.axis_index("seq"), lax.axis_index("shard"), lax.axis_index("replica")

    def block_copy(h, i, at):
        return remote(o_s.at[h, i], r_s.at[at * heads + h], send.at[h, i], recv.at[h, at], (i, s_at, x))

    down = Gather(down_ref, down_all, sems)
    greet([((z + i) % blocks, s_at, x) for i in range(1, blocks)] + down.peers())
    down.start()
    convolve(proj_ref, conv_ref, wide, heads, (qs, ks, vs))
    def head(h, _):
        for j in range(down.chunks):
            @pl.when(h == 1 + (j + 1) // 2)
            def _():
                down.relay(j)
        def qblock(i, _):
            q = qs[h, pl.ds(pl.multiple_of(i*rows, rows), rows)]
            m_s[...] = jnp.full((1, rows), NEG, F32)
            l_s[...] = jnp.zeros((1, rows), F32)
            acc_s[...] = jnp.zeros((HEAD_DIM, rows), F32)
            def step(j, masked):
                at = pl.ds(pl.multiple_of(j*rows, rows), rows)
                s = nt(ks[h, at], q)
                if masked:
                    s = jnp.where(mask_t(i, j, rows, prefix), s, NEG)
                m_old = m_s[...]
                m_new = jnp.maximum(m_old, jnp.max(s, axis=0, keepdims=True))
                p = jnp.exp(s - m_new)
                a = jnp.exp(m_old - m_new)
                m_s[...] = m_new
                l_s[...] = a*l_s[...] + jnp.sum(p, axis=0, keepdims=True)
                acc_s[...] = a*acc_s[...] + tn(vs[h, at], p.astype(BF))
                return 0
            lax.fori_loop(0, i, lambda j, _: step(j, False), 0)
            lax.fori_loop(i, jnp.maximum(i+1, blocks//2), lambda j, _: step(j, True), 0)
            l = l_s[...]
            done = (acc_s[...]/l).astype(BF)
            o_s[h, i] = done
            own_ref[h, i] = done
            @pl.when(i != z)
            def _():
                block_copy(h, i, z).start()
            lse = m_s[...] + jnp.log(l)
            lse_ref[h, :, pl.ds(pl.multiple_of(i*rows, rows), rows)] = jnp.broadcast_to(lse, (8, rows))
            return 0
        lax.fori_loop(0, blocks, qblock, 0)
        r_s[z * heads + h] = o_s[h, z]
        return 0
    lax.fori_loop(0, heads, head, 0)
    for j in range(down.chunks):
        if 1 + (j + 1) // 2 >= heads:
            down.relay(j)
    down.finish()
    def finish(h, _):
        for i in range(1, blocks):
            there = (z + i) % blocks
            block_copy(h, there, there).wait_recv()
            block_copy(h, there, z).wait_send()
        return 0
    lax.fori_loop(0, heads, finish, 0)
    rows_ref[...] = r_s[...]

def attention_fwd(prefix, proj, conv, down, blocks, shards):
    length, width = proj.shape
    heads = width//(3*HEAD_DIM)
    rows = length // blocks
    vm = pl.BlockSpec(memory_space=pltpu.VMEM)
    own = (heads, blocks, HEAD_DIM, rows)
    every = (heads * blocks, HEAD_DIM, rows)
    return pl.pallas_call(
        fwd_kernel,
        out_shape=(jax.ShapeDtypeStruct(own, BF), jax.ShapeDtypeStruct((heads, 8, length), F32), jax.ShapeDtypeStruct(every, BF),
            jax.ShapeDtypeStruct((shards,) + down.shape, BF)),
        in_specs=[pl.BlockSpec(memory_space=pltpu.SMEM), vm, vm, vm],
        out_specs=(vm, vm, vm, pl.BlockSpec(memory_space=pl.ANY)),
        scratch_shapes=[pltpu.VMEM((8+length, width), F32)] + [pltpu.VMEM((heads, length, HEAD_DIM), BF)]*3 + [
            pltpu.VMEM((1,rows),F32), pltpu.VMEM((1,rows),F32), pltpu.VMEM((HEAD_DIM,rows),F32), pltpu.VMEM(own,BF), pltpu.VMEM(every,BF),
            pltpu.SemaphoreType.DMA((heads, blocks)), pltpu.SemaphoreType.DMA((heads, blocks))] + Gather.sems(shards, down.shape[0]),
        compiler_params=pltpu.CompilerParams(vmem_limit_bytes=60*1024*1024, collective_id=2, has_side_effects=True),
        cost_estimate=pl.CostEstimate(flops=4*heads*length*length*HEAD_DIM, bytes_accessed=length*width*2, transcendentals=heads*length*length),
        name="attention_fwd",
    )(prefix, proj, conv, down)

class Sums:
    def __init__(self, parts, out_ref, bufs, sems, nz):
        self.parts, self.out = parts, out_ref
        self.a, self.b, self.c, self.d = bufs
        self.sa, self.ra, self.sb, self.rb, self.sc, self.rc, self.sd, self.rd, self.se, self.re, self.sf, self.rf = sems
        self.chunks, self.ny = self.a.shape[:2]
        self.nx = self.c.shape[1]
        self.nz = nz
        self.half = self.c.shape[2]
        self.piece = self.half // nz
        self.me = split_shard()
        z, y, c, x = self.me
        self.core = (z, 2 * y + 1 - c, x)

    def py(self, i):
        return (self.me[1] + i) % self.ny

    def px(self, i):
        return (self.me[3] + i) % self.nx

    def pz(self, i):
        return (self.me[0] + i) % self.nz

    def dy(self, i):
        z, y, c, x = self.me
        return (z, 2 * self.py(i) + c, x)

    def dx(self, i):
        z, y, c, x = self.me
        return (z, 2 * y + c, self.px(i))

    def dz(self, i):
        z, y, c, x = self.me
        return (self.pz(i), 2 * y + c, x)

    def peers(self):
        out = [self.core] + [self.dy(i) for i in range(1, self.ny)]
        out += [self.dx(i) for i in range(1, self.nx)]
        return out + [self.dz(i) for i in range(1, self.nz)]

    def copy_a(self, k, src):
        return remote(src, self.a.at[k], self.sa.at[k], self.ra.at[k], self.core)

    def start(self):
        c = self.me[2]
        for ref, first, count in self.parts:
            for j in range(count):
                src = ref.at[:, 1 - c, j]
                self.copy_a(first + j, src).start()

    def copy_b(self, k, i, there):
        slot = self.me[1] if there else self.py(i)
        return remote(self.a.at[k, self.py(i)], self.b.at[k, slot], self.sb.at[k, self.py(i)], self.rb.at[k, slot], self.dy(i))

    def stage_b(self, k):
        c = self.me[2]
        self.copy_a(k, self.a.at[k]).wait_recv()
        for i in list(range(1, self.ny)) + [0]:
            p = self.py(i)
            for ref, first, count in self.parts:
                @pl.when((k >= first) & (k < first + count))
                def _():
                    j = jnp.clip(k - first, 0, count - 1)
                    self.a[k, p] = (self.a[k, p].astype(F32) + ref[p, c, j].astype(F32)).astype(BF)
            if i:
                self.copy_b(k, i, True).start()

    def copy_c(self, k, i, there):
        slot = self.me[3] if there else self.px(i)
        src = self.a.at[k, self.me[1], pl.ds(self.px(i) * self.half, self.half)]
        return remote(src, self.c.at[k, slot], self.sc.at[k, self.px(i)], self.rc.at[k, slot], self.dx(i))

    def stage_c(self, k):
        y = self.me[1]
        total = self.a[k, y].astype(F32)
        for i in range(1, self.ny):
            self.copy_b(k, i, False).wait_recv()
            total = total + self.b[k, self.py(i)].astype(F32)
        for i in range(1, self.ny):
            self.copy_b(k, i, True).wait_send()
        self.a[k, y] = total.astype(BF)
        for i in range(1, self.nx):
            self.copy_c(k, i, True).start()

    def copy_d(self, k, i, there):
        z, y, c, x = self.me
        slot = z if there else self.pz(i)
        src = self.a.at[k, y, pl.ds(x * self.half + self.pz(i) * self.piece, self.piece)]
        return remote(src, self.d.at[k, slot], self.sd.at[k, self.pz(i)], self.rd.at[k, slot], self.dz(i))

    def stage_d(self, k):
        z, y, c, x = self.me
        mine = pl.ds(x * self.half, self.half)
        total = self.a[k, y, mine].astype(F32)
        for i in range(1, self.nx):
            self.copy_c(k, i, False).wait_recv()
            total = total + self.c[k, self.px(i)].astype(F32)
        for i in range(1, self.nx):
            self.copy_c(k, i, True).wait_send()
        self.a[k, y, mine] = total.astype(BF)
        for i in range(1, self.nz):
            self.copy_d(k, i, True).start()

    def copy_e(self, k, i, there):
        slot = self.me[0] if there else self.pz(i)
        ref = self.out.at[k, pl.ds(self.me[3] * self.half + slot * self.piece, self.piece)]
        return remote(ref, ref, self.se.at[k, self.pz(i)], self.re.at[k, slot], self.dz(i))

    def stage_e(self, k):
        z, y, c, x = self.me
        mine = pl.ds(x * self.half + z * self.piece, self.piece)
        total = self.a[k, y, mine].astype(F32)
        for i in range(1, self.nz):
            self.copy_d(k, i, False).wait_recv()
            total = total + self.d[k, self.pz(i)].astype(F32)
        self.out[k, mine] = total.astype(BF)
        for i in range(1, self.nz):
            self.copy_e(k, i, True).start()

    def copy_f(self, k, i, there):
        slot = self.me[3] if there else self.px(i)
        ref = self.out.at[k, pl.ds(slot * self.half, self.half)]
        return remote(ref, ref, self.sf.at[k, self.px(i)], self.rf.at[k, slot], self.dx(i))

    def stage_f(self, k):
        for i in range(1, self.nz):
            self.copy_e(k, i, False).wait_recv()
        for i in range(1, self.nx):
            self.copy_f(k, i, True).start()

    def step(self, t):
        for lag, stage in enumerate((self.stage_c, self.stage_d, self.stage_e, self.stage_f)):
            @pl.when((t >= lag) & (t < self.chunks + lag))
            def _():
                stage(t - lag)

    def finish(self):
        def body(k, _):
            for i in range(1, self.nx):
                self.copy_f(k, i, False).wait_recv()
            self.copy_a(k, self.a.at[k]).wait_send()
            for i in range(1, self.nx):
                self.copy_f(k, i, True).wait_send()
            for i in range(1, self.nz):
                self.copy_d(k, i, True).wait_send()
                self.copy_e(k, i, True).wait_send()
            return 0

        lax.fori_loop(0, self.chunks, body, 0)

    @staticmethod
    def sems(chunks, ny, nx, nz):
        out = [pltpu.SemaphoreType.DMA((chunks,))] * 2
        for n in (ny, nx, nz, nz, nx):
            out += [pltpu.SemaphoreType.DMA((chunks, n))] * 2
        return out


def bwd_kernel(counts, *refs):
    parts_n = len(counts)
    prefix_ref, proj_ref, conv_ref, do_ref, o_ref, lse_ref = refs[:6]
    part_refs = refs[6:6 + parts_n]
    gp_ref, gconv_ref, sum_ref = refs[6 + parts_n:9 + parts_n]
    wide, qs, ks, vs, dos, delta, dq, dk, dv, gq, gk, gv, gwide, send, recv = refs[9 + parts_n:24 + parts_n]
    bufs = refs[24 + parts_n:28 + parts_n]
    sems = refs[28 + parts_n:]
    heads = qs.shape[0]
    length, width = proj_ref.shape
    blocks = dos.shape[1]
    rows = length//blocks
    prefix = prefix_ref[0]
    parts = []
    first = 0
    for ref, count in zip(part_refs, counts):
        parts.append((ref, first, count))
        first += count
    sums = Sums(parts, sum_ref, bufs, sems, blocks)
    z, y, c, x = sums.me
    greet(sums.peers())
    sums.start()

    def block_copy(h, i, at):
        return remote(do_ref.at[i * heads + h], dos.at[h, at], send.at[h, i], recv.at[h, at], (i, 2 * y + c, x))

    for h in range(heads):
        for i in range(1, blocks):
            block_copy(h, (z + i) % blocks, z).start()
        dos[h, z] = do_ref[z * heads + h]
    convolve(proj_ref, conv_ref, wide, heads, (qs, ks, vs))

    def head(h, _):
        for i in range(1, blocks):
            there = (z + i) % blocks
            block_copy(h, there, there).wait_recv()
        for i in range(blocks):
            prod = dos[h, i].astype(F32) * o_ref[h, i].astype(F32)
            delta[i] = jnp.broadcast_to(jnp.sum(prod, axis=0, keepdims=True), (8, rows))
        dq[...] = jnp.zeros(dq.shape, F32)
        def kblock(j, _):
            t = h*blocks + j
            @pl.when(t < sums.chunks)
            def _():
                sums.stage_b(t)
            turn = (2*t)//3
            @pl.when((turn > 0) & ((2*t)%3 != 2))
            def _():
                sums.step(turn - 1)
            kat = pl.ds(pl.multiple_of(j*rows, rows), rows)
            k = ks[h, kat]; v = vs[h, kat]
            dk[...] = jnp.zeros(dk.shape, F32)
            dv[...] = jnp.zeros(dv.shape, F32)
            def step(i, masked):
                qat = pl.ds(pl.multiple_of(i*rows, rows), rows)
                q = qs[h, qat]; do = dos[h, i]
                s = nt(k, q)
                p = jnp.exp(s - lse_ref[h, 0:1, qat])
                if masked:
                    p = jnp.where(mask_t(i, j, rows, prefix), p, 0.0)
                dv[...] += nt(p.astype(BF), do)
                dp = jnp.dot(v, do, preferred_element_type=F32)
                ds = (p*(dp - delta[i, 0:1])).astype(BF)
                dk[...] += jnp.dot(ds, q, preferred_element_type=F32)
                dq[qat] += tn(ds, k)
                return 0
            lax.fori_loop(j+1, blocks, lambda i, _: step(i, False), 0)
            lax.fori_loop(jnp.where(j < blocks//2, 0, j), j+1, lambda i, _: step(i, True), 0)
            gk[h, kat] = dk[...].astype(BF)
            gv[h, kat] = dv[...].astype(BF)
            return 0
        lax.fori_loop(0, blocks, kblock, 0)
        def qout(c, _):
            at = pl.ds(pl.multiple_of(c*rows, rows), rows)
            gq[h, at] = (dq[at]*(HEAD_DIM**-0.5)).astype(BF)
            return 0
        lax.fori_loop(0, blocks, qout, 0)
        return 0
    lax.fori_loop(0, heads, head, 0)
    steps = heads*blocks
    turns = (2*(steps - 1))//3
    def rest(t, _):
        sums.stage_b(t)
        return 0
    lax.fori_loop(steps, sums.chunks, rest, 0)
    taps = conv_ref[...].astype(F32)
    gwide[length:length+8] = jnp.zeros((8, width), F32)
    def fill(c, _):
        at = pl.ds(pl.multiple_of(c*rows, rows), rows)
        gwide[at] = jnp.concatenate([r[h, at] for r in (gq, gk, gv) for h in range(heads)], axis=1).astype(F32)
        return 0
    lax.fori_loop(0, blocks, fill, 0)
    def out(c, total):
        sums.step(turns + c)
        base = pl.multiple_of(c*rows, rows)
        g = gwide[pl.ds(base, rows+8)]
        x = wide[pl.ds(base, rows+8)]
        g0 = g[:rows]
        gp = taps[0:1]*g0 + taps[1:2]*g[1:rows+1] + taps[2:3]*g[2:rows+2]
        gp_ref[pl.ds(base, rows)] = gp.astype(BF)
        add = [jnp.sum(g0*x[8-t:8-t+rows], axis=0, keepdims=True) for t in range(3)]
        return tuple(a+b for a, b in zip(total, add))
    total = lax.fori_loop(0, blocks, out, tuple(jnp.zeros((1, width), F32) for _ in range(3)))
    gconv_ref[...] = jnp.concatenate(total, axis=0)
    def tail(t, _):
        sums.step(t)
        return 0
    lax.fori_loop(turns + blocks, max(sums.chunks + 3, turns + blocks), tail, 0)
    sums.finish()
    def sent(h, _):
        for i in range(1, blocks):
            block_copy(h, (z + i) % blocks, z).wait_send()
        return 0
    lax.fori_loop(0, heads, sent, 0)

def attention_bwd(prefix, proj, conv, do, o, lse, parts, nx):
    length, width = proj.shape
    heads, blocks = o.shape[:2]
    rows = length // blocks
    counts = tuple(part.shape[2] for part in parts)
    ny, _, _, units = parts[0].shape[:4]
    unit = parts[0].shape[4:]
    chunks = sum(counts)
    half = units // nx
    vm = pl.BlockSpec(memory_space=pltpu.VMEM)
    per = lambda dt: pltpu.VMEM((heads, length, HEAD_DIM), dt)
    return pl.pallas_call(
        functools.partial(bwd_kernel, counts),
        out_shape=(jax.ShapeDtypeStruct((length, width), BF), jax.ShapeDtypeStruct((3, width), F32), jax.ShapeDtypeStruct((chunks, units) + unit, BF)),
        in_specs=[pl.BlockSpec(memory_space=pltpu.SMEM)] + [vm]*(5 + len(parts)),
        out_specs=(vm, vm, vm),
        scratch_shapes=[pltpu.VMEM((8+length, width), F32), per(BF), per(BF), per(BF), pltpu.VMEM(o.shape, BF), pltpu.VMEM((blocks, 8, rows), F32),
            pltpu.VMEM((length, HEAD_DIM), F32), pltpu.VMEM((rows, HEAD_DIM), F32), pltpu.VMEM((rows, HEAD_DIM), F32),
            per(BF), per(BF), per(BF), pltpu.VMEM((length+8, width), F32),
            pltpu.SemaphoreType.DMA((heads, blocks)), pltpu.SemaphoreType.DMA((heads, blocks)),
            pltpu.VMEM((chunks, ny, units) + unit, BF), pltpu.VMEM((chunks, ny, units) + unit, BF),
            pltpu.VMEM((chunks, nx, half) + unit, BF), pltpu.VMEM((chunks, blocks, half // blocks) + unit, BF)]
            + Sums.sems(chunks, ny, nx, blocks),
        compiler_params=pltpu.CompilerParams(vmem_limit_bytes=67043328, collective_id=3, has_side_effects=True),
        cost_estimate=pl.CostEstimate(flops=10*heads*length*length*HEAD_DIM, bytes_accessed=length*width*4, transcendentals=heads*length*length),
        name="attention_bwd",
    )(prefix, proj, conv, do, o, lse, *parts)


def qkv_kernel(part_ref, out_ref, qa, qb, qc, sa, ra, sb, rb, sc, rc, se, re, sf, rf, *, nx, nz):
    ny = part_ref.shape[0]
    half = part_ref.shape[2] // nx
    z, y, c, x = split_shard()
    core = (z, 2 * y + 1 - c, x)

    def py(i):
        return (y + i) % ny

    def px(i):
        return (x + i) % nx

    def pz(i):
        return (z + i) % nz

    def dy(i):
        return (z, 2 * py(i) + c, x)

    def dx(i):
        return (z, 2 * y + c, px(i))

    def dz(i):
        return (pz(i), 2 * y + c, x)

    def to_y(i, there):
        slot = y if there else py(i)
        return remote(qa.at[py(i)], qb.at[slot], sb.at[py(i)], rb.at[slot], dy(i))

    def to_x(i, there):
        slot = x if there else px(i)
        return remote(qa.at[y, pl.ds(px(i) * half, half)], qc.at[slot], sc.at[px(i)], rc.at[slot], dx(i))

    def on_z(i, there):
        slot = z if there else pz(i)
        ref = out_ref.at[slot, pl.ds(x * half, half)]
        return remote(ref, ref, se.at[pz(i)], re.at[slot], dz(i))

    def on_x(i, j, there):
        slot = x if there else px(j)
        ref = out_ref.at[pz(i), pl.ds(slot * half, half)]
        return remote(ref, ref, sf.at[pz(i), px(j)], rf.at[pz(i), slot], dx(j))

    greet([core] + [dy(i) for i in range(1, ny)] + [dx(i) for i in range(1, nx)] + [dz(i) for i in range(1, nz)])
    first = remote(part_ref.at[:, 1 - c], qa, sa.at[0], ra.at[0], core)
    first.start()
    first.wait_recv()
    for i in list(range(1, ny)) + [0]:
        qa[py(i)] = (qa[py(i)].astype(F32) + part_ref[py(i), c].astype(F32)).astype(BF)
        if i:
            to_y(i, True).start()
    total = qa[y].astype(F32)
    for i in range(1, ny):
        to_y(i, False).wait_recv()
        total = total + qb[py(i)].astype(F32)
    qa[y] = total.astype(BF)
    for i in range(1, nx):
        to_x(i, True).start()
    mine = pl.ds(x * half, half)
    total = qa[y, mine].astype(F32)
    for i in range(1, nx):
        to_x(i, False).wait_recv()
        total = total + qc[px(i)].astype(F32)
    out_ref[z, mine] = total.astype(BF)
    for i in range(1, nz):
        on_z(i, True).start()
    for i in range(nz):
        if i:
            on_z(i, False).wait_recv()
        for j in range(1, nx):
            on_x(i, j, True).start()
    for i in range(nz):
        for j in range(1, nx):
            on_x(i, j, False).wait_recv()
            on_x(i, j, True).wait_send()
    first.wait_send()
    for i in range(1, ny):
        to_y(i, True).wait_send()
    for i in range(1, nx):
        to_x(i, True).wait_send()
    for i in range(1, nz):
        on_z(i, True).wait_send()


def reduce_qkv(part, nx, nz):
    ny, _, units = part.shape[:3]
    unit = part.shape[3:]
    vm = pl.BlockSpec(memory_space=pltpu.VMEM)
    dma = pltpu.SemaphoreType.DMA
    return pl.pallas_call(
        functools.partial(qkv_kernel, nx=nx, nz=nz),
        out_shape=jax.ShapeDtypeStruct((nz, units) + unit, BF),
        in_specs=[vm],
        out_specs=vm,
        scratch_shapes=[
            pltpu.VMEM((ny, units) + unit, BF),
            pltpu.VMEM((ny, units) + unit, BF),
            pltpu.VMEM((nx, units // nx) + unit, BF),
        ]
        + [dma((1,))] * 2
        + [dma((ny,))] * 2
        + [dma((nx,))] * 2
        + [dma((nz,))] * 2
        + [dma((nz, nx))] * 2,
        compiler_params=pltpu.CompilerParams(
            collective_id=1, has_side_effects=True, vmem_limit_bytes=60 * 1024 * 1024
        ),
        name="reduce_qkv",
    )(part)


def rms_scale(values):
    return lax.rsqrt(jnp.mean(values * values, axis=-1, keepdims=True) + 1e-06)


def norm_back(values, scale_rows, gain, upstream):
    weighted = upstream * gain
    grad_values = scale_rows * weighted - values * scale_rows**3 * jnp.mean(
        weighted * values, axis=-1, keepdims=True
    )
    return grad_values


def dot(a, b):
    return jnp.dot(a, b, preferred_element_type=F32)


def per_device(
    tokens, prefix_len, w_qkv, w_out, w_up, w_down, conv_w, gain_attn, gain_ffn, cotangent
):
    blocks = lax.axis_size("seq")
    me = lax.axis_index("seq")
    rows, width = tokens.shape[1:]
    own = HEADS // blocks * HEAD_DIM
    depth = w_qkv.shape[0]

    shards, copies = lax.axis_size("shard"), lax.axis_size("replica")
    columns = lax.dynamic_index_in_dim(w_qkv.reshape(depth, 3, blocks, own), me, 2, False)
    gains = jnp.pad(jnp.stack([gain_attn, gain_ffn]), ((0, 0), (0, conv_w.shape[1] - depth)))
    small = jnp.pad(jnp.concatenate([gains, conv_w]), ((0, 3), (0, 0)))
    normed_all, projected, small, own_qkv, full_out, full_up = gather_all(
        tokens[0], small, columns.reshape(depth, 3 * own), w_out, w_up, blocks, shards
    )
    own_qkv = own_qkv.reshape(width, 3 * own)
    full_out = full_out.reshape(width, width)
    full_up = full_up.reshape(width, -1)
    full_gone = small[:, 0, 0, :depth].reshape(width).astype(F32)
    full_gtwo = small[:, 0, 1, :depth].reshape(width).astype(F32)
    full_conv = small[:, 0, 2:5].transpose(1, 0, 2)
    own_conv = lax.dynamic_index_in_dim(full_conv.reshape(3, 3, blocks, own), me, 2, False)
    own_conv = own_conv.reshape(3, 3 * own)
    attended_own, logsum, attended, full_down = attention_fwd(
        prefix_len, projected, own_conv, w_down.reshape(-1, depth, width), blocks, shards
    )
    full_down = full_down.reshape(-1, width)
    attended = attended.reshape(width, rows)

    inputs = tokens[0].astype(F32)
    scale_one = rms_scale(inputs)
    hidden = inputs + tn(attended, full_out)
    scale_two = rms_scale(hidden)
    normed_two_b = (hidden * scale_two * full_gtwo).astype(BF)
    positive = jnp.maximum(dot(normed_two_b, full_up), 0.0)
    active_b = (positive * positive).astype(BF)
    output = hidden + dot(active_b, full_down)

    incoming = cotangent[0]
    grad_upper_b = (dot(incoming, full_down.T) * 2.0 * positive).astype(BF)
    grad_normed_two = dot(grad_upper_b, full_up.T)
    grad_hidden = incoming.astype(F32) + norm_back(hidden, scale_two, full_gtwo, grad_normed_two)
    grad_hidden_b = grad_hidden.astype(BF)
    grad_attended = nt(full_out, grad_hidden_b).astype(BF)

    mine = depth // 8

    def cut(grad):
        return grad.astype(BF).reshape(shards // 2, 2, -1, mine, 8, width)

    parts = [
        cut(dot(normed_two_b.T, grad_upper_b[:, i * width : (i + 1) * width]))
        for i in range(grad_upper_b.shape[1] // width)
    ]
    parts += [cut(dot(active_b.T, incoming)), cut(dot(attended, grad_hidden_b))]
    pieces = sum(part.shape[2] for part in parts)
    if mine % (copies * blocks):
        units = -(-pieces * mine // (copies * blocks)) * copies * blocks
        joined = [part.reshape(shards // 2, 2, -1, 8, width) for part in parts]
        joined.append(jnp.zeros((shards // 2, 2, units - pieces * mine, 8, width), BF))
        joined = jnp.concatenate(joined, axis=2)
        parts = [joined.reshape(shards // 2, 2, -1, copies * blocks, 8, width)]

    grad_projected, grad_conv, sums = attention_bwd(
        prefix_len, projected, own_conv, grad_attended.reshape(HEADS, HEAD_DIM, rows),
        attended_own, logsum, parts, copies,
    )
    grad_normed = lax.psum_scatter(
        dot(grad_projected, own_qkv.T).astype(BF), "seq", scatter_dimension=0, tiled=True
    ).astype(F32)
    grad_qkv = dot(normed_all.T, grad_projected)
    grad_input = (grad_hidden + norm_back(inputs, scale_one, full_gone, grad_normed)).astype(BF)

    taps = grad_conv.shape[0]
    extra = jnp.pad(grad_conv.astype(BF), ((0, 8 - taps), (0, 0)))
    uq = -(-(mine + 1) // copies) * copies
    qkv = jnp.concatenate(
        [
            grad_qkv.astype(BF).reshape(shards, mine, 8, 3 * own),
            jnp.broadcast_to(extra, (shards, 1, 8, 3 * own)),
            jnp.zeros((shards, uq - mine - 1, 8, 3 * own), BF),
        ],
        axis=1,
    ).reshape(shards // 2, 2, uq, 8, 3 * own)
    own_sums = reduce_qkv(qkv, copies, blocks)
    sums = sums.reshape(-1, 8, width)[: pieces * mine].reshape(pieces, depth, width)
    ups = w_up.shape[1] // width
    total_up = jnp.concatenate(list(sums[:ups]), axis=1).astype(F32)
    total_down = sums[ups:-1].reshape(-1, width).astype(F32)
    total_out = sums[-1].astype(F32)

    def merge(array):
        return jnp.concatenate(
            [array[j, :, p * own : (p + 1) * own] for p in range(3) for j in range(blocks)], axis=1
        ).astype(F32)

    total_qkv = merge(own_sums[:, :mine].reshape(blocks, depth, 3 * own))
    total_conv = merge(own_sums[:, mine, :taps])
    at = lax.axis_index("shard")

    def gain_grad(grad, weight, gain):
        return jnp.sum(grad * weight.astype(F32), axis=1) / gain.astype(F32)

    return (
        output[None].astype(BF),
        grad_input[None],
        total_qkv,
        total_out,
        total_up,
        total_down,
        lax.dynamic_slice_in_dim(total_conv, at * conv_w.shape[1], conv_w.shape[1], 1),
        gain_grad(total_qkv, w_qkv, gain_attn),
        gain_grad(total_up, w_up, gain_ffn),
    )


def solution(mesh):
    placed = (
        P(("shard", "replica"), "seq", None),
        P(("shard", "replica")),
        P("shard", None),
        P("shard", None),
        P("shard", None),
        P("shard", None),
        P(None, "shard"),
        P("shard"),
        P("shard"),
        P(("shard", "replica"), "seq", None),
    )
    return jax.shard_map(
        per_device,
        mesh=mesh,
        in_specs=placed,
        out_specs=(
            P(("shard", "replica"), "seq", None),
            P(("shard", "replica"), "seq", None),
            P("shard", None),
            P("shard", None),
            P("shard", None),
            P("shard", None),
            P(None, "shard"),
            P("shard"),
            P("shard"),
        ),
        check_vma=False,
    )
```

```python
import functools

import jax
import jax.numpy as jnp
from jax import lax
from jax.experimental import pallas as pl
from jax.experimental.pallas import tpu as pltpu
from jax.sharding import PartitionSpec as P

HEADS = 12
HEAD_DIM=64
NEG=-1e30
F32=jnp.float32
BF=jnp.bfloat16

def nt(a,b):
    return lax.dot_general(a,b,(((1,),(1,)),((),())),preferred_element_type=F32)
def tn(a,b):
    return lax.dot_general(a,b,(((0,),(0,)),((),())),preferred_element_type=F32)

def convolve(proj_ref, conv_ref, wide, parts):
    length = proj_ref.shape[0]
    heads, _, width = wide.shape
    rows = min(512, length)
    for h in range(heads):
        wide[h, 0:8] = jnp.zeros((8, width), F32)
        for c in range(length//rows):
            wide[h, 8+c*rows:8+(c+1)*rows] = proj_ref[c*rows:(c+1)*rows, h*width:(h+1)*width].astype(F32)
    def body(c, _):
        base = pl.multiple_of(c*rows, rows)
        for h in range(heads):
            x = wide[h, pl.ds(base, rows+8)]
            taps = conv_ref[h]
            mixed = taps[0:1]*x[8:] + taps[1:2]*x[7:7+rows] + taps[2:3]*x[6:6+rows]
            for p, ref in enumerate(parts):
                piece = mixed[:, p*HEAD_DIM:(p+1)*HEAD_DIM].astype(BF)
                if p == 0:
                    piece = piece * jnp.asarray(HEAD_DIM**-0.5, BF)
                ref[h, pl.ds(base, rows)] = piece
        return 0
    lax.fori_loop(0, length//rows, body, 0)

def mask_t(i, j, rows, prefix):
    kpos = j*rows + lax.broadcasted_iota(jnp.int32, (rows, 1), 0)
    qpos = i*rows + lax.broadcasted_iota(jnp.int32, (1, rows), 1)
    return (kpos <= qpos) | ((kpos < prefix) & (qpos < prefix))

def mask_n(i, j, rows, prefix):
    qpos = i*rows + lax.broadcasted_iota(jnp.int32, (rows, 1), 0)
    kpos = j*rows + lax.broadcasted_iota(jnp.int32, (1, rows), 1)
    return (kpos <= qpos) | ((kpos < prefix) & (qpos < prefix))

MESH = pl.DeviceIdType.MESH


def remote(src, dst, send, recv, peer):
    return pltpu.make_async_remote_copy(
        src_ref=src, dst_ref=dst, send_sem=send, recv_sem=recv, device_id=peer, device_id_type=MESH
    )


def greet(peers):
    barrier = pltpu.get_barrier_semaphore()
    for peer in peers:
        pl.semaphore_signal(barrier, inc=1, device_id=peer, device_id_type=MESH)
    pl.semaphore_wait(barrier, len(peers))


def split_shard():
    s = lax.axis_index("shard")
    return lax.axis_index("seq"), s // 2, s % 2, lax.axis_index("replica")


class Gather:
    def __init__(self, src, dst, sems, major=False):
        self.src, self.dst, self.major = src, dst, major
        self.sy, self.ry, self.sk, self.rk, self.local = sems
        self.ny = dst.shape[1 if major else 0] // 2
        self.chunks = dst.shape[0 if major else 1]
        self.z, self.y, self.c, self.x = split_shard()
        self.core = (self.z, 2 * self.y + 1 - self.c, self.x)

    def py(self, i):
        return (self.y + i) % self.ny

    def dy(self, i):
        return (self.z, 2 * self.py(i) + self.c, self.x)

    def peers(self):
        return [self.core] + [self.dy(i) for i in range(1, self.ny)]

    def slot(self, p, core, j):
        shard = 2 * p + core
        return self.dst.at[j, shard] if self.major else self.dst.at[shard, j]

    def own(self):
        shard = 2 * self.y + self.c
        dst = self.dst.at[:, shard] if self.major else self.dst.at[shard]
        return pltpu.make_async_copy(self.src, dst, self.local.at[0])

    def over_y(self, j, i):
        slot = self.slot(self.y, self.c, j)
        return remote(self.src.at[j], slot, self.sy.at[j, self.py(i)], self.ry.at[j, self.y], self.dy(i))

    def to_core(self, j):
        slot = self.slot(self.y, self.c, j)
        return remote(self.src.at[j], slot, self.sk.at[j, self.y], self.rk.at[j, self.y], self.core)

    def pass_on(self, j, i):
        ref = self.slot(self.py(i), self.c, j)
        return remote(ref, ref, self.sk.at[j, self.py(i)], self.rk.at[j, self.py(i)], self.core)

    def send(self, j):
        for i in range(1, self.ny):
            self.over_y(j, i).start()
        self.to_core(j).start()

    def start(self):
        for j in range(self.chunks):
            self.send(j)
        self.own().start()

    def relay(self, j):
        for i in range(1, self.ny):
            ref = self.slot(self.py(i), self.c, j)
            remote(ref, ref, self.sy.at[j, self.py(i)], self.ry.at[j, self.py(i)], self.dy(i)).wait_recv()
            self.pass_on(j, i).start()

    def arrive(self, j):
        for i in range(self.ny):
            ref = self.slot(self.py(i), 1 - self.c, j)
            remote(ref, ref, self.sk.at[j, self.py(i)], self.rk.at[j, self.py(i)], self.core).wait_recv()

    def sent(self, j):
        self.to_core(j).wait_send()
        for i in range(1, self.ny):
            self.over_y(j, i).wait_send()
            self.pass_on(j, i).wait_send()

    def finish(self):
        self.own().wait()
        for j in range(self.chunks):
            self.arrive(j)
            self.sent(j)

    @staticmethod
    def sems(shards, chunks):
        return [pltpu.SemaphoreType.DMA((chunks, shards // 2))] * 4 + [pltpu.SemaphoreType.DMA((1,))]


def gather_kernel(
    tok_ref, small_ref, qkv_ref, out_ref, up_ref,
    normed_ref, proj_ref, small_all, qkv_all, out_all, up_all,
    toks, sl, sr, rl, rr, *sems,
):
    blocks, rows, width = toks.shape
    _, shards, depth, columns = qkv_all.shape
    small, qkv, out, up = (
        Gather(src, dst, sems[5 * i : 5 * i + 5], major=i == 1)
        for i, (src, dst) in enumerate(
            ((small_ref, small_all), (qkv_ref, qkv_all), (out_ref, out_all), (up_ref, up_all))
        )
    )
    z, y, c, x = split_shard()
    shard = 2 * y + c
    left, right = (z - 1, shard, x), (z + 1, shard, x)
    has_left, has_right = z > 0, z < blocks - 1
    greet(small.peers() + [((z + i) % blocks, shard, x) for i in range(1, blocks)])

    def go_left(b, src):
        return remote(src, toks.at[b], sl.at[b], rr.at[b], left)

    def go_right(b, src):
        return remote(src, toks.at[b], sr.at[b], rl.at[b], right)

    small.start()
    qkv.send(z)
    qkv.own().start()

    @pl.when(has_left)
    def _():
        go_left(z, tok_ref).start()

    @pl.when(has_right)
    def _():
        go_right(z, tok_ref).start()

    out.start()
    up.start()
    for i in range(1, blocks):
        qkv.send((z + i) % blocks)
    small.relay(0)
    qkv.relay(z)
    small.finish()
    qkv.own().wait()
    qkv.arrive(z)
    gain = jnp.concatenate([small_all[s, 0, 0:1, :depth] for s in range(shards)], axis=1).astype(F32)
    weight = qkv_all[z].reshape(shards * depth, columns)

    def project(b, values):
        at = pl.ds(pl.multiple_of(b * rows, rows), rows)
        values = values.astype(F32)
        scale = lax.rsqrt(jnp.mean(values * values, axis=-1, keepdims=True) + 1e-06)
        normed = values * scale * gain
        proj_ref[at] = jnp.dot(normed.astype(BF), weight, preferred_element_type=F32).astype(BF)
        normed_ref[:, at] = jnp.transpose(normed).astype(BF)

    project(z, tok_ref[...])
    for d in range(1, blocks):
        before, after = z - d, z + d

        @pl.when(before >= 0)
        def _():
            go_right(before, toks.at[before]).wait_recv()

            @pl.when(has_right)
            def _():
                go_right(before, toks.at[before]).start()

        @pl.when(after < blocks)
        def _():
            go_left(after, toks.at[after]).wait_recv()

            @pl.when(has_left)
            def _():
                go_left(after, toks.at[after]).start()

        @pl.when(before >= 0)
        def _():
            project(before, toks[before])

        @pl.when(after < blocks)
        def _():
            project(after, toks[after])

        if d == 1:
            out.relay(0)
        last = up.chunks * d // (blocks - 1)
        for j in range(up.chunks * (d - 1) // (blocks - 1), last):
            up.relay(j)

    for i in range(1, blocks):
        qkv.relay((z + i) % blocks)
    out.finish()
    up.finish()
    for i in range(1, blocks):
        qkv.arrive((z + i) % blocks)
    for j in range(blocks):
        qkv.sent(j)

    def sent(b, _):
        @pl.when((b <= z) & has_right)
        def _():
            go_right(b, toks.at[b]).wait_send()

        @pl.when((b >= z) & has_left)
        def _():
            go_left(b, toks.at[b]).wait_send()

        return 0

    lax.fori_loop(0, blocks, sent, 0)


def gather_all(tokens, small, qkv, out, up, blocks, shards):
    rows, width = tokens.shape
    vm = pl.BlockSpec(memory_space=pltpu.VMEM)
    hbm = pl.BlockSpec(memory_space=pl.ANY)
    cut = 4
    arrays = [
        small[None],
        qkv,
        out[None],
        up.reshape(cut, up.shape[0] // cut, up.shape[1]),
    ]
    dma = pltpu.SemaphoreType.DMA
    sems = [dma((blocks,))] * 4
    for array in arrays:
        sems += Gather.sems(shards, array.shape[0])
    return pl.pallas_call(
        gather_kernel,
        out_shape=[
            jax.ShapeDtypeStruct((width, blocks * rows), BF),
            jax.ShapeDtypeStruct((blocks * rows, qkv.shape[2]), BF),
        ]
        + [
            jax.ShapeDtypeStruct(
                (blocks, shards) + array.shape[1:] if i == 1 else (shards,) + array.shape, BF
            )
            for i, array in enumerate(arrays)
        ],
        in_specs=[vm] * 5,
        out_specs=[vm] * 4 + [hbm] * 2,
        scratch_shapes=[pltpu.VMEM((blocks, rows, width), BF)] + sems,
        compiler_params=pltpu.CompilerParams(
            vmem_limit_bytes=60 * 1024 * 1024, collective_id=4, has_side_effects=True
        ),
        name="gather_all",
    )(tokens, *arrays)


def fwd_kernel(prefix_ref, proj_ref, conv_ref, down_ref, own_ref, lse_ref, rows_ref, down_all, wide, qs, ks, vs, m_s, l_s, acc_s, o_s, r_s, send, recv, *sems):
    heads = qs.shape[0]
    length = proj_ref.shape[0]
    blocks = own_ref.shape[1]
    rows = length // blocks
    prefix = prefix_ref[0]
    z, s_at, x = lax.axis_index("seq"), lax.axis_index("shard"), lax.axis_index("replica")

    def block_copy(h, i, at):
        return remote(o_s.at[h, i], r_s.at[at * heads + h], send.at[h, i], recv.at[h, at], (i, s_at, x))

    down = Gather(down_ref, down_all, sems)
    greet([((z + i) % blocks, s_at, x) for i in range(1, blocks)] + down.peers())
    down.start()
    convolve(proj_ref, conv_ref, wide, (qs, ks, vs))
    def head(h, _):
        for j in range(down.chunks):
            @pl.when(h == 1 + (j + 1) // 2)
            def _():
                down.relay(j)
        def qblock(i, _):
            q = qs[h, pl.ds(pl.multiple_of(i*rows, rows), rows)]
            m_s[...] = jnp.full((1, rows), NEG, F32)
            l_s[...] = jnp.zeros((1, rows), F32)
            acc_s[...] = jnp.zeros((HEAD_DIM, rows), F32)
            def step(j, masked):
                at = pl.ds(pl.multiple_of(j*rows, rows), rows)
                s = nt(ks[h, at], q)
                if masked:
                    s = jnp.where(mask_t(i, j, rows, prefix), s, NEG)
                m_old = m_s[...]
                m_new = jnp.maximum(m_old, jnp.max(s, axis=0, keepdims=True))
                p = jnp.exp(s - m_new)
                a = jnp.exp(m_old - m_new)
                m_s[...] = m_new
                l_s[...] = a*l_s[...] + jnp.sum(p, axis=0, keepdims=True)
                acc_s[...] = a*acc_s[...] + tn(vs[h, at], p.astype(BF))
                return 0
            lax.fori_loop(0, i, lambda j, _: step(j, False), 0)
            lax.fori_loop(i, jnp.maximum(i+1, blocks//2), lambda j, _: step(j, True), 0)
            l = l_s[...]
            done = (acc_s[...]/l).astype(BF)
            o_s[h, i] = done
            own_ref[h, i] = done
            @pl.when(i != z)
            def _():
                block_copy(h, i, z).start()
            lse = m_s[...] + jnp.log(l)
            lse_ref[h, :, pl.ds(pl.multiple_of(i*rows, rows), rows)] = jnp.broadcast_to(lse, (8, rows))
            return 0
        lax.fori_loop(0, blocks, qblock, 0)
        r_s[z * heads + h] = o_s[h, z]
        return 0
    lax.fori_loop(0, heads, head, 0)
    for j in range(down.chunks):
        if 1 + (j + 1) // 2 >= heads:
            down.relay(j)
    down.finish()
    def finish(h, _):
        for i in range(1, blocks):
            there = (z + i) % blocks
            block_copy(h, there, there).wait_recv()
            block_copy(h, there, z).wait_send()
        return 0
    lax.fori_loop(0, heads, finish, 0)
    rows_ref[...] = r_s[...]

def attention_fwd(prefix, proj, conv, down, blocks, shards):
    length, width = proj.shape
    heads = width//(3*HEAD_DIM)
    rows = length // blocks
    vm = pl.BlockSpec(memory_space=pltpu.VMEM)
    own = (heads, blocks, HEAD_DIM, rows)
    every = (heads * blocks, HEAD_DIM, rows)
    return pl.pallas_call(
        fwd_kernel,
        out_shape=(jax.ShapeDtypeStruct(own, BF), jax.ShapeDtypeStruct((heads, 8, length), F32), jax.ShapeDtypeStruct(every, BF),
            jax.ShapeDtypeStruct((shards,) + down.shape, BF)),
        in_specs=[pl.BlockSpec(memory_space=pltpu.SMEM), vm, vm, vm],
        out_specs=(vm, vm, vm, pl.BlockSpec(memory_space=pl.ANY)),
        scratch_shapes=[pltpu.VMEM((heads, 8+length, 3*HEAD_DIM), F32)] + [pltpu.VMEM((heads, length, HEAD_DIM), BF)]*3 + [
            pltpu.VMEM((1,rows),F32), pltpu.VMEM((1,rows),F32), pltpu.VMEM((HEAD_DIM,rows),F32), pltpu.VMEM(own,BF), pltpu.VMEM(every,BF),
            pltpu.SemaphoreType.DMA((heads, blocks)), pltpu.SemaphoreType.DMA((heads, blocks))] + Gather.sems(shards, down.shape[0]),
        compiler_params=pltpu.CompilerParams(vmem_limit_bytes=60*1024*1024, collective_id=2, has_side_effects=True),
        cost_estimate=pl.CostEstimate(flops=4*heads*length*length*HEAD_DIM, bytes_accessed=length*width*2, transcendentals=heads*length*length),
        name="attention_fwd",
    )(prefix, proj, conv, down)

class Sums:
    def __init__(self, parts, out_ref, bufs, sems, nz):
        self.parts, self.out = parts, out_ref
        self.a, self.b, self.c, self.near, self.far = bufs
        self.sa, self.ra, self.sb, self.rb, self.sc, self.rc, self.sz, self.rz, self.sf, self.rf = sems
        self.chunks, self.ny = self.a.shape[:2]
        self.nx = self.c.shape[1]
        self.nz = nz
        self.half = self.c.shape[2]
        self.piece = self.half // nz
        self.me = split_shard()
        z, y, c, x = self.me
        self.core = (z, 2 * y + 1 - c, x)
        self.low, self.high = z % 2, z // 2
        self.one = (z + 1 - 2 * self.low, 2 * y + c, x)
        self.two = (z + 2 - 4 * self.high, 2 * y + c, x)

    def py(self, i):
        return (self.me[1] + i) % self.ny

    def px(self, i):
        return (self.me[3] + i) % self.nx

    def pz(self, i):
        return (self.me[0] + i) % self.nz

    def dy(self, i):
        z, y, c, x = self.me
        return (z, 2 * self.py(i) + c, x)

    def dx(self, i):
        z, y, c, x = self.me
        return (z, 2 * y + c, self.px(i))

    def dz(self, i):
        z, y, c, x = self.me
        return (self.pz(i), 2 * y + c, x)

    def peers(self):
        out = [self.core] + [self.dy(i) for i in range(1, self.ny)]
        out += [self.dx(i) for i in range(1, self.nx)]
        return out + [self.dz(i) for i in range(1, self.nz)]

    def copy_a(self, k, src):
        return remote(src, self.a.at[k], self.sa.at[k], self.ra.at[k], self.core)

    def start(self):
        c = self.me[2]
        for ref, first, count in self.parts:
            for j in range(count):
                src = ref.at[:, 1 - c, j]
                self.copy_a(first + j, src).start()

    def copy_b(self, k, i, there):
        slot = self.ny - i - 1 if there else i - 1
        return remote(self.a.at[k, self.py(i)], self.b.at[k, slot], self.sb.at[k, i - 1], self.rb.at[k, slot], self.dy(i))

    def stage_b(self, k):
        c = self.me[2]
        self.copy_a(k, self.a.at[k]).wait_recv()
        for i in list(range(1, self.ny)) + [0]:
            p = self.py(i)
            for ref, first, count in self.parts:
                @pl.when((k >= first) & (k < first + count))
                def _():
                    j = jnp.clip(k - first, 0, count - 1)
                    self.a[k, p] = (self.a[k, p].astype(F32) + ref[p, c, j].astype(F32)).astype(BF)
            if i:
                self.copy_b(k, i, True).start()

    def copy_c(self, k, i, there):
        slot = self.me[3] if there else self.px(i)
        src = self.a.at[k, self.me[1], pl.ds(self.px(i) * self.half, self.half)]
        return remote(src, self.c.at[k, slot], self.sc.at[k, self.px(i)], self.rc.at[k, slot], self.dx(i))

    def stage_c(self, k):
        y = self.me[1]
        total = self.a[k, y].astype(F32)
        for i in range(1, self.ny):
            self.copy_b(k, i, False).wait_recv()
            total = total + self.b[k, i - 1].astype(F32)
        for i in range(1, self.ny):
            self.copy_b(k, i, True).wait_send()
        self.a[k, y] = total.astype(BF)
        for i in range(1, self.nx):
            self.copy_c(k, i, True).start()

    def pieces(self, low, high, count):
        return pl.ds(self.me[3] * self.half + (2 * low + high) * self.piece, count * self.piece)

    def copy_z(self, k, stage):
        if stage == 0:
            src, dst, peer = self.a.at[k, self.me[1], self.pieces(1 - self.low, 0, 2)], self.near.at[k], self.one
        elif stage == 1:
            src, dst, peer = self.a.at[k, self.me[1], self.pieces(self.low, 1 - self.high, 1)], self.far.at[k], self.two
        elif stage == 2:
            src = dst = self.out.at[k, self.pieces(self.low, self.high, 1)]
            peer = self.two
        else:
            src = dst = self.out.at[k, self.pieces(self.low, 0, 2)]
            peer = self.one
        return remote(src, dst, self.sz.at[k, stage], self.rz.at[k, stage], peer)

    def stage_d(self, k):
        z, y, c, x = self.me
        mine = pl.ds(x * self.half, self.half)
        total = self.a[k, y, mine].astype(F32)
        for i in range(1, self.nx):
            self.copy_c(k, i, False).wait_recv()
            total = total + self.c[k, self.px(i)].astype(F32)
        for i in range(1, self.nx):
            self.copy_c(k, i, True).wait_send()
        self.a[k, y, mine] = total.astype(BF)
        self.copy_z(k, 0).start()

    def stage_near(self, k):
        y = self.me[1]
        self.copy_z(k, 0).wait_recv()
        self.copy_z(k, 0).wait_send()
        mine = self.pieces(self.low, 0, 2)
        self.a[k, y, mine] = (self.a[k, y, mine].astype(F32) + self.near[k].astype(F32)).astype(BF)
        self.copy_z(k, 1).start()

    def stage_far(self, k):
        self.copy_z(k, 1).wait_recv()
        mine = self.pieces(self.low, self.high, 1)
        self.out[k, mine] = (self.a[k, self.me[1], mine].astype(F32) + self.far[k].astype(F32)).astype(BF)
        self.copy_z(k, 2).start()

    def stage_back(self, k):
        ref = self.out.at[k, self.pieces(self.low, 1 - self.high, 1)]
        remote(ref, ref, self.sz.at[k, 2], self.rz.at[k, 2], self.two).wait_recv()
        self.copy_z(k, 3).start()

    def copy_f(self, k, i, there):
        slot = self.me[3] if there else self.px(i)
        ref = self.out.at[k, pl.ds(slot * self.half, self.half)]
        return remote(ref, ref, self.sf.at[k, self.px(i)], self.rf.at[k, slot], self.dx(i))

    def stage_f(self, k):
        ref = self.out.at[k, self.pieces(1 - self.low, 0, 2)]
        remote(ref, ref, self.sz.at[k, 3], self.rz.at[k, 3], self.one).wait_recv()
        for i in range(1, self.nx):
            self.copy_f(k, i, True).start()

    def step(self, t):
        for lag, stage in enumerate(
            (self.stage_c, self.stage_d, self.stage_near, self.stage_far, self.stage_back, self.stage_f)
        ):
            @pl.when((t >= lag) & (t < self.chunks + lag))
            def _():
                stage(t - lag)

    def finish(self):
        def body(k, _):
            for i in range(1, self.nx):
                self.copy_f(k, i, False).wait_recv()
            self.copy_a(k, self.a.at[k]).wait_send()
            for i in range(1, self.nx):
                self.copy_f(k, i, True).wait_send()
            for stage in range(1, 4):
                self.copy_z(k, stage).wait_send()
            return 0

        lax.fori_loop(0, self.chunks, body, 0)

    @staticmethod
    def sems(chunks, ny, nx):
        out = [pltpu.SemaphoreType.DMA((chunks,))] * 2
        for n in (ny - 1, nx, 4, nx):
            out += [pltpu.SemaphoreType.DMA((chunks, n))] * 2
        return out


class OwnSums:
    def __init__(self, sums, part, out, bufs, sems):
        self.s, self.part, self.out = sums, part, out
        self.a, self.b, self.c = bufs
        self.sa, self.ra, self.sb, self.rb, self.sc, self.rc, self.se, self.re, self.sf, self.rf = sems
        self.half = self.c.shape[2]

    def copy_a(self, h):
        return remote(self.part.at[h, :, 1 - self.s.me[2]], self.a.at[h], self.sa.at[h], self.ra.at[h], self.s.core)

    def copy_b(self, h, i, there):
        s = self.s
        slot = s.ny - i - 1 if there else i - 1
        return remote(self.a.at[h, s.py(i)], self.b.at[h, slot], self.sb.at[h, i - 1], self.rb.at[h, slot], s.dy(i))

    def copy_c(self, h, i, there):
        s = self.s
        slot = s.me[3] if there else s.px(i)
        src = self.a.at[h, s.me[1], pl.ds(s.px(i) * self.half, self.half)]
        return remote(src, self.c.at[h, slot], self.sc.at[h, s.px(i)], self.rc.at[h, slot], s.dx(i))

    def copy_e(self, h, i, there):
        s = self.s
        slot = s.me[0] if there else s.pz(i)
        ref = self.out.at[h, slot, pl.ds(s.me[3] * self.half, self.half)]
        return remote(ref, ref, self.se.at[h, s.pz(i)], self.re.at[h, slot], s.dz(i))

    def copy_f(self, h, i, there):
        s = self.s
        slot = s.me[3] if there else s.px(i)
        ref = self.out.at[h, :, pl.ds(slot * self.half, self.half)]
        return remote(ref, ref, self.sf.at[h, s.px(i)], self.rf.at[h, slot], s.dx(i))

    def stage_b(self, h):
        s = self.s
        self.copy_a(h).wait_recv()
        for i in list(range(1, s.ny)) + [0]:
            p = s.py(i)
            self.a[h, p] = (self.a[h, p].astype(F32) + self.part[h, p, s.me[2]].astype(F32)).astype(BF)
            if i:
                self.copy_b(h, i, True).start()

    def stage_c(self, h):
        s = self.s
        total = self.a[h, s.me[1]].astype(F32)
        for i in range(1, s.ny):
            self.copy_b(h, i, False).wait_recv()
            total = total + self.b[h, i - 1].astype(F32)
        self.a[h, s.me[1]] = total.astype(BF)
        for i in range(1, s.nx):
            self.copy_c(h, i, True).start()

    def stage_e(self, h):
        s = self.s
        mine = pl.ds(s.me[3] * self.half, self.half)
        total = self.a[h, s.me[1], mine].astype(F32)
        for i in range(1, s.nx):
            self.copy_c(h, i, False).wait_recv()
            total = total + self.c[h, s.px(i)].astype(F32)
        self.out[h, s.me[0], mine] = total.astype(BF)
        for i in range(1, s.nz):
            self.copy_e(h, i, True).start()

    def stage_f(self, h):
        s = self.s
        for i in range(1, s.nz):
            self.copy_e(h, i, False).wait_recv()
        for i in range(1, s.nx):
            self.copy_f(h, i, True).start()

    def stages(self):
        return (self.stage_b, self.stage_c, self.stage_e, self.stage_f)

    def finish(self, h):
        s = self.s
        self.copy_a(h).wait_send()
        for i in range(1, s.ny):
            self.copy_b(h, i, True).wait_send()
        for i in range(1, s.nx):
            self.copy_c(h, i, True).wait_send()
            self.copy_f(h, i, False).wait_recv()
            self.copy_f(h, i, True).wait_send()
        for i in range(1, s.nz):
            self.copy_e(h, i, True).wait_send()

    @staticmethod
    def sems(heads, ny, nx, nz):
        out = [pltpu.SemaphoreType.DMA((heads,))] * 2
        for n in (ny - 1, nx, nz, nx):
            out += [pltpu.SemaphoreType.DMA((heads, n))] * 2
        return out


def bwd_kernel(counts, *refs):
    refs = list(refs)

    def take(n):
        out = refs[:n]
        del refs[:n]
        return out

    prefix_ref, proj_ref, conv_ref, do_ref, o_ref, lse_ref, normed_ref = take(7)
    part_refs = take(len(counts))
    gp_ref, sum_ref, own_ref = take(3)
    wide, qs, ks, vs, dos, delta, dq, dk, dv, gk, gv, gwide, gp_s, gpt, own_part = take(15)
    send, recv, gsend, grecv = take(4)
    bufs = take(5)
    sems = take(10)
    own_bufs = take(3)
    own_sems = take(10)
    heads, length, _ = qs.shape
    width = gwide.shape[1]
    blocks = dos.shape[1]
    rows = length//blocks
    prefix = prefix_ref[0]
    parts = []
    first = 0
    for ref, count in zip(part_refs, counts):
        parts.append((ref, first, count))
        first += count
    sums = Sums(parts, sum_ref, bufs, sems, blocks)
    own = OwnSums(sums, own_part, own_ref, own_bufs, own_sems)
    z, y, c, x = sums.me
    greet(sums.peers())
    sums.start()

    def block_copy(h, i, at):
        return remote(do_ref.at[i * heads + h], dos.at[h, at], send.at[h, i], recv.at[h, at], (i, 2 * y + c, x))

    for h in range(heads):
        for i in range(1, blocks):
            block_copy(h, (z + i) % blocks, z).start()
        dos[h, z] = do_ref[z * heads + h]

    def gp_copy(h, i, at):
        return remote(gpt.at[h, i], gp_ref.at[at * heads + h], gsend.at[h, i], grecv.at[h, at], (i, 2 * y + c, x))

    convolve(proj_ref, conv_ref, wide, (qs, ks, vs))

    def head(h, _):
        for i in range(1, blocks):
            there = (z + i) % blocks
            block_copy(h, there, there).wait_recv()
        for i in range(blocks):
            prod = dos[h, i].astype(F32) * o_ref[h, i].astype(F32)
            delta[i] = jnp.broadcast_to(jnp.sum(prod, axis=0, keepdims=True), (8, rows))
        dq[...] = jnp.zeros(dq.shape, F32)
        def kblock(j, _):
            t = h*blocks + j
            @pl.when(t < sums.chunks)
            def _():
                sums.stage_b(t)
            turn = (2*t)//3
            @pl.when((turn > 0) & ((2*t)%3 != 2))
            def _():
                sums.step(turn - 1)
            for n, stage in enumerate(own.stages()):
                @pl.when((h > 0) & (j == n))
                def _():
                    stage(h - 1)
            kat = pl.ds(pl.multiple_of(j*rows, rows), rows)
            k = ks[h, kat]; v = vs[h, kat]
            dk[...] = jnp.zeros(dk.shape, F32)
            dv[...] = jnp.zeros(dv.shape, F32)
            def step(i, masked):
                qat = pl.ds(pl.multiple_of(i*rows, rows), rows)
                q = qs[h, qat]; do = dos[h, i]
                s = nt(k, q)
                p = jnp.exp(s - lse_ref[h, 0:1, qat])
                if masked:
                    p = jnp.where(mask_t(i, j, rows, prefix), p, 0.0)
                dv[...] += nt(p.astype(BF), do)
                dp = jnp.dot(v, do, preferred_element_type=F32)
                ds = (p*(dp - delta[i, 0:1])).astype(BF)
                dk[...] += jnp.dot(ds, q, preferred_element_type=F32)
                dq[qat] += tn(ds, k)
                return 0
            lax.fori_loop(j+1, blocks, lambda i, _: step(i, False), 0)
            lax.fori_loop(jnp.where(j < blocks//2, 0, j), j+1, lambda i, _: step(i, True), 0)
            gk[kat] = dk[...].astype(BF)
            gv[kat] = dv[...].astype(BF)
            return 0
        lax.fori_loop(0, blocks, kblock, 0)
        def fill(c, _):
            at = pl.ds(pl.multiple_of(c*rows, rows), rows)
            gq = (dq[at]*(HEAD_DIM**-0.5)).astype(BF)
            gwide[at] = jnp.concatenate([gq, gk[at], gv[at]], axis=1).astype(F32)
            return 0
        lax.fori_loop(0, blocks, fill, 0)
        taps = conv_ref[h]
        def out(i, total):
            base = pl.multiple_of(i*rows, rows)
            g = gwide[pl.ds(base, rows+8)]
            w = wide[h, pl.ds(base, rows+8)]
            g0 = g[:rows]
            gp = taps[0:1]*g0 + taps[1:2]*g[1:rows+1] + taps[2:3]*g[2:rows+2]
            gp_s[pl.ds(base, rows)] = gp.astype(BF)
            gpt[h, i] = jnp.transpose(gp).astype(BF)
            @pl.when(i != z)
            def _():
                gp_copy(h, i, z).start()
            add = [jnp.sum(g0*w[8-t:8-t+rows], axis=0, keepdims=True) for t in range(3)]
            return tuple(a+b for a, b in zip(total, add))
        total = lax.fori_loop(0, blocks, out, tuple(jnp.zeros((1, width), F32) for _ in range(3)))
        gp_ref[z * heads + h] = gpt[h, z]
        grad = jnp.dot(normed_ref[...], gp_s[...], preferred_element_type=F32).astype(BF)
        shape = own_part.shape[1:]
        mine = grad.shape[0] // (8 * shape[0] * shape[1])
        own_part[h, :, :, 0:mine] = grad.reshape(shape[0], shape[1], mine, 8, width)
        extra = jnp.concatenate(list(total) + [jnp.zeros((5, width), F32)], axis=0).astype(BF)
        own_part[h, :, :, mine] = jnp.broadcast_to(extra, shape[:2] + (8, width))
        for spare in range(mine + 1, shape[2]):
            own_part[h, :, :, spare] = jnp.zeros(shape[:2] + (8, width), BF)
        own.copy_a(h).start()
        return 0
    gwide[length:length+8] = jnp.zeros((8, width), F32)
    lax.fori_loop(0, heads, head, 0)
    steps = heads*blocks
    turns = (2*(steps - 1))//3
    def rest(t, _):
        sums.stage_b(t)
        return 0
    lax.fori_loop(steps, sums.chunks, rest, 0)
    for n, stage in enumerate(own.stages()):
        sums.step(turns + n)
        stage(heads - 1)
    count = len(own.stages())
    def tail(t, _):
        sums.step(t)
        return 0
    lax.fori_loop(turns + count, max(sums.chunks + 5, turns + count), tail, 0)
    sums.finish()
    def done(h, _):
        own.finish(h)
        for i in range(1, blocks):
            there = (z + i) % blocks
            block_copy(h, there, z).wait_send()
            gp_copy(h, there, there).wait_recv()
            gp_copy(h, there, z).wait_send()
        return 0
    lax.fori_loop(0, heads, done, 0)

def attention_bwd(prefix, proj, conv, do, o, lse, normed, parts, shape):
    length = proj.shape[0]
    heads, blocks = o.shape[:2]
    width = 3 * HEAD_DIM
    rows = length // blocks
    counts = tuple(part.shape[2] for part in parts)
    ny, _, _, units = parts[0].shape[:4]
    unit = parts[0].shape[4:]
    nx = shape["replica"]
    chunks = sum(counts)
    half = units // nx
    own_units = -(-(normed.shape[0] // (16 * ny) + 1) // nx) * nx
    own_unit = (8, width)
    vm = pl.BlockSpec(memory_space=pltpu.VMEM)
    dma = pltpu.SemaphoreType.DMA
    per = pltpu.VMEM((heads, length, HEAD_DIM), BF)
    return pl.pallas_call(
        functools.partial(bwd_kernel, counts),
        out_shape=(
            jax.ShapeDtypeStruct((heads * blocks, width, rows), BF),
            jax.ShapeDtypeStruct((chunks, units) + unit, BF),
            jax.ShapeDtypeStruct((heads, blocks, own_units) + own_unit, BF),
        ),
        in_specs=[pl.BlockSpec(memory_space=pltpu.SMEM)] + [vm]*(6 + len(parts)),
        out_specs=(vm, vm, vm),
        scratch_shapes=[pltpu.VMEM((heads, 8+length, width), F32), per, per, per, pltpu.VMEM(o.shape, BF), pltpu.VMEM((blocks, 8, rows), F32),
            pltpu.VMEM((length, HEAD_DIM), F32), pltpu.VMEM((rows, HEAD_DIM), F32), pltpu.VMEM((rows, HEAD_DIM), F32),
            pltpu.VMEM((length, HEAD_DIM), BF), pltpu.VMEM((length, HEAD_DIM), BF),
            pltpu.VMEM((length+8, width), F32), pltpu.VMEM((length, width), BF), pltpu.VMEM((heads, blocks, width, rows), BF),
            pltpu.VMEM((heads, ny, 2, own_units) + own_unit, BF)]
            + [dma((heads, blocks))] * 4
            + [pltpu.VMEM((chunks, ny, units) + unit, BF), pltpu.VMEM((chunks, ny - 1, units) + unit, BF),
            pltpu.VMEM((chunks, nx, half) + unit, BF), pltpu.VMEM((chunks, half // 2) + unit, BF), pltpu.VMEM((chunks, half // 4) + unit, BF)]
            + Sums.sems(chunks, ny, nx)
            + [pltpu.VMEM((heads, ny, own_units) + own_unit, BF), pltpu.VMEM((heads, ny - 1, own_units) + own_unit, BF),
            pltpu.VMEM((heads, nx, own_units // nx) + own_unit, BF)]
            + OwnSums.sems(heads, ny, nx, blocks),
        compiler_params=pltpu.CompilerParams(vmem_limit_bytes=67043328, collective_id=3, has_side_effects=True),
        cost_estimate=pl.CostEstimate(flops=10*heads*length*length*HEAD_DIM, bytes_accessed=length*width*4, transcendentals=heads*length*length),
        name="attention_bwd",
    )(prefix, proj, conv, do, o, lse, normed, *parts)


def rms_scale(values):
    return lax.rsqrt(jnp.mean(values * values, axis=-1, keepdims=True) + 1e-06)


def norm_back(values, scale_rows, gain, upstream):
    weighted = upstream * gain
    grad_values = scale_rows * weighted - values * scale_rows**3 * jnp.mean(
        weighted * values, axis=-1, keepdims=True
    )
    return grad_values


def dot(a, b):
    return jnp.dot(a, b, preferred_element_type=F32)


def per_device(
    tokens, prefix_len, w_qkv, w_out, w_up, w_down, conv_w, gain_attn, gain_ffn, cotangent
):
    blocks = lax.axis_size("seq")
    me = lax.axis_index("seq")
    rows, width = tokens.shape[1:]
    own = HEADS // blocks * HEAD_DIM
    depth = w_qkv.shape[0]

    shards, copies = lax.axis_size("shard"), lax.axis_size("replica")
    heads = HEADS // blocks
    columns = w_qkv.reshape(depth, 3, blocks, heads, HEAD_DIM).transpose(2, 0, 3, 1, 4)
    gains = jnp.pad(jnp.stack([gain_attn, gain_ffn]), ((0, 0), (0, conv_w.shape[1] - depth)))
    small = jnp.pad(jnp.concatenate([gains, conv_w]), ((0, 3), (0, 0)))
    normed_all, projected, small, full_qkv, full_out, full_up = gather_all(
        tokens[0], small, columns.reshape(blocks, depth, 3 * own), w_out, w_up, blocks, shards
    )
    full_qkv = full_qkv.reshape(blocks, width, 3 * own)
    full_out = full_out.reshape(width, width)
    full_up = full_up.reshape(width, -1)
    full_gone = small[:, 0, 0, :depth].reshape(width).astype(F32)
    full_gtwo = small[:, 0, 1, :depth].reshape(width).astype(F32)
    full_conv = small[:, 0, 2:5].transpose(1, 0, 2)
    own_conv = lax.dynamic_index_in_dim(full_conv.reshape(3, 3, blocks, heads, HEAD_DIM), me, 2, False)
    own_conv = own_conv.transpose(2, 0, 1, 3).reshape(heads, 3, 3 * HEAD_DIM).astype(F32)
    attended_own, logsum, attended, full_down = attention_fwd(
        prefix_len, projected, own_conv, w_down.reshape(-1, depth, width), blocks, shards
    )
    full_down = full_down.reshape(-1, width)
    attended = attended.reshape(width, rows)

    inputs = tokens[0].astype(F32)
    scale_one = rms_scale(inputs)
    hidden = inputs + tn(attended, full_out)
    scale_two = rms_scale(hidden)
    normed_two_b = (hidden * scale_two * full_gtwo).astype(BF)
    positive = jnp.maximum(dot(normed_two_b, full_up), 0.0)
    active_b = (positive * positive).astype(BF)
    output = hidden + dot(active_b, full_down)

    incoming = cotangent[0]
    grad_upper_b = (dot(incoming, full_down.T) * 2.0 * positive).astype(BF)
    grad_normed_two = dot(grad_upper_b, full_up.T)
    grad_hidden = incoming.astype(F32) + norm_back(hidden, scale_two, full_gtwo, grad_normed_two)
    grad_hidden_b = grad_hidden.astype(BF)
    grad_attended = nt(full_out, grad_hidden_b).astype(BF)

    mine = depth // 8

    def cut(grad):
        return grad.astype(BF).reshape(shards // 2, 2, -1, mine, 8, width)

    parts = [
        cut(dot(normed_two_b.T, grad_upper_b[:, i * width : (i + 1) * width]))
        for i in range(grad_upper_b.shape[1] // width)
    ]
    parts += [cut(dot(active_b.T, incoming)), cut(dot(attended, grad_hidden_b))]
    pieces = sum(part.shape[2] for part in parts)
    if mine % (copies * blocks):
        units = -(-pieces * mine // (copies * blocks)) * copies * blocks
        joined = [part.reshape(shards // 2, 2, -1, 8, width) for part in parts]
        joined.append(jnp.zeros((shards // 2, 2, units - pieces * mine, 8, width), BF))
        joined = jnp.concatenate(joined, axis=2)
        parts = [joined.reshape(shards // 2, 2, -1, copies * blocks, 8, width)]

    grad_projected, sums, own_sums = attention_bwd(
        prefix_len, projected, own_conv, grad_attended.reshape(HEADS, HEAD_DIM, rows),
        attended_own, logsum, normed_all, parts, {"replica": copies},
    )
    grad_projected = grad_projected.reshape(blocks, 3 * own, rows)
    grad_normed = sum(
        lax.dot_general(
            grad_projected[j], full_qkv[j], (((0,), (1,)), ((), ())), preferred_element_type=F32
        )
        for j in range(blocks)
    )
    grad_input = (grad_hidden + norm_back(inputs, scale_one, full_gone, grad_normed)).astype(BF)

    sums = sums.reshape(-1, 8, width)[: pieces * mine].reshape(pieces, depth, width)
    ups = w_up.shape[1] // width
    total_up = jnp.concatenate(list(sums[:ups]), axis=1).astype(F32)
    total_down = sums[ups:-1].reshape(-1, width).astype(F32)
    total_out = sums[-1].astype(F32)

    def merge(array):
        array = array.reshape(heads, blocks, -1, 3, HEAD_DIM).transpose(2, 3, 1, 0, 4)
        return array.reshape(array.shape[0], -1).astype(F32)

    total_qkv = merge(own_sums[:, :, :mine].reshape(heads, blocks, depth, -1))
    total_conv = merge(own_sums[:, :, mine, :3])
    at = lax.axis_index("shard")

    def gain_grad(grad, weight, gain):
        return jnp.sum(grad * weight.astype(F32), axis=1) / gain.astype(F32)

    return (
        output[None].astype(BF),
        grad_input[None],
        total_qkv,
        total_out,
        total_up,
        total_down,
        lax.dynamic_slice_in_dim(total_conv, at * conv_w.shape[1], conv_w.shape[1], 1),
        gain_grad(total_qkv, w_qkv, gain_attn),
        gain_grad(total_up, w_up, gain_ffn),
    )


def solution(mesh):
    placed = (
        P(("shard", "replica"), "seq", None),
        P(("shard", "replica")),
        P("shard", None),
        P("shard", None),
        P("shard", None),
        P("shard", None),
        P(None, "shard"),
        P("shard"),
        P("shard"),
        P(("shard", "replica"), "seq", None),
    )
    return jax.shard_map(
        per_device,
        mesh=mesh,
        in_specs=placed,
        out_specs=(
            P(("shard", "replica"), "seq", None),
            P(("shard", "replica"), "seq", None),
            P("shard", None),
            P("shard", None),
            P("shard", None),
            P("shard", None),
            P(None, "shard"),
            P("shard"),
            P("shard"),
        ),
        check_vma=False,
    )
```

```python
import functools

import jax
import jax.numpy as jnp
from jax import lax
from jax.experimental import pallas as pl
from jax.experimental.pallas import tpu as pltpu
from jax.sharding import PartitionSpec as P

HEADS = 12
HEAD_DIM=64
NEG=-1e30
F32=jnp.float32
BF=jnp.bfloat16

def nt(a,b):
    return lax.dot_general(a,b,(((1,),(1,)),((),())),preferred_element_type=F32)
def tn(a,b):
    return lax.dot_general(a,b,(((0,),(0,)),((),())),preferred_element_type=F32)

def convolve(proj_ref, conv_ref, wide, parts):
    length = proj_ref.shape[0]
    heads, _, width = wide.shape
    rows = min(512, length)
    for h in range(heads):
        wide[h, 0:8] = jnp.zeros((8, width), F32)
        for c in range(length//rows):
            wide[h, 8+c*rows:8+(c+1)*rows] = proj_ref[c*rows:(c+1)*rows, h*width:(h+1)*width].astype(F32)
    def body(c, _):
        base = pl.multiple_of(c*rows, rows)
        for h in range(heads):
            x = wide[h, pl.ds(base, rows+8)]
            taps = conv_ref[h]
            mixed = taps[0:1]*x[8:] + taps[1:2]*x[7:7+rows] + taps[2:3]*x[6:6+rows]
            for p, ref in enumerate(parts):
                piece = mixed[:, p*HEAD_DIM:(p+1)*HEAD_DIM].astype(BF)
                if p == 0:
                    piece = piece * jnp.asarray(HEAD_DIM**-0.5, BF)
                ref[h, pl.ds(base, rows)] = piece
        return 0
    lax.fori_loop(0, length//rows, body, 0)

def mask_t(i, j, rows, prefix):
    kpos = j*rows + lax.broadcasted_iota(jnp.int32, (rows, 1), 0)
    qpos = i*rows + lax.broadcasted_iota(jnp.int32, (1, rows), 1)
    return (kpos <= qpos) | ((kpos < prefix) & (qpos < prefix))

def mask_n(i, j, rows, prefix):
    qpos = i*rows + lax.broadcasted_iota(jnp.int32, (rows, 1), 0)
    kpos = j*rows + lax.broadcasted_iota(jnp.int32, (1, rows), 1)
    return (kpos <= qpos) | ((kpos < prefix) & (qpos < prefix))

MESH = pl.DeviceIdType.MESH


def remote(src, dst, send, recv, peer):
    return pltpu.make_async_remote_copy(
        src_ref=src, dst_ref=dst, send_sem=send, recv_sem=recv, device_id=peer, device_id_type=MESH
    )


def greet(peers):
    barrier = pltpu.get_barrier_semaphore()
    for peer in peers:
        pl.semaphore_signal(barrier, inc=1, device_id=peer, device_id_type=MESH)
    pl.semaphore_wait(barrier, len(peers))


def split_shard():
    s = lax.axis_index("shard")
    return lax.axis_index("seq"), s // 2, s % 2, lax.axis_index("replica")


class Gather:
    def __init__(self, src, dst, sems, major=False):
        self.src, self.dst, self.major = src, dst, major
        self.sy, self.ry, self.sk, self.rk, self.local = sems
        self.ny = dst.shape[1 if major else 0] // 2
        self.chunks = dst.shape[0 if major else 1]
        self.z, self.y, self.c, self.x = split_shard()
        self.core = (self.z, 2 * self.y + 1 - self.c, self.x)

    def py(self, i):
        return (self.y + i) % self.ny

    def dy(self, i):
        return (self.z, 2 * self.py(i) + self.c, self.x)

    def peers(self):
        return [self.core] + [self.dy(i) for i in range(1, self.ny)]

    def slot(self, p, core, j):
        shard = 2 * p + core
        return self.dst.at[j, shard] if self.major else self.dst.at[shard, j]

    def own(self):
        shard = 2 * self.y + self.c
        dst = self.dst.at[:, shard] if self.major else self.dst.at[shard]
        return pltpu.make_async_copy(self.src, dst, self.local.at[0])

    def over_y(self, j, i):
        slot = self.slot(self.y, self.c, j)
        return remote(self.src.at[j], slot, self.sy.at[j, self.py(i)], self.ry.at[j, self.y], self.dy(i))

    def to_core(self, j):
        slot = self.slot(self.y, self.c, j)
        return remote(self.src.at[j], slot, self.sk.at[j, self.y], self.rk.at[j, self.y], self.core)

    def pass_on(self, j, i):
        ref = self.slot(self.py(i), self.c, j)
        return remote(ref, ref, self.sk.at[j, self.py(i)], self.rk.at[j, self.py(i)], self.core)

    def send(self, j):
        for i in range(1, self.ny):
            self.over_y(j, i).start()
        self.to_core(j).start()

    def start(self):
        for j in range(self.chunks):
            self.send(j)
        self.own().start()

    def relay(self, j):
        for i in range(1, self.ny):
            ref = self.slot(self.py(i), self.c, j)
            remote(ref, ref, self.sy.at[j, self.py(i)], self.ry.at[j, self.py(i)], self.dy(i)).wait_recv()
            self.pass_on(j, i).start()

    def arrive(self, j):
        for i in range(self.ny):
            ref = self.slot(self.py(i), 1 - self.c, j)
            remote(ref, ref, self.sk.at[j, self.py(i)], self.rk.at[j, self.py(i)], self.core).wait_recv()

    def sent(self, j):
        self.to_core(j).wait_send()
        for i in range(1, self.ny):
            self.over_y(j, i).wait_send()
            self.pass_on(j, i).wait_send()

    def finish(self):
        self.own().wait()
        for j in range(self.chunks):
            self.arrive(j)
            self.sent(j)

    @staticmethod
    def sems(shards, chunks):
        return [pltpu.SemaphoreType.DMA((chunks, shards // 2))] * 4 + [pltpu.SemaphoreType.DMA((1,))]


def gather_kernel(
    tok_ref, small_ref, qkv_ref, out_ref, up_ref,
    normed_ref, proj_ref, small_all, qkv_all, out_all, up_all,
    toks, weight_s, wsem, sl, sr, rl, rr, *sems,
):
    blocks, rows, width = toks.shape
    _, shards, depth, columns = qkv_all.shape
    small, qkv, out, up = (
        Gather(src, dst, sems[5 * i : 5 * i + 5], major=i == 1)
        for i, (src, dst) in enumerate(
            ((small_ref, small_all), (qkv_ref, qkv_all), (out_ref, out_all), (up_ref, up_all))
        )
    )
    z, y, c, x = split_shard()
    shard = 2 * y + c
    left, right = (z - 1, shard, x), (z + 1, shard, x)
    has_left, has_right = z > 0, z < blocks - 1
    greet(small.peers() + [((z + i) % blocks, shard, x) for i in range(1, blocks)])

    def go_left(b, src):
        return remote(src, toks.at[b], sl.at[b], rr.at[b], left)

    def go_right(b, src):
        return remote(src, toks.at[b], sr.at[b], rl.at[b], right)

    small.start()
    qkv.send(z)
    qkv.own().start()

    @pl.when(has_left)
    def _():
        go_left(z, tok_ref).start()

    @pl.when(has_right)
    def _():
        go_right(z, tok_ref).start()

    out.start()
    up.start()
    for i in range(1, blocks):
        qkv.send((z + i) % blocks)
    small.relay(0)
    qkv.relay(z)
    small.finish()
    qkv.own().wait()
    qkv.arrive(z)
    gain = jnp.concatenate([small_all[s, 0, 0:1, :depth] for s in range(shards)], axis=1).astype(F32)
    fetch = pltpu.make_async_copy(qkv_all.at[z], weight_s, wsem.at[0])
    fetch.start()
    fetch.wait()
    weight = weight_s[...].reshape(shards * depth, columns)

    def project(b, values):
        at = pl.ds(pl.multiple_of(b * rows, rows), rows)
        values = values.astype(F32)
        scale = lax.rsqrt(jnp.mean(values * values, axis=-1, keepdims=True) + 1e-06)
        normed = values * scale * gain
        proj_ref[at] = jnp.dot(normed.astype(BF), weight, preferred_element_type=F32).astype(BF)
        normed_ref[:, at] = jnp.transpose(normed).astype(BF)

    project(z, tok_ref[...])
    for d in range(1, blocks):
        before, after = z - d, z + d

        @pl.when(before >= 0)
        def _():
            go_right(before, toks.at[before]).wait_recv()

            @pl.when(has_right)
            def _():
                go_right(before, toks.at[before]).start()

        @pl.when(after < blocks)
        def _():
            go_left(after, toks.at[after]).wait_recv()

            @pl.when(has_left)
            def _():
                go_left(after, toks.at[after]).start()

        @pl.when(before >= 0)
        def _():
            project(before, toks[before])

        @pl.when(after < blocks)
        def _():
            project(after, toks[after])

        if d == 1:
            out.relay(0)
        last = up.chunks * d // (blocks - 1)
        for j in range(up.chunks * (d - 1) // (blocks - 1), last):
            up.relay(j)

    for i in range(1, blocks):
        qkv.relay((z + i) % blocks)
    out.finish()
    up.finish()
    for i in range(1, blocks):
        qkv.arrive((z + i) % blocks)
    for j in range(blocks):
        qkv.sent(j)

    def sent(b, _):
        @pl.when((b <= z) & has_right)
        def _():
            go_right(b, toks.at[b]).wait_send()

        @pl.when((b >= z) & has_left)
        def _():
            go_left(b, toks.at[b]).wait_send()

        return 0

    lax.fori_loop(0, blocks, sent, 0)


def gather_all(tokens, small, qkv, out, up, blocks, shards):
    rows, width = tokens.shape
    vm = pl.BlockSpec(memory_space=pltpu.VMEM)
    hbm = pl.BlockSpec(memory_space=pl.ANY)
    cut = 4
    arrays = [
        small[None],
        qkv,
        out[None],
        up.reshape(cut, up.shape[0] // cut, up.shape[1]),
    ]
    dma = pltpu.SemaphoreType.DMA
    sems = [dma((blocks,))] * 4
    for array in arrays:
        sems += Gather.sems(shards, array.shape[0])
    return pl.pallas_call(
        gather_kernel,
        out_shape=[
            jax.ShapeDtypeStruct((width, blocks * rows), BF),
            jax.ShapeDtypeStruct((blocks * rows, qkv.shape[2]), BF),
        ]
        + [
            jax.ShapeDtypeStruct(
                (blocks, shards) + array.shape[1:] if i == 1 else (shards,) + array.shape, BF
            )
            for i, array in enumerate(arrays)
        ],
        in_specs=[vm] * 5,
        out_specs=[vm] * 3 + [hbm] * 3,
        scratch_shapes=[pltpu.VMEM((blocks, rows, width), BF), pltpu.VMEM((shards,) + qkv.shape[1:], BF), dma((1,))]
        + sems,
        compiler_params=pltpu.CompilerParams(
            vmem_limit_bytes=60 * 1024 * 1024, collective_id=4, has_side_effects=True
        ),
        name="gather_all",
    )(tokens, *arrays)


def fwd_kernel(prefix_ref, proj_ref, conv_ref, down_ref, own_ref, lse_ref, rows_ref, down_all, wide, qs, ks, vs, m_s, l_s, acc_s, o_s, r_s, send, recv, *sems):
    heads = qs.shape[0]
    length = proj_ref.shape[0]
    blocks = own_ref.shape[1]
    rows = length // blocks
    prefix = prefix_ref[0]
    z, s_at, x = lax.axis_index("seq"), lax.axis_index("shard"), lax.axis_index("replica")

    def block_copy(h, i, at):
        return remote(o_s.at[h, i], r_s.at[at * heads + h], send.at[h, i], recv.at[h, at], (i, s_at, x))

    down = Gather(down_ref, down_all, sems)
    greet([((z + i) % blocks, s_at, x) for i in range(1, blocks)] + down.peers())
    down.start()
    convolve(proj_ref, conv_ref, wide, (qs, ks, vs))
    def head(h, _):
        for j in range(down.chunks):
            @pl.when(h == 1 + (j + 1) // 2)
            def _():
                down.relay(j)
        def qblock(i, _):
            q = qs[h, pl.ds(pl.multiple_of(i*rows, rows), rows)]
            m_s[...] = jnp.full((1, rows), NEG, F32)
            l_s[...] = jnp.zeros((1, rows), F32)
            acc_s[...] = jnp.zeros((HEAD_DIM, rows), F32)
            def step(j, masked):
                at = pl.ds(pl.multiple_of(j*rows, rows), rows)
                s = nt(ks[h, at], q)
                if masked:
                    s = jnp.where(mask_t(i, j, rows, prefix), s, NEG)
                m_old = m_s[...]
                m_new = jnp.maximum(m_old, jnp.max(s, axis=0, keepdims=True))
                p = jnp.exp(s - m_new)
                a = jnp.exp(m_old - m_new)
                m_s[...] = m_new
                l_s[...] = a*l_s[...] + jnp.sum(p, axis=0, keepdims=True)
                acc_s[...] = a*acc_s[...] + tn(vs[h, at], p.astype(BF))
                return 0
            lax.fori_loop(0, i, lambda j, _: step(j, False), 0)
            lax.fori_loop(i, jnp.maximum(i+1, blocks//2), lambda j, _: step(j, True), 0)
            l = l_s[...]
            done = (acc_s[...]/l).astype(BF)
            o_s[h, i] = done
            own_ref[h, i] = done
            @pl.when(i != z)
            def _():
                block_copy(h, i, z).start()
            lse = m_s[...] + jnp.log(l)
            lse_ref[h, :, pl.ds(pl.multiple_of(i*rows, rows), rows)] = jnp.broadcast_to(lse, (8, rows))
            return 0
        lax.fori_loop(0, blocks, qblock, 0)
        r_s[z * heads + h] = o_s[h, z]
        return 0
    lax.fori_loop(0, heads, head, 0)
    for j in range(down.chunks):
        if 1 + (j + 1) // 2 >= heads:
            down.relay(j)
    down.finish()
    def finish(h, _):
        for i in range(1, blocks):
            there = (z + i) % blocks
            block_copy(h, there, there).wait_recv()
            block_copy(h, there, z).wait_send()
        return 0
    lax.fori_loop(0, heads, finish, 0)
    rows_ref[...] = r_s[...]

def attention_fwd(prefix, proj, conv, down, blocks, shards):
    length, width = proj.shape
    heads = width//(3*HEAD_DIM)
    rows = length // blocks
    vm = pl.BlockSpec(memory_space=pltpu.VMEM)
    own = (heads, blocks, HEAD_DIM, rows)
    every = (heads * blocks, HEAD_DIM, rows)
    return pl.pallas_call(
        fwd_kernel,
        out_shape=(jax.ShapeDtypeStruct(own, BF), jax.ShapeDtypeStruct((heads, 8, length), F32), jax.ShapeDtypeStruct(every, BF),
            jax.ShapeDtypeStruct((shards,) + down.shape, BF)),
        in_specs=[pl.BlockSpec(memory_space=pltpu.SMEM), vm, vm, vm],
        out_specs=(vm, vm, vm, pl.BlockSpec(memory_space=pl.ANY)),
        scratch_shapes=[pltpu.VMEM((heads, 8+length, 3*HEAD_DIM), F32)] + [pltpu.VMEM((heads, length, HEAD_DIM), BF)]*3 + [
            pltpu.VMEM((1,rows),F32), pltpu.VMEM((1,rows),F32), pltpu.VMEM((HEAD_DIM,rows),F32), pltpu.VMEM(own,BF), pltpu.VMEM(every,BF),
            pltpu.SemaphoreType.DMA((heads, blocks)), pltpu.SemaphoreType.DMA((heads, blocks))] + Gather.sems(shards, down.shape[0]),
        compiler_params=pltpu.CompilerParams(vmem_limit_bytes=60*1024*1024, collective_id=2, has_side_effects=True),
        cost_estimate=pl.CostEstimate(flops=4*heads*length*length*HEAD_DIM, bytes_accessed=length*width*2, transcendentals=heads*length*length),
        name="attention_fwd",
    )(prefix, proj, conv, down)

class Sums:
    def __init__(self, parts, out_ref, bufs, sems, nz):
        self.parts, self.out = parts, out_ref
        self.a, self.b, self.c, self.near, self.far = bufs
        self.sa, self.ra, self.sb, self.rb, self.sc, self.rc, self.sz, self.rz, self.sf, self.rf = sems
        self.chunks, self.ny = self.a.shape[:2]
        self.nx = self.c.shape[1]
        self.nz = nz
        self.half = self.c.shape[2]
        self.piece = self.half // nz
        self.me = split_shard()
        z, y, c, x = self.me
        self.core = (z, 2 * y + 1 - c, x)
        self.low, self.high = z % 2, z // 2
        self.one = (z + 1 - 2 * self.low, 2 * y + c, x)
        self.two = (z + 2 - 4 * self.high, 2 * y + c, x)

    def py(self, i):
        return (self.me[1] + i) % self.ny

    def px(self, i):
        return (self.me[3] + i) % self.nx

    def pz(self, i):
        return (self.me[0] + i) % self.nz

    def dy(self, i):
        z, y, c, x = self.me
        return (z, 2 * self.py(i) + c, x)

    def dx(self, i):
        z, y, c, x = self.me
        return (z, 2 * y + c, self.px(i))

    def dz(self, i):
        z, y, c, x = self.me
        return (self.pz(i), 2 * y + c, x)

    def peers(self):
        out = [self.core] + [self.dy(i) for i in range(1, self.ny)]
        out += [self.dx(i) for i in range(1, self.nx)]
        return out + [self.dz(i) for i in range(1, self.nz)]

    def copy_a(self, k, src):
        return remote(src, self.a.at[k], self.sa.at[k], self.ra.at[k], self.core)

    def start(self):
        c = self.me[2]
        for ref, first, count in self.parts:
            for j in range(count):
                src = ref.at[:, 1 - c, j]
                self.copy_a(first + j, src).start()

    def copy_b(self, k, i, there):
        slot = self.ny - i - 1 if there else i - 1
        return remote(self.a.at[k, self.py(i)], self.b.at[k, slot], self.sb.at[k, i - 1], self.rb.at[k, slot], self.dy(i))

    def stage_b(self, k):
        c = self.me[2]
        self.copy_a(k, self.a.at[k]).wait_recv()
        for i in list(range(1, self.ny)) + [0]:
            p = self.py(i)
            for ref, first, count in self.parts:
                @pl.when((k >= first) & (k < first + count))
                def _():
                    j = jnp.clip(k - first, 0, count - 1)
                    self.a[k, p] = (self.a[k, p].astype(F32) + ref[p, c, j].astype(F32)).astype(BF)
            if i:
                self.copy_b(k, i, True).start()

    def copy_c(self, k, i, there):
        slot = self.me[3] if there else self.px(i)
        src = self.a.at[k, self.me[1], pl.ds(self.px(i) * self.half, self.half)]
        return remote(src, self.c.at[k, slot], self.sc.at[k, self.px(i)], self.rc.at[k, slot], self.dx(i))

    def stage_c(self, k):
        y = self.me[1]
        total = self.a[k, y].astype(F32)
        for i in range(1, self.ny):
            self.copy_b(k, i, False).wait_recv()
            total = total + self.b[k, i - 1].astype(F32)
        for i in range(1, self.ny):
            self.copy_b(k, i, True).wait_send()
        self.a[k, y] = total.astype(BF)
        for i in range(1, self.nx):
            self.copy_c(k, i, True).start()

    def pieces(self, low, high, count):
        return pl.ds(self.me[3] * self.half + (2 * low + high) * self.piece, count * self.piece)

    def copy_z(self, k, stage):
        if stage == 0:
            src, dst, peer = self.a.at[k, self.me[1], self.pieces(1 - self.low, 0, 2)], self.near.at[k], self.one
        elif stage == 1:
            src, dst, peer = self.a.at[k, self.me[1], self.pieces(self.low, 1 - self.high, 1)], self.far.at[k], self.two
        elif stage == 2:
            src = dst = self.out.at[k, self.pieces(self.low, self.high, 1)]
            peer = self.two
        else:
            src = dst = self.out.at[k, self.pieces(self.low, 0, 2)]
            peer = self.one
        return remote(src, dst, self.sz.at[k, stage], self.rz.at[k, stage], peer)

    def stage_d(self, k):
        z, y, c, x = self.me
        mine = pl.ds(x * self.half, self.half)
        total = self.a[k, y, mine].astype(F32)
        for i in range(1, self.nx):
            self.copy_c(k, i, False).wait_recv()
            total = total + self.c[k, self.px(i)].astype(F32)
        for i in range(1, self.nx):
            self.copy_c(k, i, True).wait_send()
        self.a[k, y, mine] = total.astype(BF)
        self.copy_z(k, 0).start()

    def stage_near(self, k):
        y = self.me[1]
        self.copy_z(k, 0).wait_recv()
        self.copy_z(k, 0).wait_send()
        mine = self.pieces(self.low, 0, 2)
        self.a[k, y, mine] = (self.a[k, y, mine].astype(F32) + self.near[k].astype(F32)).astype(BF)
        self.copy_z(k, 1).start()

    def stage_far(self, k):
        self.copy_z(k, 1).wait_recv()
        mine = self.pieces(self.low, self.high, 1)
        self.out[k, mine] = (self.a[k, self.me[1], mine].astype(F32) + self.far[k].astype(F32)).astype(BF)
        self.copy_z(k, 2).start()

    def stage_back(self, k):
        ref = self.out.at[k, self.pieces(self.low, 1 - self.high, 1)]
        remote(ref, ref, self.sz.at[k, 2], self.rz.at[k, 2], self.two).wait_recv()
        self.copy_z(k, 3).start()

    def copy_f(self, k, i, there):
        slot = self.me[3] if there else self.px(i)
        ref = self.out.at[k, pl.ds(slot * self.half, self.half)]
        return remote(ref, ref, self.sf.at[k, self.px(i)], self.rf.at[k, slot], self.dx(i))

    def stage_f(self, k):
        ref = self.out.at[k, self.pieces(1 - self.low, 0, 2)]
        remote(ref, ref, self.sz.at[k, 3], self.rz.at[k, 3], self.one).wait_recv()
        for i in range(1, self.nx):
            self.copy_f(k, i, True).start()

    LAGS = (0, 1, 3, 5, 7, 9)

    def step(self, t):
        stages = (self.stage_c, self.stage_d, self.stage_near, self.stage_far, self.stage_back, self.stage_f)
        for lag, stage in zip(self.LAGS, stages):
            @pl.when((t >= lag) & (t < self.chunks + lag))
            def _():
                stage(t - lag)

    def finish(self):
        def body(k, _):
            for i in range(1, self.nx):
                self.copy_f(k, i, False).wait_recv()
            self.copy_a(k, self.a.at[k]).wait_send()
            for i in range(1, self.nx):
                self.copy_f(k, i, True).wait_send()
            for stage in range(1, 4):
                self.copy_z(k, stage).wait_send()
            return 0

        lax.fori_loop(0, self.chunks, body, 0)

    @staticmethod
    def sems(chunks, ny, nx):
        out = [pltpu.SemaphoreType.DMA((chunks,))] * 2
        for n in (ny - 1, nx, 4, nx):
            out += [pltpu.SemaphoreType.DMA((chunks, n))] * 2
        return out


class OwnSums:
    def __init__(self, sums, part, out, bufs, sems):
        self.s, self.part, self.out = sums, part, out
        self.a, self.b, self.c = bufs
        self.sa, self.ra, self.sb, self.rb, self.sc, self.rc, self.se, self.re, self.sf, self.rf = sems
        self.half = self.c.shape[2]

    def copy_a(self, h):
        return remote(self.part.at[h, :, 1 - self.s.me[2]], self.a.at[h], self.sa.at[h], self.ra.at[h], self.s.core)

    def copy_b(self, h, i, there):
        s = self.s
        slot = s.ny - i - 1 if there else i - 1
        return remote(self.a.at[h, s.py(i)], self.b.at[h, slot], self.sb.at[h, i - 1], self.rb.at[h, slot], s.dy(i))

    def copy_c(self, h, i, there):
        s = self.s
        slot = s.me[3] if there else s.px(i)
        src = self.a.at[h, s.me[1], pl.ds(s.px(i) * self.half, self.half)]
        return remote(src, self.c.at[h, slot], self.sc.at[h, s.px(i)], self.rc.at[h, slot], s.dx(i))

    def copy_e(self, h, i, there):
        s = self.s
        slot = s.me[0] if there else s.pz(i)
        ref = self.out.at[h, slot, pl.ds(s.me[3] * self.half, self.half)]
        return remote(ref, ref, self.se.at[h, s.pz(i)], self.re.at[h, slot], s.dz(i))

    def copy_f(self, h, i, there):
        s = self.s
        slot = s.me[3] if there else s.px(i)
        ref = self.out.at[h, :, pl.ds(slot * self.half, self.half)]
        return remote(ref, ref, self.sf.at[h, s.px(i)], self.rf.at[h, slot], s.dx(i))

    def stage_b(self, h):
        s = self.s
        self.copy_a(h).wait_recv()
        for i in list(range(1, s.ny)) + [0]:
            p = s.py(i)
            self.a[h, p] = (self.a[h, p].astype(F32) + self.part[h, p, s.me[2]].astype(F32)).astype(BF)
            if i:
                self.copy_b(h, i, True).start()

    def stage_c(self, h):
        s = self.s
        total = self.a[h, s.me[1]].astype(F32)
        for i in range(1, s.ny):
            self.copy_b(h, i, False).wait_recv()
            total = total + self.b[h, i - 1].astype(F32)
        self.a[h, s.me[1]] = total.astype(BF)
        for i in range(1, s.nx):
            self.copy_c(h, i, True).start()

    def stage_e(self, h):
        s = self.s
        mine = pl.ds(s.me[3] * self.half, self.half)
        total = self.a[h, s.me[1], mine].astype(F32)
        for i in range(1, s.nx):
            self.copy_c(h, i, False).wait_recv()
            total = total + self.c[h, s.px(i)].astype(F32)
        self.out[h, s.me[0], mine] = total.astype(BF)
        for i in range(1, s.nz):
            self.copy_e(h, i, True).start()

    def stage_f(self, h):
        s = self.s
        for i in range(1, s.nz):
            self.copy_e(h, i, False).wait_recv()
        for i in range(1, s.nx):
            self.copy_f(h, i, True).start()

    def stages(self):
        return (self.stage_b, self.stage_c, self.stage_e, self.stage_f)

    def finish(self, h):
        s = self.s
        self.copy_a(h).wait_send()
        for i in range(1, s.ny):
            self.copy_b(h, i, True).wait_send()
        for i in range(1, s.nx):
            self.copy_c(h, i, True).wait_send()
            self.copy_f(h, i, False).wait_recv()
            self.copy_f(h, i, True).wait_send()
        for i in range(1, s.nz):
            self.copy_e(h, i, True).wait_send()

    @staticmethod
    def sems(heads, ny, nx, nz):
        out = [pltpu.SemaphoreType.DMA((heads,))] * 2
        for n in (ny - 1, nx, nz, nx):
            out += [pltpu.SemaphoreType.DMA((heads, n))] * 2
        return out


def bwd_kernel(counts, *refs):
    refs = list(refs)

    def take(n):
        out = refs[:n]
        del refs[:n]
        return out

    prefix_ref, proj_ref, conv_ref, do_ref, o_ref, lse_ref, normed_ref = take(7)
    part_refs = take(len(counts))
    gp_ref, sum_ref, own_ref = take(3)
    wide, qs, ks, vs, dos, delta, dq, dk, dv, gk, gv, gwide, gp_s, gpt, own_part = take(15)
    send, recv, gsend, grecv = take(4)
    bufs = take(5)
    sems = take(10)
    own_bufs = take(3)
    own_sems = take(10)
    heads, length, _ = qs.shape
    width = gwide.shape[1]
    blocks = dos.shape[1]
    rows = length//blocks
    prefix = prefix_ref[0]
    parts = []
    first = 0
    for ref, count in zip(part_refs, counts):
        parts.append((ref, first, count))
        first += count
    sums = Sums(parts, sum_ref, bufs, sems, blocks)
    own = OwnSums(sums, own_part, own_ref, own_bufs, own_sems)
    z, y, c, x = sums.me
    greet(sums.peers())
    sums.start()

    def block_copy(h, i, at):
        return remote(do_ref.at[i * heads + h], dos.at[h, at], send.at[h, i], recv.at[h, at], (i, 2 * y + c, x))

    for h in range(heads):
        for i in range(1, blocks):
            block_copy(h, (z + i) % blocks, z).start()
        dos[h, z] = do_ref[z * heads + h]

    def gp_copy(h, i, at):
        return remote(gpt.at[h, i], gp_ref.at[at * heads + h], gsend.at[h, i], grecv.at[h, at], (i, 2 * y + c, x))

    ahead = min(2, sums.chunks)
    for k in range(ahead):
        sums.stage_b(k)
    convolve(proj_ref, conv_ref, wide, (qs, ks, vs))

    def head(h, _):
        for i in range(1, blocks):
            there = (z + i) % blocks
            block_copy(h, there, there).wait_recv()
        for i in range(blocks):
            prod = dos[h, i].astype(F32) * o_ref[h, i].astype(F32)
            delta[i] = jnp.broadcast_to(jnp.sum(prod, axis=0, keepdims=True), (8, rows))
        dq[...] = jnp.zeros(dq.shape, F32)
        def kblock(j, _):
            t = h*blocks + j
            @pl.when(t + ahead < sums.chunks)
            def _():
                sums.stage_b(t + ahead)
            @pl.when((t > 0) & (t != 3))
            def _():
                sums.step(jnp.where(t < 3, t - 1, t - 2))
            @pl.when((h > 0) & (j > 0))
            def _():
                gp_copy(h - 1, (z + j) % blocks, z).start()
            for n, stage in enumerate(own.stages()):
                @pl.when((h > 0) & (j == n))
                def _():
                    stage(h - 1)
            kat = pl.ds(pl.multiple_of(j*rows, rows), rows)
            k = ks[h, kat]; v = vs[h, kat]
            dk[...] = jnp.zeros(dk.shape, F32)
            dv[...] = jnp.zeros(dv.shape, F32)
            def step(i, masked):
                qat = pl.ds(pl.multiple_of(i*rows, rows), rows)
                q = qs[h, qat]; do = dos[h, i]
                s = nt(k, q)
                p = jnp.exp(s - lse_ref[h, 0:1, qat])
                if masked:
                    p = jnp.where(mask_t(i, j, rows, prefix), p, 0.0)
                dv[...] += nt(p.astype(BF), do)
                dp = jnp.dot(v, do, preferred_element_type=F32)
                ds = (p*(dp - delta[i, 0:1])).astype(BF)
                dk[...] += jnp.dot(ds, q, preferred_element_type=F32)
                dq[qat] += tn(ds, k)
                return 0
            lax.fori_loop(j+1, blocks, lambda i, _: step(i, False), 0)
            lax.fori_loop(jnp.where(j < blocks//2, 0, j), j+1, lambda i, _: step(i, True), 0)
            gk[kat] = dk[...].astype(BF)
            gv[kat] = dv[...].astype(BF)
            return 0
        lax.fori_loop(0, blocks, kblock, 0)
        def fill(c, _):
            at = pl.ds(pl.multiple_of(c*rows, rows), rows)
            gq = (dq[at]*(HEAD_DIM**-0.5)).astype(BF)
            gwide[at] = jnp.concatenate([gq, gk[at], gv[at]], axis=1).astype(F32)
            return 0
        lax.fori_loop(0, blocks, fill, 0)
        taps = conv_ref[h]
        def out(i, total):
            base = pl.multiple_of(i*rows, rows)
            g = gwide[pl.ds(base, rows+8)]
            w = wide[h, pl.ds(base, rows+8)]
            g0 = g[:rows]
            gp = taps[0:1]*g0 + taps[1:2]*g[1:rows+1] + taps[2:3]*g[2:rows+2]
            gp_s[pl.ds(base, rows)] = gp.astype(BF)
            gpt[h, i] = jnp.transpose(gp).astype(BF)
            add = [jnp.sum(g0*w[8-t:8-t+rows], axis=0, keepdims=True) for t in range(3)]
            return tuple(a+b for a, b in zip(total, add))
        total = lax.fori_loop(0, blocks, out, tuple(jnp.zeros((1, width), F32) for _ in range(3)))
        gp_ref[z * heads + h] = gpt[h, z]
        grad = jnp.dot(normed_ref[...], gp_s[...], preferred_element_type=F32).astype(BF)
        shape = own_part.shape[1:]
        mine = grad.shape[0] // (8 * shape[0] * shape[1])
        own_part[h, :, :, 0:mine] = grad.reshape(shape[0], shape[1], mine, 8, width)
        extra = jnp.concatenate(list(total) + [jnp.zeros((5, width), F32)], axis=0).astype(BF)
        own_part[h, :, :, mine] = jnp.broadcast_to(extra, shape[:2] + (8, width))
        for spare in range(mine + 1, shape[2]):
            own_part[h, :, :, spare] = jnp.zeros(shape[:2] + (8, width), BF)
        own.copy_a(h).start()
        return 0
    gwide[length:length+8] = jnp.zeros((8, width), F32)
    lax.fori_loop(0, heads, head, 0)
    steps = heads*blocks
    turns = steps - 2
    def rest(t, _):
        sums.stage_b(t)
        return 0
    lax.fori_loop(steps + ahead, sums.chunks, rest, 0)
    for n, stage in enumerate(own.stages()):
        sums.step(turns + n)
        if 0 < n < blocks:
            gp_copy(heads - 1, (z + n) % blocks, z).start()
        stage(heads - 1)
    count = len(own.stages())
    for n in range(count, blocks):
        gp_copy(heads - 1, (z + n) % blocks, z).start()
    def tail(t, _):
        sums.step(t)
        return 0
    lax.fori_loop(turns + count, max(sums.chunks + sums.LAGS[-1], turns + count), tail, 0)
    sums.finish()
    def done(h, _):
        own.finish(h)
        for i in range(1, blocks):
            there = (z + i) % blocks
            block_copy(h, there, z).wait_send()
            gp_copy(h, there, there).wait_recv()
            gp_copy(h, there, z).wait_send()
        return 0
    lax.fori_loop(0, heads, done, 0)

def attention_bwd(prefix, proj, conv, do, o, lse, normed, parts, shape):
    length = proj.shape[0]
    heads, blocks = o.shape[:2]
    width = 3 * HEAD_DIM
    rows = length // blocks
    counts = tuple(part.shape[2] for part in parts)
    ny, _, _, units = parts[0].shape[:4]
    unit = parts[0].shape[4:]
    nx = shape["replica"]
    chunks = sum(counts)
    half = units // nx
    own_units = -(-(normed.shape[0] // (16 * ny) + 1) // nx) * nx
    own_unit = (8, width)
    vm = pl.BlockSpec(memory_space=pltpu.VMEM)
    dma = pltpu.SemaphoreType.DMA
    per = pltpu.VMEM((heads, length, HEAD_DIM), BF)
    return pl.pallas_call(
        functools.partial(bwd_kernel, counts),
        out_shape=(
            jax.ShapeDtypeStruct((heads * blocks, width, rows), BF),
            jax.ShapeDtypeStruct((chunks, units) + unit, BF),
            jax.ShapeDtypeStruct((heads, blocks, own_units) + own_unit, BF),
        ),
        in_specs=[pl.BlockSpec(memory_space=pltpu.SMEM)] + [vm]*(6 + len(parts)),
        out_specs=(vm, vm, vm),
        scratch_shapes=[pltpu.VMEM((heads, 8+length, width), F32), per, per, per, pltpu.VMEM(o.shape, BF), pltpu.VMEM((blocks, 8, rows), F32),
            pltpu.VMEM((length, HEAD_DIM), F32), pltpu.VMEM((rows, HEAD_DIM), F32), pltpu.VMEM((rows, HEAD_DIM), F32),
            pltpu.VMEM((length, HEAD_DIM), BF), pltpu.VMEM((length, HEAD_DIM), BF),
            pltpu.VMEM((length+8, width), F32), pltpu.VMEM((length, width), BF), pltpu.VMEM((heads, blocks, width, rows), BF),
            pltpu.VMEM((heads, ny, 2, own_units) + own_unit, BF)]
            + [dma((heads, blocks))] * 4
            + [pltpu.VMEM((chunks, ny, units) + unit, BF), pltpu.VMEM((chunks, ny - 1, units) + unit, BF),
            pltpu.VMEM((chunks, nx, half) + unit, BF), pltpu.VMEM((chunks, half // 2) + unit, BF), pltpu.VMEM((chunks, half // 4) + unit, BF)]
            + Sums.sems(chunks, ny, nx)
            + [pltpu.VMEM((heads, ny, own_units) + own_unit, BF), pltpu.VMEM((heads, ny - 1, own_units) + own_unit, BF),
            pltpu.VMEM((heads, nx, own_units // nx) + own_unit, BF)]
            + OwnSums.sems(heads, ny, nx, blocks),
        compiler_params=pltpu.CompilerParams(vmem_limit_bytes=67043328, collective_id=3, has_side_effects=True),
        cost_estimate=pl.CostEstimate(flops=10*heads*length*length*HEAD_DIM, bytes_accessed=length*width*4, transcendentals=heads*length*length),
        name="attention_bwd",
    )(prefix, proj, conv, do, o, lse, normed, *parts)


def finish_kernel(
    gp_ref, sum_ref, own_ref, wq_ref, tok_ref, gh_ref, gone_ref, w_qkv_ref, w_up_ref, gains_ref,
    gin_out, qkv_out, out_out, up_out, down_out, conv_ref, ggain_ref,
    wq, tok, gh, w_qkv, w_up, gin, qkv, out, up, down, isem, osem,
):
    depth = w_qkv.shape[0]
    width = tok.shape[1]
    heads, blocks = own_ref.shape[:2]
    mine = depth // 8
    loads = [
        pltpu.make_async_copy(src, dst, isem.at[i])
        for i, (src, dst) in enumerate(
            ((wq_ref, wq), (tok_ref, tok), (gh_ref, gh), (w_up_ref, w_up), (w_qkv_ref, w_qkv))
        )
    ]
    for load in loads:
        load.start()
    stores = [
        pltpu.make_async_copy(src, dst, osem.at[i])
        for i, (src, dst) in enumerate(
            ((down, down_out), (out, out_out), (up, up_out), (qkv, qkv_out), (gin, gin_out))
        )
    ]
    ups = w_up.shape[1] // width
    downs = down.shape[0] // depth

    def rows_of(first, count):
        return sum_ref[first * mine : (first + count) * mine].reshape(count * depth, width).astype(F32)

    for i in range(downs):
        down[i * depth : (i + 1) * depth] = rows_of(ups + i, 1)
    stores[0].start()
    out[...] = rows_of(ups + downs, 1)
    stores[1].start()
    loads[3].wait()
    total = jnp.zeros((depth, 1), F32)
    for i in range(ups):
        at = slice(i * width, (i + 1) * width)
        grad = rows_of(i, 1)
        up[:, at] = grad
        total = total + jnp.sum(grad * w_up[:, at].astype(F32), axis=1, keepdims=True)
    stores[2].start()
    grads = [own_ref[h, j, :mine].reshape(depth, 3 * HEAD_DIM) for j in range(blocks) for h in range(heads)]
    taps = [own_ref[h, j, mine] for j in range(blocks) for h in range(heads)]

    def merge(pieces, p):
        return jnp.concatenate([piece[:, p * HEAD_DIM : (p + 1) * HEAD_DIM] for piece in pieces], axis=1)

    loads[4].wait()
    attn = jnp.zeros((depth, 1), F32)
    for p in range(3):
        at = slice(p * width, (p + 1) * width)
        grad = merge(grads, p).astype(F32)
        qkv[:, at] = grad
        attn = attn + jnp.sum(grad * w_qkv[:, at].astype(F32), axis=1, keepdims=True)
        conv_ref[:, at] = merge(taps, p).astype(F32)
    stores[3].start()
    gains = gains_ref[...]
    ggain_ref[...] = jnp.concatenate([attn / gains[:, 0:1], total / gains[:, 1:2]], axis=1)
    for load in loads[:3]:
        load.wait()
    e1 = jnp.zeros(gh.shape, F32)
    for j in range(blocks):
        e1 = e1 + lax.dot_general(gp_ref[j], wq[j], (((0,), (1,)), ((), ())), preferred_element_type=F32)
    x = tok[...].astype(F32)
    scale = lax.rsqrt(jnp.mean(x * x, axis=-1, keepdims=True) + 1e-06)
    weighted = e1 * gone_ref[...]
    back = scale * weighted - x * scale**3 * jnp.mean(weighted * x, axis=-1, keepdims=True)
    gin[...] = (gh[...] + back).astype(BF)
    stores[4].start()
    for store in stores:
        store.wait()


def finish(gp, sums, own_sums, wq, tok, gh, gone, w_qkv, w_up, gains, ff):
    depth, width = w_qkv.shape[0], tok.shape[1]
    vm = pl.BlockSpec(memory_space=pltpu.VMEM)
    hbm = pl.BlockSpec(memory_space=pl.ANY)
    dma = pltpu.SemaphoreType.DMA
    outs = [
        (tok.shape, BF),
        (w_qkv.shape, F32),
        ((depth, width), F32),
        (w_up.shape, F32),
        ((ff, width), F32),
    ]
    flat = [((8, w_qkv.shape[1]), F32), ((depth, 2), F32)]
    kept = [(a.shape, a.dtype) for a in (wq, tok, gh, w_qkv, w_up)]
    return pl.pallas_call(
        finish_kernel,
        out_shape=[jax.ShapeDtypeStruct(*o) for o in outs + flat],
        in_specs=[vm] * 3 + [hbm] * 3 + [vm] + [hbm] * 2 + [vm],
        out_specs=[hbm] * 5 + [vm] * 2,
        scratch_shapes=[pltpu.VMEM(*o) for o in kept + outs] + [dma((5,)), dma((5,))],
        compiler_params=pltpu.CompilerParams(vmem_limit_bytes=60 * 1024 * 1024),
        name="finish",
    )(gp, sums, own_sums, wq, tok, gh, gone, w_qkv, w_up, gains)


def rms_scale(values):
    return lax.rsqrt(jnp.mean(values * values, axis=-1, keepdims=True) + 1e-06)


def norm_back(values, scale_rows, gain, upstream):
    weighted = upstream * gain
    grad_values = scale_rows * weighted - values * scale_rows**3 * jnp.mean(
        weighted * values, axis=-1, keepdims=True
    )
    return grad_values


def dot(a, b):
    return jnp.dot(a, b, preferred_element_type=F32)


def per_device(
    tokens, prefix_len, w_qkv, w_out, w_up, w_down, conv_w, gain_attn, gain_ffn, cotangent
):
    blocks = lax.axis_size("seq")
    me = lax.axis_index("seq")
    rows, width = tokens.shape[1:]
    own = HEADS // blocks * HEAD_DIM
    depth = w_qkv.shape[0]

    shards, copies = lax.axis_size("shard"), lax.axis_size("replica")
    heads = HEADS // blocks
    columns = w_qkv.reshape(depth, 3, blocks, heads, HEAD_DIM).transpose(2, 0, 3, 1, 4)
    gains = jnp.pad(jnp.stack([gain_attn, gain_ffn]), ((0, 0), (0, conv_w.shape[1] - depth)))
    small = jnp.pad(jnp.concatenate([gains, conv_w]), ((0, 3), (0, 0)))
    normed_all, projected, small, full_qkv, full_out, full_up = gather_all(
        tokens[0], small, columns.reshape(blocks, depth, 3 * own), w_out, w_up, blocks, shards
    )
    full_qkv = full_qkv.reshape(blocks, width, 3 * own)
    full_out = full_out.reshape(width, width)
    full_up = full_up.reshape(width, -1)
    full_gone = small[:, 0, 0, :depth].reshape(width).astype(F32)
    full_gtwo = small[:, 0, 1, :depth].reshape(width).astype(F32)
    full_conv = small[:, 0, 2:5].transpose(1, 0, 2)
    own_conv = lax.dynamic_index_in_dim(full_conv.reshape(3, 3, blocks, heads, HEAD_DIM), me, 2, False)
    own_conv = own_conv.transpose(2, 0, 1, 3).reshape(heads, 3, 3 * HEAD_DIM).astype(F32)
    attended_own, logsum, attended, full_down = attention_fwd(
        prefix_len, projected, own_conv, w_down.reshape(-1, depth, width), blocks, shards
    )
    full_down = full_down.reshape(-1, width)
    attended = attended.reshape(width, rows)

    inputs = tokens[0].astype(F32)
    hidden = inputs + tn(attended, full_out)
    scale_two = rms_scale(hidden)
    normed_two_b = (hidden * scale_two * full_gtwo).astype(BF)
    positive = jnp.maximum(dot(normed_two_b, full_up), 0.0)
    active_b = (positive * positive).astype(BF)
    output = hidden + dot(active_b, full_down)

    incoming = cotangent[0]
    grad_upper_b = (dot(incoming, full_down.T) * 2.0 * positive).astype(BF)
    grad_normed_two = dot(grad_upper_b, full_up.T)
    grad_hidden = incoming.astype(F32) + norm_back(hidden, scale_two, full_gtwo, grad_normed_two)
    grad_hidden_b = grad_hidden.astype(BF)
    grad_attended = nt(full_out, grad_hidden_b).astype(BF)

    mine = depth // 8

    def cut(grad):
        return grad.astype(BF).reshape(shards // 2, 2, -1, mine, 8, width)

    parts = [
        cut(dot(normed_two_b.T, grad_upper_b[:, i * width : (i + 1) * width]))
        for i in range(grad_upper_b.shape[1] // width)
    ]
    parts += [cut(dot(active_b.T, incoming)), cut(dot(attended, grad_hidden_b))]
    pieces = sum(part.shape[2] for part in parts)
    if mine % (copies * blocks):
        units = -(-pieces * mine // (copies * blocks)) * copies * blocks
        joined = [part.reshape(shards // 2, 2, -1, 8, width) for part in parts]
        joined.append(jnp.zeros((shards // 2, 2, units - pieces * mine, 8, width), BF))
        joined = jnp.concatenate(joined, axis=2)
        parts = [joined.reshape(shards // 2, 2, -1, copies * blocks, 8, width)]

    grad_projected, sums, own_sums = attention_bwd(
        prefix_len, projected, own_conv, grad_attended.reshape(HEADS, HEAD_DIM, rows),
        attended_own, logsum, normed_all, parts, {"replica": copies},
    )
    grad_projected = grad_projected.reshape(blocks, 3 * own, rows)
    sums = sums.reshape(-1, 8, width)
    gains = jnp.stack([gain_attn, gain_ffn], axis=1).astype(F32)
    grad_input, total_qkv, total_out, total_up, total_down, total_conv, grad_gains = finish(
        grad_projected, sums, own_sums, full_qkv, tokens[0], grad_hidden, full_gone[None],
        w_qkv, w_up, gains, w_down.shape[0],
    )
    at = lax.axis_index("shard")
    return (
        output[None].astype(BF),
        grad_input[None],
        total_qkv,
        total_out,
        total_up,
        total_down,
        lax.dynamic_slice_in_dim(total_conv[:3], at * conv_w.shape[1], conv_w.shape[1], 1),
        grad_gains[:, 0],
        grad_gains[:, 1],
    )


def solution(mesh):
    placed = (
        P(("shard", "replica"), "seq", None),
        P(("shard", "replica")),
        P("shard", None),
        P("shard", None),
        P("shard", None),
        P("shard", None),
        P(None, "shard"),
        P("shard"),
        P("shard"),
        P(("shard", "replica"), "seq", None),
    )
    return jax.shard_map(
        per_device,
        mesh=mesh,
        in_specs=placed,
        out_specs=(
            P(("shard", "replica"), "seq", None),
            P(("shard", "replica"), "seq", None),
            P("shard", None),
            P("shard", None),
            P("shard", None),
            P("shard", None),
            P(None, "shard"),
            P("shard"),
            P("shard"),
        ),
        check_vma=False,
    )
```

```python
import functools

import jax
import jax.numpy as jnp
from jax import lax
from jax.experimental import pallas as pl
from jax.experimental.pallas import tpu as pltpu
from jax.sharding import PartitionSpec as P

HEADS = 12
HEAD_DIM=64
NEG=-1e30
F32=jnp.float32
BF=jnp.bfloat16

def nt(a,b):
    return lax.dot_general(a,b,(((1,),(1,)),((),())),preferred_element_type=F32)
def tn(a,b):
    return lax.dot_general(a,b,(((0,),(0,)),((),())),preferred_element_type=F32)

def convolve(proj_ref, conv_ref, wide, parts):
    length = proj_ref.shape[0]
    heads, _, width = wide.shape
    rows = min(512, length)
    for h in range(heads):
        wide[h, 0:8] = jnp.zeros((8, width), F32)
        for c in range(length//rows):
            wide[h, 8+c*rows:8+(c+1)*rows] = proj_ref[c*rows:(c+1)*rows, h*width:(h+1)*width].astype(F32)
    def body(c, _):
        base = pl.multiple_of(c*rows, rows)
        for h in range(heads):
            x = wide[h, pl.ds(base, rows+8)]
            taps = conv_ref[h]
            mixed = taps[0:1]*x[8:] + taps[1:2]*x[7:7+rows] + taps[2:3]*x[6:6+rows]
            for p, ref in enumerate(parts):
                piece = mixed[:, p*HEAD_DIM:(p+1)*HEAD_DIM].astype(BF)
                if p == 0:
                    piece = piece * jnp.asarray(HEAD_DIM**-0.5, BF)
                ref[h, pl.ds(base, rows)] = piece
        return 0
    lax.fori_loop(0, length//rows, body, 0)

def mask_t(i, j, rows, prefix):
    kpos = j*rows + lax.broadcasted_iota(jnp.int32, (rows, 1), 0)
    qpos = i*rows + lax.broadcasted_iota(jnp.int32, (1, rows), 1)
    return (kpos <= qpos) | ((kpos < prefix) & (qpos < prefix))

def mask_n(i, j, rows, prefix):
    qpos = i*rows + lax.broadcasted_iota(jnp.int32, (rows, 1), 0)
    kpos = j*rows + lax.broadcasted_iota(jnp.int32, (1, rows), 1)
    return (kpos <= qpos) | ((kpos < prefix) & (qpos < prefix))

MESH = pl.DeviceIdType.MESH


def remote(src, dst, send, recv, peer):
    return pltpu.make_async_remote_copy(
        src_ref=src, dst_ref=dst, send_sem=send, recv_sem=recv, device_id=peer, device_id_type=MESH
    )


def greet(peers):
    barrier = pltpu.get_barrier_semaphore()
    for peer in peers:
        pl.semaphore_signal(barrier, inc=1, device_id=peer, device_id_type=MESH)
    pl.semaphore_wait(barrier, len(peers))


def split_shard():
    s = lax.axis_index("shard")
    return lax.axis_index("seq"), s // 2, s % 2, lax.axis_index("replica")


class Gather:
    def __init__(self, src, dst, sems, major=False):
        self.src, self.dst, self.major = src, dst, major
        self.sy, self.ry, self.sk, self.rk, self.local = sems
        self.ny = dst.shape[1 if major else 0] // 2
        self.chunks = dst.shape[0 if major else 1]
        self.z, self.y, self.c, self.x = split_shard()
        self.core = (self.z, 2 * self.y + 1 - self.c, self.x)

    def py(self, i):
        return (self.y + i) % self.ny

    def dy(self, i):
        return (self.z, 2 * self.py(i) + self.c, self.x)

    def peers(self):
        return [self.core] + [self.dy(i) for i in range(1, self.ny)]

    def slot(self, p, core, j):
        shard = 2 * p + core
        return self.dst.at[j, shard] if self.major else self.dst.at[shard, j]

    def own(self):
        shard = 2 * self.y + self.c
        dst = self.dst.at[:, shard] if self.major else self.dst.at[shard]
        return pltpu.make_async_copy(self.src, dst, self.local.at[0])

    def over_y(self, j, i):
        slot = self.slot(self.y, self.c, j)
        return remote(self.src.at[j], slot, self.sy.at[j, self.py(i)], self.ry.at[j, self.y], self.dy(i))

    def to_core(self, j):
        slot = self.slot(self.y, self.c, j)
        return remote(self.src.at[j], slot, self.sk.at[j, self.y], self.rk.at[j, self.y], self.core)

    def pass_on(self, j, i):
        ref = self.slot(self.py(i), self.c, j)
        return remote(ref, ref, self.sk.at[j, self.py(i)], self.rk.at[j, self.py(i)], self.core)

    def send(self, j):
        for i in range(1, self.ny):
            self.over_y(j, i).start()
        self.to_core(j).start()

    def start(self):
        for j in range(self.chunks):
            self.send(j)
        self.own().start()

    def relay(self, j):
        for i in range(1, self.ny):
            ref = self.slot(self.py(i), self.c, j)
            remote(ref, ref, self.sy.at[j, self.py(i)], self.ry.at[j, self.py(i)], self.dy(i)).wait_recv()
            self.pass_on(j, i).start()

    def arrive(self, j):
        for i in range(self.ny):
            ref = self.slot(self.py(i), 1 - self.c, j)
            remote(ref, ref, self.sk.at[j, self.py(i)], self.rk.at[j, self.py(i)], self.core).wait_recv()

    def sent(self, j):
        self.to_core(j).wait_send()
        for i in range(1, self.ny):
            self.over_y(j, i).wait_send()
            self.pass_on(j, i).wait_send()

    def finish(self):
        self.own().wait()
        for j in range(self.chunks):
            self.arrive(j)
            self.sent(j)

    @staticmethod
    def sems(shards, chunks):
        return [pltpu.SemaphoreType.DMA((chunks, shards // 2))] * 4 + [pltpu.SemaphoreType.DMA((1,))]


def gather_kernel(
    tok_ref, small_ref, qkv_ref, out_ref, up_ref,
    normed_ref, proj_ref, small_all, qkv_all, out_all, up_all,
    toks, weight_s, wsem, sl, sr, rl, rr, *sems,
):
    blocks, rows, width = toks.shape
    _, shards, depth, columns = qkv_all.shape
    small, qkv, out, up = (
        Gather(src, dst, sems[5 * i : 5 * i + 5], major=i == 1)
        for i, (src, dst) in enumerate(
            ((small_ref, small_all), (qkv_ref, qkv_all), (out_ref, out_all), (up_ref, up_all))
        )
    )
    z, y, c, x = split_shard()
    shard = 2 * y + c
    left, right = (z - 1, shard, x), (z + 1, shard, x)
    has_left, has_right = z > 0, z < blocks - 1
    greet(small.peers() + [((z + i) % blocks, shard, x) for i in range(1, blocks)])

    def go_left(b, src):
        return remote(src, toks.at[b], sl.at[b], rr.at[b], left)

    def go_right(b, src):
        return remote(src, toks.at[b], sr.at[b], rl.at[b], right)

    small.start()
    qkv.send(z)
    qkv.own().start()

    @pl.when(has_left)
    def _():
        go_left(z, tok_ref).start()

    @pl.when(has_right)
    def _():
        go_right(z, tok_ref).start()

    out.start()
    up.start()
    for i in range(1, blocks):
        qkv.send((z + i) % blocks)
    small.relay(0)
    qkv.relay(z)
    small.finish()
    qkv.own().wait()
    qkv.arrive(z)
    gain = jnp.concatenate([small_all[s, 0, 0:1, :depth] for s in range(shards)], axis=1).astype(F32)
    fetch = pltpu.make_async_copy(qkv_all.at[z], weight_s, wsem.at[0])
    fetch.start()
    fetch.wait()
    weight = weight_s[...].reshape(shards * depth, columns)

    def project(b, values):
        at = pl.ds(pl.multiple_of(b * rows, rows), rows)
        values = values.astype(F32)
        scale = lax.rsqrt(jnp.mean(values * values, axis=-1, keepdims=True) + 1e-06)
        normed = values * scale * gain
        proj_ref[at] = jnp.dot(normed.astype(BF), weight, preferred_element_type=F32).astype(BF)
        normed_ref[:, at] = jnp.transpose(normed).astype(BF)

    project(z, tok_ref[...])
    for d in range(1, blocks):
        before, after = z - d, z + d

        @pl.when(before >= 0)
        def _():
            go_right(before, toks.at[before]).wait_recv()

            @pl.when(has_right)
            def _():
                go_right(before, toks.at[before]).start()

        @pl.when(after < blocks)
        def _():
            go_left(after, toks.at[after]).wait_recv()

            @pl.when(has_left)
            def _():
                go_left(after, toks.at[after]).start()

        @pl.when(before >= 0)
        def _():
            project(before, toks[before])

        @pl.when(after < blocks)
        def _():
            project(after, toks[after])

        if d == 1:
            out.relay(0)
        last = up.chunks * d // (blocks - 1)
        for j in range(up.chunks * (d - 1) // (blocks - 1), last):
            up.relay(j)

    for i in range(1, blocks):
        qkv.relay((z + i) % blocks)
    out.finish()
    up.finish()
    for i in range(1, blocks):
        qkv.arrive((z + i) % blocks)
    for j in range(blocks):
        qkv.sent(j)

    def sent(b, _):
        @pl.when((b <= z) & has_right)
        def _():
            go_right(b, toks.at[b]).wait_send()

        @pl.when((b >= z) & has_left)
        def _():
            go_left(b, toks.at[b]).wait_send()

        return 0

    lax.fori_loop(0, blocks, sent, 0)


def gather_all(tokens, small, qkv, out, up, blocks, shards):
    rows, width = tokens.shape
    vm = pl.BlockSpec(memory_space=pltpu.VMEM)
    hbm = pl.BlockSpec(memory_space=pl.ANY)
    cut = 4
    arrays = [
        small[None],
        qkv,
        out[None],
        up.reshape(cut, up.shape[0] // cut, up.shape[1]),
    ]
    dma = pltpu.SemaphoreType.DMA
    sems = [dma((blocks,))] * 4
    for array in arrays:
        sems += Gather.sems(shards, array.shape[0])
    return pl.pallas_call(
        gather_kernel,
        out_shape=[
            jax.ShapeDtypeStruct((width, blocks * rows), BF),
            jax.ShapeDtypeStruct((blocks * rows, qkv.shape[2]), BF),
        ]
        + [
            jax.ShapeDtypeStruct(
                (blocks, shards) + array.shape[1:] if i == 1 else (shards,) + array.shape, BF
            )
            for i, array in enumerate(arrays)
        ],
        in_specs=[vm] * 5,
        out_specs=[vm] * 3 + [hbm] * 3,
        scratch_shapes=[pltpu.VMEM((blocks, rows, width), BF), pltpu.VMEM((shards,) + qkv.shape[1:], BF), dma((1,))]
        + sems,
        compiler_params=pltpu.CompilerParams(
            vmem_limit_bytes=60 * 1024 * 1024, collective_id=4, has_side_effects=True
        ),
        name="gather_all",
    )(tokens, *arrays)


def fwd_kernel(prefix_ref, proj_ref, conv_ref, down_ref, own_ref, lse_ref, rows_ref, down_all, wide, qs, ks, vs, m_s, l_s, acc_s, o_s, r_s, send, recv, *sems):
    heads = qs.shape[0]
    length = proj_ref.shape[0]
    blocks = own_ref.shape[1]
    rows = length // blocks
    prefix = prefix_ref[0]
    z, s_at, x = lax.axis_index("seq"), lax.axis_index("shard"), lax.axis_index("replica")

    def block_copy(h, i, at):
        return remote(o_s.at[h, i], r_s.at[at * heads + h], send.at[h, i], recv.at[h, at], (i, s_at, x))

    down = Gather(down_ref, down_all, sems)
    greet([((z + i) % blocks, s_at, x) for i in range(1, blocks)] + down.peers())
    down.start()
    convolve(proj_ref, conv_ref, wide, (qs, ks, vs))
    def head(h, _):
        for j in range(down.chunks):
            @pl.when(h == 1 + (j + 1) // 2)
            def _():
                down.relay(j)
        def qblock(i, _):
            q = qs[h, pl.ds(pl.multiple_of(i*rows, rows), rows)]
            m_s[...] = jnp.full((1, rows), NEG, F32)
            l_s[...] = jnp.zeros((1, rows), F32)
            acc_s[...] = jnp.zeros((HEAD_DIM, rows), F32)
            def step(j, masked):
                at = pl.ds(pl.multiple_of(j*rows, rows), rows)
                s = nt(ks[h, at], q)
                if masked:
                    s = jnp.where(mask_t(i, j, rows, prefix), s, NEG)
                m_old = m_s[...]
                m_new = jnp.maximum(m_old, jnp.max(s, axis=0, keepdims=True))
                p = jnp.exp(s - m_new)
                a = jnp.exp(m_old - m_new)
                m_s[...] = m_new
                l_s[...] = a*l_s[...] + jnp.sum(p, axis=0, keepdims=True)
                acc_s[...] = a*acc_s[...] + tn(vs[h, at], p.astype(BF))
                return 0
            lax.fori_loop(0, i, lambda j, _: step(j, False), 0)
            lax.fori_loop(i, jnp.maximum(i+1, blocks//2), lambda j, _: step(j, True), 0)
            l = l_s[...]
            done = (acc_s[...]/l).astype(BF)
            o_s[h, i] = done
            own_ref[h, i] = done
            @pl.when(i != z)
            def _():
                block_copy(h, i, z).start()
            lse = m_s[...] + jnp.log(l)
            lse_ref[h, :, pl.ds(pl.multiple_of(i*rows, rows), rows)] = jnp.broadcast_to(lse, (8, rows))
            return 0
        lax.fori_loop(0, blocks, qblock, 0)
        r_s[z * heads + h] = o_s[h, z]
        return 0
    lax.fori_loop(0, heads, head, 0)
    for j in range(down.chunks):
        if 1 + (j + 1) // 2 >= heads:
            down.relay(j)
    down.finish()
    def finish(h, _):
        for i in range(1, blocks):
            there = (z + i) % blocks
            block_copy(h, there, there).wait_recv()
            block_copy(h, there, z).wait_send()
        return 0
    lax.fori_loop(0, heads, finish, 0)
    rows_ref[...] = r_s[...]

def attention_fwd(prefix, proj, conv, down, blocks, shards):
    length, width = proj.shape
    heads = width//(3*HEAD_DIM)
    rows = length // blocks
    vm = pl.BlockSpec(memory_space=pltpu.VMEM)
    own = (heads, blocks, HEAD_DIM, rows)
    every = (heads * blocks, HEAD_DIM, rows)
    return pl.pallas_call(
        fwd_kernel,
        out_shape=(jax.ShapeDtypeStruct(own, BF), jax.ShapeDtypeStruct((heads, 8, length), F32), jax.ShapeDtypeStruct(every, BF),
            jax.ShapeDtypeStruct((shards,) + down.shape, BF)),
        in_specs=[pl.BlockSpec(memory_space=pltpu.SMEM), vm, vm, vm],
        out_specs=(vm, vm, vm, pl.BlockSpec(memory_space=pl.ANY)),
        scratch_shapes=[pltpu.VMEM((heads, 8+length, 3*HEAD_DIM), F32)] + [pltpu.VMEM((heads, length, HEAD_DIM), BF)]*3 + [
            pltpu.VMEM((1,rows),F32), pltpu.VMEM((1,rows),F32), pltpu.VMEM((HEAD_DIM,rows),F32), pltpu.VMEM(own,BF), pltpu.VMEM(every,BF),
            pltpu.SemaphoreType.DMA((heads, blocks)), pltpu.SemaphoreType.DMA((heads, blocks))] + Gather.sems(shards, down.shape[0]),
        compiler_params=pltpu.CompilerParams(vmem_limit_bytes=60*1024*1024, collective_id=2, has_side_effects=True),
        cost_estimate=pl.CostEstimate(flops=4*heads*length*length*HEAD_DIM, bytes_accessed=length*width*2, transcendentals=heads*length*length),
        name="attention_fwd",
    )(prefix, proj, conv, down)

class Sums:
    def __init__(self, parts, out_ref, bufs, sems, nz):
        self.parts, self.out = parts, out_ref
        self.a, self.b, self.c, self.near, self.far = bufs
        self.sa, self.ra, self.sb, self.rb, self.sc, self.rc, self.sz, self.rz, self.sf, self.rf = sems
        self.chunks, self.ny = self.a.shape[:2]
        self.nx = self.c.shape[1]
        self.nz = nz
        self.half = self.c.shape[2]
        self.piece = self.half // nz
        self.me = split_shard()
        z, y, c, x = self.me
        self.core = (z, 2 * y + 1 - c, x)
        self.low, self.high = z % 2, z // 2
        self.one = (z + 1 - 2 * self.low, 2 * y + c, x)
        self.two = (z + 2 - 4 * self.high, 2 * y + c, x)

    def py(self, i):
        return (self.me[1] + i) % self.ny

    def px(self, i):
        return (self.me[3] + i) % self.nx

    def pz(self, i):
        return (self.me[0] + i) % self.nz

    def dy(self, i):
        z, y, c, x = self.me
        return (z, 2 * self.py(i) + c, x)

    def dx(self, i):
        z, y, c, x = self.me
        return (z, 2 * y + c, self.px(i))

    def dz(self, i):
        z, y, c, x = self.me
        return (self.pz(i), 2 * y + c, x)

    def peers(self):
        out = [self.core] + [self.dy(i) for i in range(1, self.ny)]
        out += [self.dx(i) for i in range(1, self.nx)]
        return out + [self.dz(i) for i in range(1, self.nz)]

    def copy_a(self, k, src):
        return remote(src, self.a.at[k], self.sa.at[k], self.ra.at[k], self.core)

    def start(self):
        c = self.me[2]
        for ref, first, count in self.parts:
            for j in range(count):
                src = ref.at[:, 1 - c, j]
                self.copy_a(first + j, src).start()

    def copy_b(self, k, i, there):
        slot = self.ny - i - 1 if there else i - 1
        return remote(self.a.at[k, self.py(i)], self.b.at[k, slot], self.sb.at[k, i - 1], self.rb.at[k, slot], self.dy(i))

    def stage_b(self, k):
        c = self.me[2]
        self.copy_a(k, self.a.at[k]).wait_recv()
        for i in list(range(1, self.ny)) + [0]:
            p = self.py(i)
            for ref, first, count in self.parts:
                @pl.when((k >= first) & (k < first + count))
                def _():
                    j = jnp.clip(k - first, 0, count - 1)
                    self.a[k, p] = (self.a[k, p].astype(F32) + ref[p, c, j].astype(F32)).astype(BF)
            if i:
                self.copy_b(k, i, True).start()

    def copy_c(self, k, i, there):
        slot = self.me[3] if there else self.px(i)
        src = self.a.at[k, self.me[1], pl.ds(self.px(i) * self.half, self.half)]
        return remote(src, self.c.at[k, slot], self.sc.at[k, self.px(i)], self.rc.at[k, slot], self.dx(i))

    def stage_c(self, k):
        y = self.me[1]
        total = self.a[k, y].astype(F32)
        for i in range(1, self.ny):
            self.copy_b(k, i, False).wait_recv()
            total = total + self.b[k, i - 1].astype(F32)
        for i in range(1, self.ny):
            self.copy_b(k, i, True).wait_send()
        self.a[k, y] = total.astype(BF)
        for i in range(1, self.nx):
            self.copy_c(k, i, True).start()

    def pieces(self, low, high, count):
        return pl.ds(self.me[3] * self.half + (2 * low + high) * self.piece, count * self.piece)

    def copy_z(self, k, stage):
        if stage == 0:
            src, dst, peer = self.a.at[k, self.me[1], self.pieces(1 - self.low, 0, 2)], self.near.at[k], self.one
        elif stage == 1:
            src, dst, peer = self.a.at[k, self.me[1], self.pieces(self.low, 1 - self.high, 1)], self.far.at[k], self.two
        elif stage == 2:
            src = dst = self.out.at[k, self.pieces(self.low, self.high, 1)]
            peer = self.two
        else:
            src = dst = self.out.at[k, self.pieces(self.low, 0, 2)]
            peer = self.one
        return remote(src, dst, self.sz.at[k, stage], self.rz.at[k, stage], peer)

    def stage_d(self, k):
        z, y, c, x = self.me
        mine = pl.ds(x * self.half, self.half)
        total = self.a[k, y, mine].astype(F32)
        for i in range(1, self.nx):
            self.copy_c(k, i, False).wait_recv()
            total = total + self.c[k, self.px(i)].astype(F32)
        for i in range(1, self.nx):
            self.copy_c(k, i, True).wait_send()
        self.a[k, y, mine] = total.astype(BF)
        self.copy_z(k, 0).start()

    def stage_near(self, k):
        y = self.me[1]
        self.copy_z(k, 0).wait_recv()
        self.copy_z(k, 0).wait_send()
        mine = self.pieces(self.low, 0, 2)
        self.a[k, y, mine] = (self.a[k, y, mine].astype(F32) + self.near[k].astype(F32)).astype(BF)
        self.copy_z(k, 1).start()

    def stage_far(self, k):
        self.copy_z(k, 1).wait_recv()
        mine = self.pieces(self.low, self.high, 1)
        self.out[k, mine] = (self.a[k, self.me[1], mine].astype(F32) + self.far[k].astype(F32)).astype(BF)
        self.copy_z(k, 2).start()

    def stage_back(self, k):
        ref = self.out.at[k, self.pieces(self.low, 1 - self.high, 1)]
        remote(ref, ref, self.sz.at[k, 2], self.rz.at[k, 2], self.two).wait_recv()
        self.copy_z(k, 3).start()

    def copy_f(self, k, i, there):
        slot = self.me[3] if there else self.px(i)
        ref = self.out.at[k, pl.ds(slot * self.half, self.half)]
        return remote(ref, ref, self.sf.at[k, self.px(i)], self.rf.at[k, slot], self.dx(i))

    def stage_f(self, k):
        ref = self.out.at[k, self.pieces(1 - self.low, 0, 2)]
        remote(ref, ref, self.sz.at[k, 3], self.rz.at[k, 3], self.one).wait_recv()
        for i in range(1, self.nx):
            self.copy_f(k, i, True).start()

    LAGS = (0, 1, 2, 3, 4, 5)

    def step(self, t):
        stages = (self.stage_c, self.stage_d, self.stage_near, self.stage_far, self.stage_back, self.stage_f)
        for lag, stage in zip(self.LAGS, stages):
            @pl.when((t >= lag) & (t < self.chunks + lag))
            def _():
                stage(t - lag)

    def finish(self):
        def body(k, _):
            for i in range(1, self.nx):
                self.copy_f(k, i, False).wait_recv()
            self.copy_a(k, self.a.at[k]).wait_send()
            for i in range(1, self.nx):
                self.copy_f(k, i, True).wait_send()
            for stage in range(1, 4):
                self.copy_z(k, stage).wait_send()
            return 0

        lax.fori_loop(0, self.chunks, body, 0)

    @staticmethod
    def sems(chunks, ny, nx):
        out = [pltpu.SemaphoreType.DMA((chunks,))] * 2
        for n in (ny - 1, nx, 4, nx):
            out += [pltpu.SemaphoreType.DMA((chunks, n))] * 2
        return out


class OwnSums:
    def __init__(self, sums, part, out, bufs, sems):
        self.s, self.part, self.out = sums, part, out
        self.a, self.b, self.c = bufs
        self.sa, self.ra, self.sb, self.rb, self.sc, self.rc, self.se, self.re, self.sf, self.rf = sems
        self.half = self.c.shape[2]

    def copy_a(self, h):
        return remote(self.part.at[h, :, 1 - self.s.me[2]], self.a.at[h], self.sa.at[h], self.ra.at[h], self.s.core)

    def copy_b(self, h, i, there):
        s = self.s
        slot = s.ny - i - 1 if there else i - 1
        return remote(self.a.at[h, s.py(i)], self.b.at[h, slot], self.sb.at[h, i - 1], self.rb.at[h, slot], s.dy(i))

    def copy_c(self, h, i, there):
        s = self.s
        slot = s.me[3] if there else s.px(i)
        src = self.a.at[h, s.me[1], pl.ds(s.px(i) * self.half, self.half)]
        return remote(src, self.c.at[h, slot], self.sc.at[h, s.px(i)], self.rc.at[h, slot], s.dx(i))

    def copy_e(self, h, i, there):
        s = self.s
        slot = s.me[0] if there else s.pz(i)
        ref = self.out.at[h, slot, pl.ds(s.me[3] * self.half, self.half)]
        return remote(ref, ref, self.se.at[h, s.pz(i)], self.re.at[h, slot], s.dz(i))

    def copy_f(self, h, i, there):
        s = self.s
        slot = s.me[3] if there else s.px(i)
        ref = self.out.at[h, :, pl.ds(slot * self.half, self.half)]
        return remote(ref, ref, self.sf.at[h, s.px(i)], self.rf.at[h, slot], s.dx(i))

    def stage_b(self, h):
        s = self.s
        self.copy_a(h).wait_recv()
        for i in list(range(1, s.ny)) + [0]:
            p = s.py(i)
            self.a[h, p] = (self.a[h, p].astype(F32) + self.part[h, p, s.me[2]].astype(F32)).astype(BF)
            if i:
                self.copy_b(h, i, True).start()

    def stage_c(self, h):
        s = self.s
        total = self.a[h, s.me[1]].astype(F32)
        for i in range(1, s.ny):
            self.copy_b(h, i, False).wait_recv()
            total = total + self.b[h, i - 1].astype(F32)
        self.a[h, s.me[1]] = total.astype(BF)
        for i in range(1, s.nx):
            self.copy_c(h, i, True).start()

    def stage_e(self, h):
        s = self.s
        mine = pl.ds(s.me[3] * self.half, self.half)
        total = self.a[h, s.me[1], mine].astype(F32)
        for i in range(1, s.nx):
            self.copy_c(h, i, False).wait_recv()
            total = total + self.c[h, s.px(i)].astype(F32)
        self.out[h, s.me[0], mine] = total.astype(BF)
        for i in range(1, s.nz):
            self.copy_e(h, i, True).start()

    def stage_f(self, h):
        s = self.s
        for i in range(1, s.nz):
            self.copy_e(h, i, False).wait_recv()
        for i in range(1, s.nx):
            self.copy_f(h, i, True).start()

    def stages(self):
        return (self.stage_b, self.stage_c, self.stage_e, self.stage_f)

    def finish(self, h):
        s = self.s
        self.copy_a(h).wait_send()
        for i in range(1, s.ny):
            self.copy_b(h, i, True).wait_send()
        for i in range(1, s.nx):
            self.copy_c(h, i, True).wait_send()
            self.copy_f(h, i, False).wait_recv()
            self.copy_f(h, i, True).wait_send()
        for i in range(1, s.nz):
            self.copy_e(h, i, True).wait_send()

    @staticmethod
    def sems(heads, ny, nx, nz):
        out = [pltpu.SemaphoreType.DMA((heads,))] * 2
        for n in (ny - 1, nx, nz, nx):
            out += [pltpu.SemaphoreType.DMA((heads, n))] * 2
        return out


def bwd_kernel(counts, *refs):
    refs = list(refs)

    def take(n):
        out = refs[:n]
        del refs[:n]
        return out

    prefix_ref, proj_ref, conv_ref, do_ref, o_ref, lse_ref, normed_ref = take(7)
    part_refs = take(len(counts))
    gp_ref, sum_ref, own_ref = take(3)
    wide, qs, ks, vs, dos, delta, dq, dk, dv, gk, gv, gwide, gp_s, gpt, own_part = take(15)
    send, recv, gsend, grecv = take(4)
    bufs = take(5)
    sems = take(10)
    own_bufs = take(3)
    own_sems = take(10)
    heads, length, _ = qs.shape
    width = gwide.shape[1]
    blocks = dos.shape[1]
    rows = length//blocks
    prefix = prefix_ref[0]
    parts = []
    first = 0
    for ref, count in zip(part_refs, counts):
        parts.append((ref, first, count))
        first += count
    sums = Sums(parts, sum_ref, bufs, sems, blocks)
    own = OwnSums(sums, own_part, own_ref, own_bufs, own_sems)
    z, y, c, x = sums.me
    greet(sums.peers())
    sums.start()

    def block_copy(h, i, at):
        return remote(do_ref.at[i * heads + h], dos.at[h, at], send.at[h, i], recv.at[h, at], (i, 2 * y + c, x))

    for h in range(heads):
        for i in range(1, blocks):
            block_copy(h, (z + i) % blocks, z).start()
        dos[h, z] = do_ref[z * heads + h]

    def gp_copy(h, i, at):
        return remote(gpt.at[h, i], gp_ref.at[at * heads + h], gsend.at[h, i], grecv.at[h, at], (i, 2 * y + c, x))

    ahead = min(2, sums.chunks)
    for k in range(ahead):
        sums.stage_b(k)
    convolve(proj_ref, conv_ref, wide, (qs, ks, vs))

    def head(h, _):
        for i in range(1, blocks):
            there = (z + i) % blocks
            block_copy(h, there, there).wait_recv()
        for i in range(blocks):
            prod = dos[h, i].astype(F32) * o_ref[h, i].astype(F32)
            delta[i] = jnp.broadcast_to(jnp.sum(prod, axis=0, keepdims=True), (8, rows))
        dq[...] = jnp.zeros(dq.shape, F32)
        def kblock(j, _):
            t = h*blocks + j
            @pl.when(t + ahead < sums.chunks)
            def _():
                sums.stage_b(t + ahead)
            @pl.when((t > 0) & (t != 3))
            def _():
                sums.step(jnp.where(t < 3, t - 1, t - 2))
            for n, stage in enumerate(own.stages()[:3], 1):
                @pl.when((h > 0) & (j == n))
                def _():
                    stage(h - 1)
            kat = pl.ds(pl.multiple_of(j*rows, rows), rows)
            k = ks[h, kat]; v = vs[h, kat]
            dk[...] = jnp.zeros(dk.shape, F32)
            dv[...] = jnp.zeros(dv.shape, F32)
            def step(i, masked):
                qat = pl.ds(pl.multiple_of(i*rows, rows), rows)
                q = qs[h, qat]; do = dos[h, i]
                s = nt(k, q)
                p = jnp.exp(s - lse_ref[h, 0:1, qat])
                if masked:
                    p = jnp.where(mask_t(i, j, rows, prefix), p, 0.0)
                dv[...] += nt(p.astype(BF), do)
                dp = jnp.dot(v, do, preferred_element_type=F32)
                ds = (p*(dp - delta[i, 0:1])).astype(BF)
                dk[...] += jnp.dot(ds, q, preferred_element_type=F32)
                dq[qat] += tn(ds, k)
                return 0
            lax.fori_loop(j+1, blocks, lambda i, _: step(i, False), 0)
            lax.fori_loop(jnp.where(j < blocks//2, 0, j), j+1, lambda i, _: step(i, True), 0)
            gk[kat] = dk[...].astype(BF)
            gv[kat] = dv[...].astype(BF)
            return 0
        lax.fori_loop(0, blocks, kblock, 0)
        def fill(c, _):
            at = pl.ds(pl.multiple_of(c*rows, rows), rows)
            gq = (dq[at]*(HEAD_DIM**-0.5)).astype(BF)
            gwide[at] = jnp.concatenate([gq, gk[at], gv[at]], axis=1).astype(F32)
            return 0
        lax.fori_loop(0, blocks, fill, 0)
        taps = conv_ref[h]
        def out(i, total):
            base = pl.multiple_of(i*rows, rows)
            g = gwide[pl.ds(base, rows+8)]
            w = wide[h, pl.ds(base, rows+8)]
            g0 = g[:rows]
            gp = taps[0:1]*g0 + taps[1:2]*g[1:rows+1] + taps[2:3]*g[2:rows+2]
            gp_s[pl.ds(base, rows)] = gp.astype(BF)
            gpt[h, i] = jnp.transpose(gp).astype(BF)
            add = [jnp.sum(g0*w[8-t:8-t+rows], axis=0, keepdims=True) for t in range(3)]
            return tuple(a+b for a, b in zip(total, add))
        total = lax.fori_loop(0, blocks, out, tuple(jnp.zeros((1, width), F32) for _ in range(3)))
        @pl.when(h < heads - 1)
        def _():
            for i in range(1, blocks):
                gp_copy(h, (z + i) % blocks, z).start()
        gp_ref[z * heads + h] = gpt[h, z]
        grad = jnp.dot(normed_ref[...], gp_s[...], preferred_element_type=F32).astype(BF)
        shape = own_part.shape[1:]
        mine = grad.shape[0] // (16 * shape[0] * shape[1])
        grad = grad.reshape(shape[0] * shape[1], 2, 8 * mine, width)
        grad = jnp.concatenate([grad[:, 0], grad[:, 1]], axis=2)
        own_part[h, :, :, 0:mine] = grad.reshape(shape[0], shape[1], mine, 8, 2 * width)
        extra = jnp.concatenate(list(total) + [jnp.zeros((5, width), F32)], axis=0)
        extra = jnp.concatenate([extra, jnp.zeros((8, width), F32)], axis=1).astype(BF)
        own_part[h, :, :, mine] = jnp.broadcast_to(extra, shape[:2] + (8, 2 * width))
        for spare in range(mine + 1, shape[2]):
            own_part[h, :, :, spare] = jnp.zeros(shape[:2] + (8, 2 * width), BF)
        own.copy_a(h).start()
        return 0
    gwide[length:length+8] = jnp.zeros((8, width), F32)
    lax.fori_loop(0, heads, head, 0)
    steps = heads*blocks
    turns = steps - 2
    def rest(t, _):
        sums.stage_b(t)
        return 0
    lax.fori_loop(steps + ahead, sums.chunks, rest, 0)
    for n, stage in enumerate(own.stages()):
        sums.step(turns + n)
        stage(heads - 1)
    def forward(h, _):
        own.stage_f(h)
        return 0
    lax.fori_loop(0, heads - 1, forward, 0)
    count = len(own.stages())
    for n in range(count, blocks):
        gp_copy(heads - 1, (z + n) % blocks, z).start()
    def tail(t, _):
        sums.step(t)
        return 0
    lax.fori_loop(turns + count, max(sums.chunks + sums.LAGS[-1], turns + count), tail, 0)
    for n in range(1, blocks):
        gp_copy(heads - 1, (z + n) % blocks, z).start()
    sums.finish()
    def done(h, _):
        own.finish(h)
        for i in range(1, blocks):
            there = (z + i) % blocks
            block_copy(h, there, z).wait_send()
            gp_copy(h, there, there).wait_recv()
            gp_copy(h, there, z).wait_send()
        return 0
    lax.fori_loop(0, heads, done, 0)

def attention_bwd(prefix, proj, conv, do, o, lse, normed, parts, shape):
    length = proj.shape[0]
    heads, blocks = o.shape[:2]
    width = 3 * HEAD_DIM
    rows = length // blocks
    counts = tuple(part.shape[2] for part in parts)
    ny, _, _, units = parts[0].shape[:4]
    unit = parts[0].shape[4:]
    nx = shape["replica"]
    chunks = sum(counts)
    half = units // nx
    own_units = -(-(normed.shape[0] // (32 * ny) + 1) // nx) * nx
    own_unit = (8, 2 * width)
    vm = pl.BlockSpec(memory_space=pltpu.VMEM)
    dma = pltpu.SemaphoreType.DMA
    per = pltpu.VMEM((heads, length, HEAD_DIM), BF)
    return pl.pallas_call(
        functools.partial(bwd_kernel, counts),
        out_shape=(
            jax.ShapeDtypeStruct((heads * blocks, width, rows), BF),
            jax.ShapeDtypeStruct((chunks, units) + unit, BF),
            jax.ShapeDtypeStruct((heads, blocks, own_units) + own_unit, BF),
        ),
        in_specs=[pl.BlockSpec(memory_space=pltpu.SMEM)] + [vm]*(6 + len(parts)),
        out_specs=(vm, vm, vm),
        scratch_shapes=[pltpu.VMEM((heads, 8+length, width), F32), per, per, per, pltpu.VMEM(o.shape, BF), pltpu.VMEM((blocks, 8, rows), F32),
            pltpu.VMEM((length, HEAD_DIM), F32), pltpu.VMEM((rows, HEAD_DIM), F32), pltpu.VMEM((rows, HEAD_DIM), F32),
            pltpu.VMEM((length, HEAD_DIM), BF), pltpu.VMEM((length, HEAD_DIM), BF),
            pltpu.VMEM((length+8, width), F32), pltpu.VMEM((length, width), BF), pltpu.VMEM((heads, blocks, width, rows), BF),
            pltpu.VMEM((heads, ny, 2, own_units) + own_unit, BF)]
            + [dma((heads, blocks))] * 4
            + [pltpu.VMEM((chunks, ny, units) + unit, BF), pltpu.VMEM((chunks, ny - 1, units) + unit, BF),
            pltpu.VMEM((chunks, nx, half) + unit, BF), pltpu.VMEM((chunks, half // 2) + unit, BF), pltpu.VMEM((chunks, half // 4) + unit, BF)]
            + Sums.sems(chunks, ny, nx)
            + [pltpu.VMEM((heads, ny, own_units) + own_unit, BF), pltpu.VMEM((heads, ny - 1, own_units) + own_unit, BF),
            pltpu.VMEM((heads, nx, own_units // nx) + own_unit, BF)]
            + OwnSums.sems(heads, ny, nx, blocks),
        compiler_params=pltpu.CompilerParams(vmem_limit_bytes=67043328, collective_id=3, has_side_effects=True),
        cost_estimate=pl.CostEstimate(flops=10*heads*length*length*HEAD_DIM, bytes_accessed=length*width*4, transcendentals=heads*length*length),
        name="attention_bwd",
    )(prefix, proj, conv, do, o, lse, normed, *parts)


def finish_kernel(
    gp_ref, sum_ref, own_ref, wq_ref, tok_ref, gh_ref, gone_ref, w_qkv_ref, w_up_ref, gains_ref,
    gin_out, qkv_out, out_out, up_out, down_out, conv_ref, ggain_ref,
    wq, tok, gh, w_qkv, w_up, gin, qkv, out, up, down, isem, osem,
):
    depth = w_qkv.shape[0]
    width = tok.shape[1]
    heads, blocks = own_ref.shape[:2]
    mine = depth // 8
    loads = [
        pltpu.make_async_copy(src, dst, isem.at[i])
        for i, (src, dst) in enumerate(
            ((wq_ref, wq), (tok_ref, tok), (gh_ref, gh), (w_up_ref, w_up), (w_qkv_ref, w_qkv))
        )
    ]
    for load in loads:
        load.start()
    stores = [
        pltpu.make_async_copy(src, dst, osem.at[i])
        for i, (src, dst) in enumerate(
            ((down, down_out), (out, out_out), (up, up_out), (qkv, qkv_out), (gin, gin_out))
        )
    ]
    ups = w_up.shape[1] // width
    downs = down.shape[0] // depth

    def rows_of(first, count):
        return sum_ref[first * mine : (first + count) * mine].reshape(count * depth, width).astype(F32)

    for i in range(downs):
        down[i * depth : (i + 1) * depth] = rows_of(ups + i, 1)
    stores[0].start()
    out[...] = rows_of(ups + downs, 1)
    stores[1].start()
    loads[3].wait()
    total = jnp.zeros((depth, 1), F32)
    for i in range(ups):
        at = slice(i * width, (i + 1) * width)
        grad = rows_of(i, 1)
        up[:, at] = grad
        total = total + jnp.sum(grad * w_up[:, at].astype(F32), axis=1, keepdims=True)
    stores[2].start()
    lanes = 3 * HEAD_DIM

    def grad_of(h, j):
        pair = own_ref[h, j, : mine // 2].reshape(depth // 2, 2 * lanes)
        return jnp.concatenate([pair[:, :lanes], pair[:, lanes:]], axis=0)

    grads = [grad_of(h, j) for j in range(blocks) for h in range(heads)]
    taps = [own_ref[h, j, mine // 2] for j in range(blocks) for h in range(heads)]

    def merge(pieces, p):
        return jnp.concatenate([piece[:, p * HEAD_DIM : (p + 1) * HEAD_DIM] for piece in pieces], axis=1)

    loads[4].wait()
    attn = jnp.zeros((depth, 1), F32)
    for p in range(3):
        at = slice(p * width, (p + 1) * width)
        grad = merge(grads, p).astype(F32)
        qkv[:, at] = grad
        attn = attn + jnp.sum(grad * w_qkv[:, at].astype(F32), axis=1, keepdims=True)
        conv_ref[:, at] = merge(taps, p).astype(F32)
    stores[3].start()
    gains = gains_ref[...]
    ggain_ref[...] = jnp.concatenate([attn / gains[:, 0:1], total / gains[:, 1:2]], axis=1)
    for load in loads[:3]:
        load.wait()
    e1 = jnp.zeros(gh.shape, F32)
    for j in range(blocks):
        e1 = e1 + lax.dot_general(gp_ref[j], wq[j], (((0,), (1,)), ((), ())), preferred_element_type=F32)
    x = tok[...].astype(F32)
    scale = lax.rsqrt(jnp.mean(x * x, axis=-1, keepdims=True) + 1e-06)
    weighted = e1 * gone_ref[...]
    back = scale * weighted - x * scale**3 * jnp.mean(weighted * x, axis=-1, keepdims=True)
    gin[...] = (gh[...] + back).astype(BF)
    stores[4].start()
    for store in stores:
        store.wait()


def finish(gp, sums, own_sums, wq, tok, gh, gone, w_qkv, w_up, gains, ff):
    depth, width = w_qkv.shape[0], tok.shape[1]
    vm = pl.BlockSpec(memory_space=pltpu.VMEM)
    hbm = pl.BlockSpec(memory_space=pl.ANY)
    dma = pltpu.SemaphoreType.DMA
    outs = [
        (tok.shape, BF),
        (w_qkv.shape, F32),
        ((depth, width), F32),
        (w_up.shape, F32),
        ((ff, width), F32),
    ]
    flat = [((8, w_qkv.shape[1]), F32), ((depth, 2), F32)]
    kept = [(a.shape, a.dtype) for a in (wq, tok, gh, w_qkv, w_up)]
    return pl.pallas_call(
        finish_kernel,
        out_shape=[jax.ShapeDtypeStruct(*o) for o in outs + flat],
        in_specs=[vm] * 3 + [hbm] * 3 + [vm] + [hbm] * 2 + [vm],
        out_specs=[hbm] * 5 + [vm] * 2,
        scratch_shapes=[pltpu.VMEM(*o) for o in kept + outs] + [dma((5,)), dma((5,))],
        compiler_params=pltpu.CompilerParams(vmem_limit_bytes=60 * 1024 * 1024),
        name="finish",
    )(gp, sums, own_sums, wq, tok, gh, gone, w_qkv, w_up, gains)


def rms_scale(values):
    return lax.rsqrt(jnp.mean(values * values, axis=-1, keepdims=True) + 1e-06)


def norm_back(values, scale_rows, gain, upstream):
    weighted = upstream * gain
    grad_values = scale_rows * weighted - values * scale_rows**3 * jnp.mean(
        weighted * values, axis=-1, keepdims=True
    )
    return grad_values


def dot(a, b):
    return jnp.dot(a, b, preferred_element_type=F32)


def per_device(
    tokens, prefix_len, w_qkv, w_out, w_up, w_down, conv_w, gain_attn, gain_ffn, cotangent
):
    blocks = lax.axis_size("seq")
    me = lax.axis_index("seq")
    rows, width = tokens.shape[1:]
    own = HEADS // blocks * HEAD_DIM
    depth = w_qkv.shape[0]

    shards, copies = lax.axis_size("shard"), lax.axis_size("replica")
    heads = HEADS // blocks
    columns = w_qkv.reshape(depth, 3, blocks, heads, HEAD_DIM).transpose(2, 0, 3, 1, 4)
    gains = jnp.pad(jnp.stack([gain_attn, gain_ffn]), ((0, 0), (0, conv_w.shape[1] - depth)))
    small = jnp.pad(jnp.concatenate([gains, conv_w]), ((0, 3), (0, 0)))
    normed_all, projected, small, full_qkv, full_out, full_up = gather_all(
        tokens[0], small, columns.reshape(blocks, depth, 3 * own), w_out, w_up, blocks, shards
    )
    full_qkv = full_qkv.reshape(blocks, width, 3 * own)
    full_out = full_out.reshape(width, width)
    full_up = full_up.reshape(width, -1)
    full_gone = small[:, 0, 0, :depth].reshape(width).astype(F32)
    full_gtwo = small[:, 0, 1, :depth].reshape(width).astype(F32)
    full_conv = small[:, 0, 2:5].transpose(1, 0, 2)
    own_conv = lax.dynamic_index_in_dim(full_conv.reshape(3, 3, blocks, heads, HEAD_DIM), me, 2, False)
    own_conv = own_conv.transpose(2, 0, 1, 3).reshape(heads, 3, 3 * HEAD_DIM).astype(F32)
    attended_own, logsum, attended, full_down = attention_fwd(
        prefix_len, projected, own_conv, w_down.reshape(-1, depth, width), blocks, shards
    )
    full_down = full_down.reshape(-1, width)
    attended = attended.reshape(width, rows)

    inputs = tokens[0].astype(F32)
    hidden = inputs + tn(attended, full_out)
    scale_two = rms_scale(hidden)
    normed_two_b = (hidden * scale_two * full_gtwo).astype(BF)
    positive = jnp.maximum(dot(normed_two_b, full_up), 0.0)
    active_b = (positive * positive).astype(BF)
    output = hidden + dot(active_b, full_down)

    incoming = cotangent[0]
    grad_upper_b = (dot(incoming, full_down.T) * 2.0 * positive).astype(BF)
    grad_normed_two = dot(grad_upper_b, full_up.T)
    grad_hidden = incoming.astype(F32) + norm_back(hidden, scale_two, full_gtwo, grad_normed_two)
    grad_hidden_b = grad_hidden.astype(BF)
    grad_attended = nt(full_out, grad_hidden_b).astype(BF)

    mine = depth // 8

    def cut(grad):
        return grad.astype(BF).reshape(shards // 2, 2, -1, mine, 8, width)

    parts = [
        cut(dot(normed_two_b.T, grad_upper_b[:, i * width : (i + 1) * width]))
        for i in range(grad_upper_b.shape[1] // width)
    ]
    parts += [cut(dot(active_b.T, incoming)), cut(dot(attended, grad_hidden_b))]
    pieces = sum(part.shape[2] for part in parts)
    if mine % (copies * blocks):
        units = -(-pieces * mine // (copies * blocks)) * copies * blocks
        joined = [part.reshape(shards // 2, 2, -1, 8, width) for part in parts]
        joined.append(jnp.zeros((shards // 2, 2, units - pieces * mine, 8, width), BF))
        joined = jnp.concatenate(joined, axis=2)
        parts = [joined.reshape(shards // 2, 2, -1, copies * blocks, 8, width)]

    grad_projected, sums, own_sums = attention_bwd(
        prefix_len, projected, own_conv, grad_attended.reshape(HEADS, HEAD_DIM, rows),
        attended_own, logsum, normed_all, parts, {"replica": copies},
    )
    grad_projected = grad_projected.reshape(blocks, 3 * own, rows)
    sums = sums.reshape(-1, 8, width)
    gains = jnp.stack([gain_attn, gain_ffn], axis=1).astype(F32)
    grad_input, total_qkv, total_out, total_up, total_down, total_conv, grad_gains = finish(
        grad_projected, sums, own_sums, full_qkv, tokens[0], grad_hidden, full_gone[None],
        w_qkv, w_up, gains, w_down.shape[0],
    )
    at = lax.axis_index("shard")
    return (
        output[None].astype(BF),
        grad_input[None],
        total_qkv,
        total_out,
        total_up,
        total_down,
        lax.dynamic_slice_in_dim(total_conv[:3], at * conv_w.shape[1], conv_w.shape[1], 1),
        grad_gains[:, 0],
        grad_gains[:, 1],
    )


def solution(mesh):
    placed = (
        P(("shard", "replica"), "seq", None),
        P(("shard", "replica")),
        P("shard", None),
        P("shard", None),
        P("shard", None),
        P("shard", None),
        P(None, "shard"),
        P("shard"),
        P("shard"),
        P(("shard", "replica"), "seq", None),
    )
    return jax.shard_map(
        per_device,
        mesh=mesh,
        in_specs=placed,
        out_specs=(
            P(("shard", "replica"), "seq", None),
            P(("shard", "replica"), "seq", None),
            P("shard", None),
            P("shard", None),
            P("shard", None),
            P("shard", None),
            P(None, "shard"),
            P("shard"),
            P("shard"),
        ),
        check_vma=False,
    )
```

```python
import functools

import jax
import jax.numpy as jnp
from jax import lax
from jax.experimental import pallas as pl
from jax.experimental.pallas import tpu as pltpu
from jax.sharding import PartitionSpec as P

HEADS = 12
HEAD_DIM=64
NEG=-1e30
F32=jnp.float32
BF=jnp.bfloat16

def nt(a,b):
    return lax.dot_general(a,b,(((1,),(1,)),((),())),preferred_element_type=F32)
def tn(a,b):
    return lax.dot_general(a,b,(((0,),(0,)),((),())),preferred_element_type=F32)

def convolve(proj_ref, conv_ref, wide, parts):
    length = proj_ref.shape[0]
    heads, _, width = wide.shape
    rows = min(512, length)
    for h in range(heads):
        wide[h, 0:8] = jnp.zeros((8, width), F32)
        for c in range(length//rows):
            wide[h, 8+c*rows:8+(c+1)*rows] = proj_ref[c*rows:(c+1)*rows, h*width:(h+1)*width].astype(F32)
    def body(c, _):
        base = pl.multiple_of(c*rows, rows)
        for h in range(heads):
            x = wide[h, pl.ds(base, rows+8)]
            taps = conv_ref[h]
            mixed = taps[0:1]*x[8:] + taps[1:2]*x[7:7+rows] + taps[2:3]*x[6:6+rows]
            for p, ref in enumerate(parts):
                piece = mixed[:, p*HEAD_DIM:(p+1)*HEAD_DIM].astype(BF)
                if p == 0:
                    piece = piece * jnp.asarray(HEAD_DIM**-0.5, BF)
                ref[h, pl.ds(base, rows)] = piece
        return 0
    lax.fori_loop(0, length//rows, body, 0)

def mask_t(i, j, rows, prefix):
    kpos = j*rows + lax.broadcasted_iota(jnp.int32, (rows, 1), 0)
    qpos = i*rows + lax.broadcasted_iota(jnp.int32, (1, rows), 1)
    return (kpos <= qpos) | ((kpos < prefix) & (qpos < prefix))

def mask_n(i, j, rows, prefix):
    qpos = i*rows + lax.broadcasted_iota(jnp.int32, (rows, 1), 0)
    kpos = j*rows + lax.broadcasted_iota(jnp.int32, (1, rows), 1)
    return (kpos <= qpos) | ((kpos < prefix) & (qpos < prefix))

MESH = pl.DeviceIdType.MESH


def remote(src, dst, send, recv, peer):
    return pltpu.make_async_remote_copy(
        src_ref=src, dst_ref=dst, send_sem=send, recv_sem=recv, device_id=peer, device_id_type=MESH
    )


def greet(peers):
    barrier = pltpu.get_barrier_semaphore()
    for peer in peers:
        pl.semaphore_signal(barrier, inc=1, device_id=peer, device_id_type=MESH)
    pl.semaphore_wait(barrier, len(peers))


def split_shard():
    s = lax.axis_index("shard")
    return lax.axis_index("seq"), s // 2, s % 2, lax.axis_index("replica")


class Gather:
    def __init__(self, src, dst, sems, major=False):
        self.src, self.dst, self.major = src, dst, major
        self.sy, self.ry, self.sk, self.rk, self.local = sems
        self.ny = dst.shape[1 if major else 0] // 2
        self.chunks = dst.shape[0 if major else 1]
        self.z, self.y, self.c, self.x = split_shard()
        self.core = (self.z, 2 * self.y + 1 - self.c, self.x)

    def py(self, i):
        return (self.y + i) % self.ny

    def dy(self, i):
        return (self.z, 2 * self.py(i) + self.c, self.x)

    def peers(self):
        return [self.core] + [self.dy(i) for i in range(1, self.ny)]

    def slot(self, p, core, j):
        shard = 2 * p + core
        return self.dst.at[j, shard] if self.major else self.dst.at[shard, j]

    def own(self):
        shard = 2 * self.y + self.c
        dst = self.dst.at[:, shard] if self.major else self.dst.at[shard]
        return pltpu.make_async_copy(self.src, dst, self.local.at[0])

    def over_y(self, j, i):
        slot = self.slot(self.y, self.c, j)
        return remote(self.src.at[j], slot, self.sy.at[j, self.py(i)], self.ry.at[j, self.y], self.dy(i))

    def to_core(self, j):
        slot = self.slot(self.y, self.c, j)
        return remote(self.src.at[j], slot, self.sk.at[j, self.y], self.rk.at[j, self.y], self.core)

    def pass_on(self, j, i):
        ref = self.slot(self.py(i), self.c, j)
        return remote(ref, ref, self.sk.at[j, self.py(i)], self.rk.at[j, self.py(i)], self.core)

    def send(self, j):
        for i in range(1, self.ny):
            self.over_y(j, i).start()
        self.to_core(j).start()

    def start(self):
        for j in range(self.chunks):
            self.send(j)
        self.own().start()

    def relay(self, j):
        for i in range(1, self.ny):
            ref = self.slot(self.py(i), self.c, j)
            remote(ref, ref, self.sy.at[j, self.py(i)], self.ry.at[j, self.py(i)], self.dy(i)).wait_recv()
            self.pass_on(j, i).start()

    def arrive(self, j):
        for i in range(self.ny):
            ref = self.slot(self.py(i), 1 - self.c, j)
            remote(ref, ref, self.sk.at[j, self.py(i)], self.rk.at[j, self.py(i)], self.core).wait_recv()

    def sent(self, j):
        self.to_core(j).wait_send()
        for i in range(1, self.ny):
            self.over_y(j, i).wait_send()
            self.pass_on(j, i).wait_send()

    def finish(self):
        self.own().wait()
        for j in range(self.chunks):
            self.arrive(j)
            self.sent(j)

    @staticmethod
    def sems(shards, chunks):
        return [pltpu.SemaphoreType.DMA((chunks, shards // 2))] * 4 + [pltpu.SemaphoreType.DMA((1,))]


def gather_kernel(
    tok_ref, small_ref, qkv_ref, out_ref, up_ref,
    normed_ref, proj_ref, small_all, qkv_all, out_all, up_all,
    toks, weight_s, wsem, sl, sr, rl, rr, *sems,
):
    blocks, rows, width = toks.shape
    _, shards, depth, columns = qkv_all.shape
    small, qkv, out, up = (
        Gather(src, dst, sems[5 * i : 5 * i + 5], major=i == 1)
        for i, (src, dst) in enumerate(
            ((small_ref, small_all), (qkv_ref, qkv_all), (out_ref, out_all), (up_ref, up_all))
        )
    )
    z, y, c, x = split_shard()
    shard = 2 * y + c
    left, right = (z - 1, shard, x), (z + 1, shard, x)
    has_left, has_right = z > 0, z < blocks - 1
    greet(small.peers() + [((z + i) % blocks, shard, x) for i in range(1, blocks)])

    def go_left(b, src):
        return remote(src, toks.at[b], sl.at[b], rr.at[b], left)

    def go_right(b, src):
        return remote(src, toks.at[b], sr.at[b], rl.at[b], right)

    small.start()
    qkv.send(z)
    qkv.own().start()

    @pl.when(has_left)
    def _():
        go_left(z, tok_ref).start()

    @pl.when(has_right)
    def _():
        go_right(z, tok_ref).start()

    out.start()
    up.start()
    for i in range(1, blocks):
        qkv.send((z + i) % blocks)
    small.relay(0)
    qkv.relay(z)
    small.finish()
    qkv.own().wait()
    qkv.arrive(z)
    gain = jnp.concatenate([small_all[s, 0, 0:1, :depth] for s in range(shards)], axis=1).astype(F32)
    fetch = pltpu.make_async_copy(qkv_all.at[z], weight_s, wsem.at[0])
    fetch.start()
    fetch.wait()
    weight = weight_s[...].reshape(shards * depth, columns)

    def project(b, values):
        at = pl.ds(pl.multiple_of(b * rows, rows), rows)
        values = values.astype(F32)
        scale = lax.rsqrt(jnp.mean(values * values, axis=-1, keepdims=True) + 1e-06)
        normed = values * scale * gain
        proj_ref[at] = jnp.dot(normed.astype(BF), weight, preferred_element_type=F32).astype(BF)
        normed_ref[:, at] = jnp.transpose(normed).astype(BF)

    project(z, tok_ref[...])
    for d in range(1, blocks):
        before, after = z - d, z + d

        @pl.when(before >= 0)
        def _():
            go_right(before, toks.at[before]).wait_recv()

            @pl.when(has_right)
            def _():
                go_right(before, toks.at[before]).start()

        @pl.when(after < blocks)
        def _():
            go_left(after, toks.at[after]).wait_recv()

            @pl.when(has_left)
            def _():
                go_left(after, toks.at[after]).start()

        @pl.when(before >= 0)
        def _():
            project(before, toks[before])

        @pl.when(after < blocks)
        def _():
            project(after, toks[after])

        if d == 1:
            out.relay(0)
        last = up.chunks * d // (blocks - 1)
        for j in range(up.chunks * (d - 1) // (blocks - 1), last):
            up.relay(j)

    for i in range(1, blocks):
        qkv.relay((z + i) % blocks)
    out.finish()
    up.finish()
    for i in range(1, blocks):
        qkv.arrive((z + i) % blocks)
    for j in range(blocks):
        qkv.sent(j)

    def sent(b, _):
        @pl.when((b <= z) & has_right)
        def _():
            go_right(b, toks.at[b]).wait_send()

        @pl.when((b >= z) & has_left)
        def _():
            go_left(b, toks.at[b]).wait_send()

        return 0

    lax.fori_loop(0, blocks, sent, 0)


def gather_all(tokens, small, qkv, out, up, blocks, shards):
    rows, width = tokens.shape
    vm = pl.BlockSpec(memory_space=pltpu.VMEM)
    hbm = pl.BlockSpec(memory_space=pl.ANY)
    cut = 4
    arrays = [
        small[None],
        qkv,
        out[None],
        up.reshape(cut, up.shape[0] // cut, up.shape[1]),
    ]
    dma = pltpu.SemaphoreType.DMA
    sems = [dma((blocks,))] * 4
    for array in arrays:
        sems += Gather.sems(shards, array.shape[0])
    return pl.pallas_call(
        gather_kernel,
        out_shape=[
            jax.ShapeDtypeStruct((width, blocks * rows), BF),
            jax.ShapeDtypeStruct((blocks * rows, qkv.shape[2]), BF),
        ]
        + [
            jax.ShapeDtypeStruct(
                (blocks, shards) + array.shape[1:] if i == 1 else (shards,) + array.shape, BF
            )
            for i, array in enumerate(arrays)
        ],
        in_specs=[vm] * 5,
        out_specs=[vm] * 3 + [hbm] * 3,
        scratch_shapes=[pltpu.VMEM((blocks, rows, width), BF), pltpu.VMEM((shards,) + qkv.shape[1:], BF), dma((1,))]
        + sems,
        compiler_params=pltpu.CompilerParams(
            vmem_limit_bytes=60 * 1024 * 1024, collective_id=4, has_side_effects=True
        ),
        name="gather_all",
    )(tokens, *arrays)


def fwd_kernel(prefix_ref, proj_ref, conv_ref, down_ref, own_ref, lse_ref, rows_ref, down_all, wide, qs, ks, vs, m_s, l_s, acc_s, o_s, r_s, send, recv, *sems):
    heads = qs.shape[0]
    length = proj_ref.shape[0]
    blocks = own_ref.shape[1]
    rows = length // blocks
    prefix = prefix_ref[0]
    z, s_at, x = lax.axis_index("seq"), lax.axis_index("shard"), lax.axis_index("replica")

    def block_copy(h, i, at):
        return remote(o_s.at[h, i], r_s.at[at * heads + h], send.at[h, i], recv.at[h, at], (i, s_at, x))

    down = Gather(down_ref, down_all, sems)
    greet([((z + i) % blocks, s_at, x) for i in range(1, blocks)] + down.peers())
    down.start()
    convolve(proj_ref, conv_ref, wide, (qs, ks, vs))
    def head(h, _):
        for j in range(down.chunks):
            @pl.when(h == 1 + (j + 1) // 2)
            def _():
                down.relay(j)
        def qblock(i, _):
            q = qs[h, pl.ds(pl.multiple_of(i*rows, rows), rows)]
            m_s[...] = jnp.full((1, rows), NEG, F32)
            l_s[...] = jnp.zeros((1, rows), F32)
            acc_s[...] = jnp.zeros((HEAD_DIM, rows), F32)
            def step(j, masked):
                at = pl.ds(pl.multiple_of(j*rows, rows), rows)
                s = nt(ks[h, at], q)
                if masked:
                    s = jnp.where(mask_t(i, j, rows, prefix), s, NEG)
                m_old = m_s[...]
                m_new = jnp.maximum(m_old, jnp.max(s, axis=0, keepdims=True))
                p = jnp.exp(s - m_new)
                a = jnp.exp(m_old - m_new)
                m_s[...] = m_new
                l_s[...] = a*l_s[...] + jnp.sum(p, axis=0, keepdims=True)
                acc_s[...] = a*acc_s[...] + tn(vs[h, at], p.astype(BF))
                return 0
            lax.fori_loop(0, i, lambda j, _: step(j, False), 0)
            lax.fori_loop(i, jnp.maximum(i+1, blocks//2), lambda j, _: step(j, True), 0)
            l = l_s[...]
            done = (acc_s[...]/l).astype(BF)
            o_s[h, i] = done
            own_ref[h, i] = done
            @pl.when(i != z)
            def _():
                block_copy(h, i, z).start()
            lse = m_s[...] + jnp.log(l)
            lse_ref[h, :, pl.ds(pl.multiple_of(i*rows, rows), rows)] = jnp.broadcast_to(lse, (8, rows))
            return 0
        lax.fori_loop(0, blocks, qblock, 0)
        r_s[z * heads + h] = o_s[h, z]
        return 0
    lax.fori_loop(0, heads, head, 0)
    for j in range(down.chunks):
        if 1 + (j + 1) // 2 >= heads:
            down.relay(j)
    down.finish()
    def finish(h, _):
        for i in range(1, blocks):
            there = (z + i) % blocks
            block_copy(h, there, there).wait_recv()
            block_copy(h, there, z).wait_send()
        return 0
    lax.fori_loop(0, heads, finish, 0)
    rows_ref[...] = r_s[...]

def attention_fwd(prefix, proj, conv, down, blocks, shards):
    length, width = proj.shape
    heads = width//(3*HEAD_DIM)
    rows = length // blocks
    vm = pl.BlockSpec(memory_space=pltpu.VMEM)
    own = (heads, blocks, HEAD_DIM, rows)
    every = (heads * blocks, HEAD_DIM, rows)
    return pl.pallas_call(
        fwd_kernel,
        out_shape=(jax.ShapeDtypeStruct(own, BF), jax.ShapeDtypeStruct((heads, 8, length), F32), jax.ShapeDtypeStruct(every, BF),
            jax.ShapeDtypeStruct((shards,) + down.shape, BF)),
        in_specs=[pl.BlockSpec(memory_space=pltpu.SMEM), vm, vm, vm],
        out_specs=(vm, vm, vm, pl.BlockSpec(memory_space=pl.ANY)),
        scratch_shapes=[pltpu.VMEM((heads, 8+length, 3*HEAD_DIM), F32)] + [pltpu.VMEM((heads, length, HEAD_DIM), BF)]*3 + [
            pltpu.VMEM((1,rows),F32), pltpu.VMEM((1,rows),F32), pltpu.VMEM((HEAD_DIM,rows),F32), pltpu.VMEM(own,BF), pltpu.VMEM(every,BF),
            pltpu.SemaphoreType.DMA((heads, blocks)), pltpu.SemaphoreType.DMA((heads, blocks))] + Gather.sems(shards, down.shape[0]),
        compiler_params=pltpu.CompilerParams(vmem_limit_bytes=60*1024*1024, collective_id=2, has_side_effects=True),
        cost_estimate=pl.CostEstimate(flops=4*heads*length*length*HEAD_DIM, bytes_accessed=length*width*2, transcendentals=heads*length*length),
        name="attention_fwd",
    )(prefix, proj, conv, down)

class Sums:
    def __init__(self, parts, out_ref, bufs, sems, nz):
        self.parts, self.out = parts, out_ref
        self.a, self.b, self.c, self.near, self.far = bufs
        self.sa, self.ra, self.sb, self.rb, self.sc, self.rc, self.sz, self.rz, self.sf, self.rf = sems
        self.chunks, self.ny = self.a.shape[:2]
        self.nx = self.c.shape[1]
        self.nz = nz
        self.half = self.c.shape[2]
        self.piece = self.half // nz
        self.me = split_shard()
        z, y, c, x = self.me
        self.core = (z, 2 * y + 1 - c, x)
        self.low, self.high = z % 2, z // 2
        self.one = (z + 1 - 2 * self.low, 2 * y + c, x)
        self.two = (z + 2 - 4 * self.high, 2 * y + c, x)

    def py(self, i):
        return (self.me[1] + i) % self.ny

    def px(self, i):
        return (self.me[3] + i) % self.nx

    def pz(self, i):
        return (self.me[0] + i) % self.nz

    def dy(self, i):
        z, y, c, x = self.me
        return (z, 2 * self.py(i) + c, x)

    def dx(self, i):
        z, y, c, x = self.me
        return (z, 2 * y + c, self.px(i))

    def dz(self, i):
        z, y, c, x = self.me
        return (self.pz(i), 2 * y + c, x)

    def peers(self):
        out = [self.core] + [self.dy(i) for i in range(1, self.ny)]
        out += [self.dx(i) for i in range(1, self.nx)]
        return out + [self.dz(i) for i in range(1, self.nz)]

    def copy_a(self, k, src):
        return remote(src, self.a.at[k], self.sa.at[k], self.ra.at[k], self.core)

    def start(self):
        c = self.me[2]
        for ref, first, count in self.parts:
            for j in range(count):
                src = ref.at[:, 1 - c, j]
                self.copy_a(first + j, src).start()

    def copy_b(self, k, i, there):
        slot = self.ny - i - 1 if there else i - 1
        return remote(self.a.at[k, self.py(i)], self.b.at[k, slot], self.sb.at[k, i - 1], self.rb.at[k, slot], self.dy(i))

    def stage_b(self, k):
        c = self.me[2]
        self.copy_a(k, self.a.at[k]).wait_recv()
        for i in list(range(1, self.ny)) + [0]:
            p = self.py(i)
            for ref, first, count in self.parts:
                @pl.when((k >= first) & (k < first + count))
                def _():
                    j = jnp.clip(k - first, 0, count - 1)
                    self.a[k, p] = (self.a[k, p].astype(F32) + ref[p, c, j].astype(F32)).astype(BF)
            if i:
                self.copy_b(k, i, True).start()

    def copy_c(self, k, i, there):
        slot = self.me[3] if there else self.px(i)
        src = self.a.at[k, self.me[1], pl.ds(self.px(i) * self.half, self.half)]
        return remote(src, self.c.at[k, slot], self.sc.at[k, self.px(i)], self.rc.at[k, slot], self.dx(i))

    def stage_c(self, k):
        y = self.me[1]
        total = self.a[k, y].astype(F32)
        for i in range(1, self.ny):
            self.copy_b(k, i, False).wait_recv()
            total = total + self.b[k, i - 1].astype(F32)
        for i in range(1, self.ny):
            self.copy_b(k, i, True).wait_send()
        self.a[k, y] = total.astype(BF)
        for i in range(1, self.nx):
            self.copy_c(k, i, True).start()

    def pieces(self, low, high, count):
        return pl.ds(self.me[3] * self.half + (2 * low + high) * self.piece, count * self.piece)

    def copy_z(self, k, stage):
        if stage == 0:
            src, dst, peer = self.a.at[k, self.me[1], self.pieces(1 - self.low, 0, 2)], self.near.at[k], self.one
        elif stage == 1:
            src, dst, peer = self.a.at[k, self.me[1], self.pieces(self.low, 1 - self.high, 1)], self.far.at[k], self.two
        elif stage == 2:
            src = dst = self.out.at[k, self.pieces(self.low, self.high, 1)]
            peer = self.two
        else:
            src = dst = self.out.at[k, self.pieces(self.low, 0, 2)]
            peer = self.one
        return remote(src, dst, self.sz.at[k, stage], self.rz.at[k, stage], peer)

    def stage_d(self, k):
        z, y, c, x = self.me
        mine = pl.ds(x * self.half, self.half)
        total = self.a[k, y, mine].astype(F32)
        for i in range(1, self.nx):
            self.copy_c(k, i, False).wait_recv()
            total = total + self.c[k, self.px(i)].astype(F32)
        for i in range(1, self.nx):
            self.copy_c(k, i, True).wait_send()
        self.a[k, y, mine] = total.astype(BF)
        self.copy_z(k, 0).start()

    def stage_near(self, k):
        y = self.me[1]
        self.copy_z(k, 0).wait_recv()
        self.copy_z(k, 0).wait_send()
        mine = self.pieces(self.low, 0, 2)
        self.a[k, y, mine] = (self.a[k, y, mine].astype(F32) + self.near[k].astype(F32)).astype(BF)
        self.copy_z(k, 1).start()

    def stage_far(self, k):
        self.copy_z(k, 1).wait_recv()
        mine = self.pieces(self.low, self.high, 1)
        self.out[k, mine] = (self.a[k, self.me[1], mine].astype(F32) + self.far[k].astype(F32)).astype(BF)
        self.copy_z(k, 2).start()

    def stage_back(self, k):
        ref = self.out.at[k, self.pieces(self.low, 1 - self.high, 1)]
        remote(ref, ref, self.sz.at[k, 2], self.rz.at[k, 2], self.two).wait_recv()
        self.copy_z(k, 3).start()

    def copy_f(self, k, i, there):
        slot = self.me[3] if there else self.px(i)
        ref = self.out.at[k, pl.ds(slot * self.half, self.half)]
        return remote(ref, ref, self.sf.at[k, self.px(i)], self.rf.at[k, slot], self.dx(i))

    def stage_f(self, k):
        ref = self.out.at[k, self.pieces(1 - self.low, 0, 2)]
        remote(ref, ref, self.sz.at[k, 3], self.rz.at[k, 3], self.one).wait_recv()
        for i in range(1, self.nx):
            self.copy_f(k, i, True).start()

    LAGS = (0, 1, 2, 3, 4, 5)

    def step(self, t):
        stages = (self.stage_c, self.stage_d, self.stage_near, self.stage_far, self.stage_back, self.stage_f)
        for lag, stage in zip(self.LAGS, stages):
            @pl.when((t >= lag) & (t < self.chunks + lag))
            def _():
                stage(t - lag)

    def finish(self):
        def body(k, _):
            for i in range(1, self.nx):
                self.copy_f(k, i, False).wait_recv()
            self.copy_a(k, self.a.at[k]).wait_send()
            for i in range(1, self.nx):
                self.copy_f(k, i, True).wait_send()
            for stage in range(1, 4):
                self.copy_z(k, stage).wait_send()
            return 0

        lax.fori_loop(0, self.chunks, body, 0)

    @staticmethod
    def sems(chunks, ny, nx):
        out = [pltpu.SemaphoreType.DMA((chunks,))] * 2
        for n in (ny - 1, nx, 4, nx):
            out += [pltpu.SemaphoreType.DMA((chunks, n))] * 2
        return out


class OwnSums:
    def __init__(self, sums, part, out, bufs, sems):
        self.s, self.part, self.out = sums, part, out
        self.a, self.b, self.c = bufs
        self.sa, self.ra, self.sb, self.rb, self.sc, self.rc, self.se, self.re, self.sf, self.rf = sems
        self.half = self.c.shape[2]

    def copy_a(self, h):
        return remote(self.part.at[h, :, 1 - self.s.me[2]], self.a.at[h], self.sa.at[h], self.ra.at[h], self.s.core)

    def copy_b(self, h, i, there):
        s = self.s
        slot = s.ny - i - 1 if there else i - 1
        return remote(self.a.at[h, s.py(i)], self.b.at[h, slot], self.sb.at[h, i - 1], self.rb.at[h, slot], s.dy(i))

    def copy_c(self, h, i, there):
        s = self.s
        slot = s.me[3] if there else s.px(i)
        src = self.a.at[h, s.me[1], pl.ds(s.px(i) * self.half, self.half)]
        return remote(src, self.c.at[h, slot], self.sc.at[h, s.px(i)], self.rc.at[h, slot], s.dx(i))

    def copy_e(self, h, i, there):
        s = self.s
        slot = s.me[0] if there else s.pz(i)
        ref = self.out.at[h, slot, pl.ds(s.me[3] * self.half, self.half)]
        return remote(ref, ref, self.se.at[h, s.pz(i)], self.re.at[h, slot], s.dz(i))

    def copy_f(self, h, i, there):
        s = self.s
        slot = s.me[3] if there else s.px(i)
        ref = self.out.at[h, :, pl.ds(slot * self.half, self.half)]
        return remote(ref, ref, self.sf.at[h, s.px(i)], self.rf.at[h, slot], s.dx(i))

    def stage_b(self, h):
        s = self.s
        self.copy_a(h).wait_recv()
        for i in list(range(1, s.ny)) + [0]:
            p = s.py(i)
            self.a[h, p] = (self.a[h, p].astype(F32) + self.part[h, p, s.me[2]].astype(F32)).astype(BF)
            if i:
                self.copy_b(h, i, True).start()

    def stage_c(self, h):
        s = self.s
        total = self.a[h, s.me[1]].astype(F32)
        for i in range(1, s.ny):
            self.copy_b(h, i, False).wait_recv()
            total = total + self.b[h, i - 1].astype(F32)
        self.a[h, s.me[1]] = total.astype(BF)
        for i in range(1, s.nx):
            self.copy_c(h, i, True).start()

    def stage_e(self, h):
        s = self.s
        mine = pl.ds(s.me[3] * self.half, self.half)
        total = self.a[h, s.me[1], mine].astype(F32)
        for i in range(1, s.nx):
            self.copy_c(h, i, False).wait_recv()
            total = total + self.c[h, s.px(i)].astype(F32)
        self.out[h, s.me[0], mine] = total.astype(BF)
        for i in range(1, s.nz):
            self.copy_e(h, i, True).start()

    def stage_f(self, h):
        s = self.s
        for i in range(1, s.nz):
            self.copy_e(h, i, False).wait_recv()
        for i in range(1, s.nx):
            self.copy_f(h, i, True).start()

    def stages(self):
        return (self.stage_b, self.stage_c, self.stage_e, self.stage_f)

    def finish(self, h):
        s = self.s
        self.copy_a(h).wait_send()
        for i in range(1, s.ny):
            self.copy_b(h, i, True).wait_send()
        for i in range(1, s.nx):
            self.copy_c(h, i, True).wait_send()
            self.copy_f(h, i, False).wait_recv()
            self.copy_f(h, i, True).wait_send()
        for i in range(1, s.nz):
            self.copy_e(h, i, True).wait_send()

    @staticmethod
    def sems(heads, ny, nx, nz):
        out = [pltpu.SemaphoreType.DMA((heads,))] * 2
        for n in (ny - 1, nx, nz, nx):
            out += [pltpu.SemaphoreType.DMA((heads, n))] * 2
        return out


def bwd_kernel(counts, *refs):
    refs = list(refs)

    def take(n):
        out = refs[:n]
        del refs[:n]
        return out

    prefix_ref, proj_ref, conv_ref, do_ref, o_ref, lse_ref, normed_ref = take(7)
    part_refs = take(len(counts))
    gp_ref, sum_ref, own_ref = take(3)
    wide, qs, ks, vs, dos, delta, dq, dk, dv, gk, gv, gwide, gp_s, gpt, own_part = take(15)
    send, recv, gsend, grecv = take(4)
    bufs = take(5)
    sems = take(10)
    own_bufs = take(3)
    own_sems = take(10)
    heads, length, _ = qs.shape
    width = gwide.shape[1]
    blocks = dos.shape[1]
    rows = length//blocks
    prefix = prefix_ref[0]
    parts = []
    first = 0
    for ref, count in zip(part_refs, counts):
        parts.append((ref, first, count))
        first += count
    sums = Sums(parts, sum_ref, bufs, sems, blocks)
    own = OwnSums(sums, own_part, own_ref, own_bufs, own_sems)
    z, y, c, x = sums.me
    greet(sums.peers())
    sums.start()

    def block_copy(h, i, at):
        return remote(do_ref.at[i * heads + h], dos.at[h, at], send.at[h, i], recv.at[h, at], (i, 2 * y + c, x))

    for h in range(heads):
        for i in range(1, blocks):
            block_copy(h, (z + i) % blocks, z).start()
        dos[h, z] = do_ref[z * heads + h]

    def gp_copy(h, i, at):
        return remote(gpt.at[h, i], gp_ref.at[at * heads + h], gsend.at[h, i], grecv.at[h, at], (i, 2 * y + c, x))

    ahead = min(0, sums.chunks)
    for k in range(ahead):
        sums.stage_b(k)
    convolve(proj_ref, conv_ref, wide, (qs, ks, vs))

    def head(h, _):
        for i in range(1, blocks):
            there = (z + i) % blocks
            block_copy(h, there, there).wait_recv()
        for i in range(blocks):
            prod = dos[h, i].astype(F32) * o_ref[h, i].astype(F32)
            delta[i] = jnp.broadcast_to(jnp.sum(prod, axis=0, keepdims=True), (8, rows))
        dq[...] = jnp.zeros(dq.shape, F32)
        def kblock(j, _):
            t = h*blocks + j
            @pl.when(t + ahead < sums.chunks)
            def _():
                sums.stage_b(t + ahead)
            @pl.when((t > 0) & (t != 3))
            def _():
                sums.step(jnp.where(t < 3, t - 1, t - 2))
            for n, stage in enumerate(own.stages()[:3], 1):
                @pl.when((h > 0) & (j == n))
                def _():
                    stage(h - 1)
            kat = pl.ds(pl.multiple_of(j*rows, rows), rows)
            k = ks[h, kat]; v = vs[h, kat]
            dk[...] = jnp.zeros(dk.shape, F32)
            dv[...] = jnp.zeros(dv.shape, F32)
            def step(i, masked):
                qat = pl.ds(pl.multiple_of(i*rows, rows), rows)
                q = qs[h, qat]; do = dos[h, i]
                s = nt(k, q)
                p = jnp.exp(s - lse_ref[h, 0:1, qat])
                if masked:
                    p = jnp.where(mask_t(i, j, rows, prefix), p, 0.0)
                dv[...] += nt(p.astype(BF), do)
                dp = jnp.dot(v, do, preferred_element_type=F32)
                ds = (p*(dp - delta[i, 0:1])).astype(BF)
                dk[...] += jnp.dot(ds, q, preferred_element_type=F32)
                dq[qat] += tn(ds, k)
                return 0
            lax.fori_loop(j+1, blocks, lambda i, _: step(i, False), 0)
            lax.fori_loop(jnp.where(j < blocks//2, 0, j), j+1, lambda i, _: step(i, True), 0)
            gk[kat] = dk[...].astype(BF)
            gv[kat] = dv[...].astype(BF)
            return 0
        lax.fori_loop(0, blocks, kblock, 0)
        def fill(c, _):
            at = pl.ds(pl.multiple_of(c*rows, rows), rows)
            gq = (dq[at]*(HEAD_DIM**-0.5)).astype(BF)
            gwide[at] = jnp.concatenate([gq, gk[at], gv[at]], axis=1).astype(F32)
            return 0
        lax.fori_loop(0, blocks, fill, 0)
        taps = conv_ref[h]
        def out(i, total):
            base = pl.multiple_of(i*rows, rows)
            g = gwide[pl.ds(base, rows+8)]
            w = wide[h, pl.ds(base, rows+8)]
            g0 = g[:rows]
            gp = taps[0:1]*g0 + taps[1:2]*g[1:rows+1] + taps[2:3]*g[2:rows+2]
            gp_s[pl.ds(base, rows)] = gp.astype(BF)
            gpt[h, i] = jnp.transpose(gp).astype(BF)
            add = [jnp.sum(g0*w[8-t:8-t+rows], axis=0, keepdims=True) for t in range(3)]
            return tuple(a+b for a, b in zip(total, add))
        total = lax.fori_loop(0, blocks, out, tuple(jnp.zeros((1, width), F32) for _ in range(3)))
        @pl.when(h < heads - 1)
        def _():
            for i in range(1, blocks):
                gp_copy(h, (z + i) % blocks, z).start()
        gp_ref[z * heads + h] = gpt[h, z]
        grad = jnp.dot(normed_ref[...], gp_s[...], preferred_element_type=F32).astype(BF)
        shape = own_part.shape[1:]
        mine = grad.shape[0] // (16 * shape[0] * shape[1])
        grad = grad.reshape(shape[0] * shape[1], 2, 8 * mine, width)
        grad = jnp.concatenate([grad[:, 0], grad[:, 1]], axis=2)
        own_part[h, :, :, 0:mine] = grad.reshape(shape[0], shape[1], mine, 8, 2 * width)
        extra = jnp.concatenate(list(total) + [jnp.zeros((5, width), F32)], axis=0)
        extra = jnp.concatenate([extra, jnp.zeros((8, width), F32)], axis=1).astype(BF)
        own_part[h, :, :, mine] = jnp.broadcast_to(extra, shape[:2] + (8, 2 * width))
        for spare in range(mine + 1, shape[2]):
            own_part[h, :, :, spare] = jnp.zeros(shape[:2] + (8, 2 * width), BF)
        own.copy_a(h).start()
        return 0
    gwide[length:length+8] = jnp.zeros((8, width), F32)
    lax.fori_loop(0, heads, head, 0)
    steps = heads*blocks
    turns = steps - 2
    def rest(t, _):
        sums.stage_b(t)
        return 0
    lax.fori_loop(steps + ahead, sums.chunks, rest, 0)
    for n, stage in enumerate(own.stages()):
        sums.step(turns + n)
        stage(heads - 1)
    def forward(h, _):
        own.stage_f(h)
        return 0
    lax.fori_loop(0, heads - 1, forward, 0)
    count = len(own.stages())
    for n in range(count, blocks):
        gp_copy(heads - 1, (z + n) % blocks, z).start()
    def tail(t, _):
        sums.step(t)
        return 0
    lax.fori_loop(turns + count, max(sums.chunks + sums.LAGS[-1], turns + count), tail, 0)
    for n in range(1, blocks):
        gp_copy(heads - 1, (z + n) % blocks, z).start()
    sums.finish()
    def done(h, _):
        own.finish(h)
        for i in range(1, blocks):
            there = (z + i) % blocks
            block_copy(h, there, z).wait_send()
            gp_copy(h, there, there).wait_recv()
            gp_copy(h, there, z).wait_send()
        return 0
    lax.fori_loop(0, heads, done, 0)

def attention_bwd(prefix, proj, conv, do, o, lse, normed, parts, shape):
    length = proj.shape[0]
    heads, blocks = o.shape[:2]
    width = 3 * HEAD_DIM
    rows = length // blocks
    counts = tuple(part.shape[2] for part in parts)
    ny, _, _, units = parts[0].shape[:4]
    unit = parts[0].shape[4:]
    nx = shape["replica"]
    chunks = sum(counts)
    half = units // nx
    own_units = -(-(normed.shape[0] // (32 * ny) + 1) // nx) * nx
    own_unit = (8, 2 * width)
    vm = pl.BlockSpec(memory_space=pltpu.VMEM)
    dma = pltpu.SemaphoreType.DMA
    per = pltpu.VMEM((heads, length, HEAD_DIM), BF)
    return pl.pallas_call(
        functools.partial(bwd_kernel, counts),
        out_shape=(
            jax.ShapeDtypeStruct((heads * blocks, width, rows), BF),
            jax.ShapeDtypeStruct((chunks, units) + unit, BF),
            jax.ShapeDtypeStruct((heads, blocks, own_units) + own_unit, BF),
        ),
        in_specs=[pl.BlockSpec(memory_space=pltpu.SMEM)] + [vm]*(6 + len(parts)),
        out_specs=(vm, vm, vm),
        scratch_shapes=[pltpu.VMEM((heads, 8+length, width), F32), per, per, per, pltpu.VMEM(o.shape, BF), pltpu.VMEM((blocks, 8, rows), F32),
            pltpu.VMEM((length, HEAD_DIM), F32), pltpu.VMEM((rows, HEAD_DIM), F32), pltpu.VMEM((rows, HEAD_DIM), F32),
            pltpu.VMEM((length, HEAD_DIM), BF), pltpu.VMEM((length, HEAD_DIM), BF),
            pltpu.VMEM((length+8, width), F32), pltpu.VMEM((length, width), BF), pltpu.VMEM((heads, blocks, width, rows), BF),
            pltpu.VMEM((heads, ny, 2, own_units) + own_unit, BF)]
            + [dma((heads, blocks))] * 4
            + [pltpu.VMEM((chunks, ny, units) + unit, BF), pltpu.VMEM((chunks, ny - 1, units) + unit, BF),
            pltpu.VMEM((chunks, nx, half) + unit, BF), pltpu.VMEM((chunks, half // 2) + unit, BF), pltpu.VMEM((chunks, half // 4) + unit, BF)]
            + Sums.sems(chunks, ny, nx)
            + [pltpu.VMEM((heads, ny, own_units) + own_unit, BF), pltpu.VMEM((heads, ny - 1, own_units) + own_unit, BF),
            pltpu.VMEM((heads, nx, own_units // nx) + own_unit, BF)]
            + OwnSums.sems(heads, ny, nx, blocks),
        compiler_params=pltpu.CompilerParams(vmem_limit_bytes=67043328, collective_id=3, has_side_effects=True),
        cost_estimate=pl.CostEstimate(flops=10*heads*length*length*HEAD_DIM, bytes_accessed=length*width*4, transcendentals=heads*length*length),
        name="attention_bwd",
    )(prefix, proj, conv, do, o, lse, normed, *parts)


def finish_kernel(
    gp_ref, sum_ref, own_ref, wq_ref, tok_ref, gh_ref, small_all, w_qkv_ref, w_up_ref, small_ref,
    gin_out, qkv_out, out_out, up_out, down_out, conv_ref, ggain_ref,
    wq, tok, gh, w_qkv, w_up, gin, qkv, out, up, down, isem, osem,
):
    depth = w_qkv.shape[0]
    width = tok.shape[1]
    heads, blocks = own_ref.shape[:2]
    mine = depth // 8
    loads = [
        pltpu.make_async_copy(src, dst, isem.at[i])
        for i, (src, dst) in enumerate(
            ((wq_ref, wq), (tok_ref, tok), (gh_ref, gh), (w_up_ref, w_up), (w_qkv_ref, w_qkv))
        )
    ]
    for load in loads:
        load.start()
    stores = [
        pltpu.make_async_copy(src, dst, osem.at[i])
        for i, (src, dst) in enumerate(
            ((down, down_out), (out, out_out), (up, up_out), (qkv, qkv_out), (gin, gin_out))
        )
    ]
    ups = w_up.shape[1] // width
    downs = down.shape[0] // depth

    def rows_of(first, count):
        return sum_ref[first * mine : (first + count) * mine].reshape(count * depth, width).astype(F32)

    for i in range(downs):
        down[i * depth : (i + 1) * depth] = rows_of(ups + i, 1)
    stores[0].start()
    out[...] = rows_of(ups + downs, 1)
    stores[1].start()
    loads[3].wait()
    total = jnp.zeros((depth, 1), F32)
    for i in range(ups):
        at = slice(i * width, (i + 1) * width)
        grad = rows_of(i, 1)
        up[:, at] = grad
        total = total + jnp.sum(grad * w_up[:, at].astype(F32), axis=1, keepdims=True)
    stores[2].start()
    lanes = 3 * HEAD_DIM

    def grad_of(h, j):
        pair = own_ref[h, j, : mine // 2].reshape(depth // 2, 2 * lanes)
        return jnp.concatenate([pair[:, :lanes], pair[:, lanes:]], axis=0)

    grads = [grad_of(h, j) for j in range(blocks) for h in range(heads)]
    taps = [own_ref[h, j, mine // 2] for j in range(blocks) for h in range(heads)]

    def merge(pieces, p):
        return jnp.concatenate([piece[:, p * HEAD_DIM : (p + 1) * HEAD_DIM] for piece in pieces], axis=1)

    loads[4].wait()
    attn = jnp.zeros((depth, 1), F32)
    for p in range(3):
        at = slice(p * width, (p + 1) * width)
        grad = merge(grads, p).astype(F32)
        qkv[:, at] = grad
        attn = attn + jnp.sum(grad * w_qkv[:, at].astype(F32), axis=1, keepdims=True)
        conv_ref[:, at] = merge(taps, p).astype(F32)
    stores[3].start()
    columns = jnp.concatenate([jnp.broadcast_to(attn, (depth, 64)), jnp.broadcast_to(total, (depth, 64))], axis=1)
    both = jnp.transpose(columns)
    gains = small_ref[...].astype(F32)[0:2, :depth]
    ggain_ref[0:1] = both[0:1] / gains[0:1]
    ggain_ref[1:2] = both[64:65] / gains[1:2]
    for load in loads[:3]:
        load.wait()
    e1 = jnp.zeros(gh.shape, F32)
    for j in range(blocks):
        e1 = e1 + lax.dot_general(gp_ref[j], wq[j], (((0,), (1,)), ((), ())), preferred_element_type=F32)
    x = tok[...].astype(F32)
    scale = lax.rsqrt(jnp.mean(x * x, axis=-1, keepdims=True) + 1e-06)
    gone = jnp.concatenate([small_all[s, 0, 0:1, :depth] for s in range(small_all.shape[0])], axis=1)
    weighted = e1 * gone.astype(F32)
    back = scale * weighted - x * scale**3 * jnp.mean(weighted * x, axis=-1, keepdims=True)
    gin[...] = (gh[...] + back).astype(BF)
    stores[4].start()
    for store in stores:
        store.wait()


def finish(gp, sums, own_sums, wq, tok, gh, small_all, w_qkv, w_up, small, ff):
    depth, width = w_qkv.shape[0], tok.shape[1]
    vm = pl.BlockSpec(memory_space=pltpu.VMEM)
    hbm = pl.BlockSpec(memory_space=pl.ANY)
    dma = pltpu.SemaphoreType.DMA
    outs = [
        (tok.shape, BF),
        (w_qkv.shape, F32),
        ((depth, width), F32),
        (w_up.shape, F32),
        ((ff, width), F32),
    ]
    flat = [((8, w_qkv.shape[1]), F32), ((2, depth), F32)]
    kept = [(a.shape, a.dtype) for a in (wq, tok, gh, w_qkv, w_up)]
    return pl.pallas_call(
        finish_kernel,
        out_shape=[jax.ShapeDtypeStruct(*o) for o in outs + flat],
        in_specs=[vm] * 3 + [hbm] * 3 + [vm] + [hbm] * 2 + [vm],
        out_specs=[hbm] * 5 + [vm] * 2,
        scratch_shapes=[pltpu.VMEM(*o) for o in kept + outs] + [dma((5,)), dma((5,))],
        compiler_params=pltpu.CompilerParams(vmem_limit_bytes=60 * 1024 * 1024),
        name="finish",
    )(gp, sums, own_sums, wq, tok, gh, small_all, w_qkv, w_up, small)


def rms_scale(values):
    return lax.rsqrt(jnp.mean(values * values, axis=-1, keepdims=True) + 1e-06)


def norm_back(values, scale_rows, gain, upstream):
    weighted = upstream * gain
    grad_values = scale_rows * weighted - values * scale_rows**3 * jnp.mean(
        weighted * values, axis=-1, keepdims=True
    )
    return grad_values


def dot(a, b):
    return jnp.dot(a, b, preferred_element_type=F32)


def per_device(
    tokens, prefix_len, w_qkv, w_out, w_up, w_down, conv_w, gain_attn, gain_ffn, cotangent
):
    blocks = lax.axis_size("seq")
    me = lax.axis_index("seq")
    rows, width = tokens.shape[1:]
    own = HEADS // blocks * HEAD_DIM
    depth = w_qkv.shape[0]

    shards, copies = lax.axis_size("shard"), lax.axis_size("replica")
    heads = HEADS // blocks
    columns = w_qkv.reshape(depth, 3, blocks, heads, HEAD_DIM).transpose(2, 0, 3, 1, 4)
    gains = jnp.pad(jnp.stack([gain_attn, gain_ffn]), ((0, 0), (0, conv_w.shape[1] - depth)))
    small = jnp.pad(jnp.concatenate([gains, conv_w]), ((0, 3), (0, 0)))
    normed_all, projected, small_all, full_qkv, full_out, full_up = gather_all(
        tokens[0], small, columns.reshape(blocks, depth, 3 * own), w_out, w_up, blocks, shards
    )
    full_qkv = full_qkv.reshape(blocks, width, 3 * own)
    full_out = full_out.reshape(width, width)
    full_up = full_up.reshape(width, -1)
    full_gtwo = small_all[:, 0, 1, :depth].reshape(width).astype(F32)
    full_conv = small_all[:, 0, 2:5].transpose(1, 0, 2)
    own_conv = lax.dynamic_index_in_dim(full_conv.reshape(3, 3, blocks, heads, HEAD_DIM), me, 2, False)
    own_conv = own_conv.transpose(2, 0, 1, 3).reshape(heads, 3, 3 * HEAD_DIM).astype(F32)
    attended_own, logsum, attended, full_down = attention_fwd(
        prefix_len, projected, own_conv, w_down.reshape(-1, depth, width), blocks, shards
    )
    full_down = full_down.reshape(-1, width)
    attended = attended.reshape(width, rows)

    inputs = tokens[0].astype(F32)
    hidden = inputs + tn(attended, full_out)
    scale_two = rms_scale(hidden)
    normed_two_b = (hidden * scale_two * full_gtwo).astype(BF)
    positive = jnp.maximum(dot(normed_two_b, full_up), 0.0)
    active_b = (positive * positive).astype(BF)
    output = hidden + dot(active_b, full_down)

    incoming = cotangent[0]
    grad_upper_b = (dot(incoming, full_down.T) * 2.0 * positive).astype(BF)
    grad_normed_two = dot(grad_upper_b, full_up.T)
    grad_hidden = incoming.astype(F32) + norm_back(hidden, scale_two, full_gtwo, grad_normed_two)
    grad_hidden_b = grad_hidden.astype(BF)
    grad_attended = nt(full_out, grad_hidden_b).astype(BF)

    mine = depth // 8

    def cut(grad):
        return grad.astype(BF).reshape(shards // 2, 2, -1, mine, 8, width)

    parts = [
        cut(dot(normed_two_b.T, grad_upper_b[:, i * width : (i + 1) * width]))
        for i in range(grad_upper_b.shape[1] // width)
    ]
    parts += [cut(dot(active_b.T, incoming)), cut(dot(attended, grad_hidden_b))]
    pieces = sum(part.shape[2] for part in parts)
    if mine % (copies * blocks):
        units = -(-pieces * mine // (copies * blocks)) * copies * blocks
        joined = [part.reshape(shards // 2, 2, -1, 8, width) for part in parts]
        joined.append(jnp.zeros((shards // 2, 2, units - pieces * mine, 8, width), BF))
        joined = jnp.concatenate(joined, axis=2)
        parts = [joined.reshape(shards // 2, 2, -1, copies * blocks, 8, width)]

    grad_projected, sums, own_sums = attention_bwd(
        prefix_len, projected, own_conv, grad_attended.reshape(HEADS, HEAD_DIM, rows),
        attended_own, logsum, normed_all, parts, {"replica": copies},
    )
    grad_projected = grad_projected.reshape(blocks, 3 * own, rows)
    sums = sums.reshape(-1, 8, width)
    grad_input, total_qkv, total_out, total_up, total_down, total_conv, grad_gains = finish(
        grad_projected, sums, own_sums, full_qkv, tokens[0], grad_hidden, small_all,
        w_qkv, w_up, small, w_down.shape[0],
    )
    at = lax.axis_index("shard")
    return (
        output[None].astype(BF),
        grad_input[None],
        total_qkv,
        total_out,
        total_up,
        total_down,
        lax.dynamic_slice_in_dim(total_conv[:3], at * conv_w.shape[1], conv_w.shape[1], 1),
        grad_gains[0],
        grad_gains[1],
    )


def solution(mesh):
    placed = (
        P(("shard", "replica"), "seq", None),
        P(("shard", "replica")),
        P("shard", None),
        P("shard", None),
        P("shard", None),
        P("shard", None),
        P(None, "shard"),
        P("shard"),
        P("shard"),
        P(("shard", "replica"), "seq", None),
    )
    return jax.shard_map(
        per_device,
        mesh=mesh,
        in_specs=placed,
        out_specs=(
            P(("shard", "replica"), "seq", None),
            P(("shard", "replica"), "seq", None),
            P("shard", None),
            P("shard", None),
            P("shard", None),
            P("shard", None),
            P(None, "shard"),
            P("shard"),
            P("shard"),
        ),
        check_vma=False,
    )
```

```python
import functools

import jax
import jax.numpy as jnp
from jax import lax
from jax.experimental import pallas as pl
from jax.experimental.pallas import tpu as pltpu
from jax.sharding import PartitionSpec as P

HEADS = 12
HEAD_DIM=64
NEG=-1e30
F32=jnp.float32
BF=jnp.bfloat16

def nt(a,b):
    return lax.dot_general(a,b,(((1,),(1,)),((),())),preferred_element_type=F32)
def tn(a,b):
    return lax.dot_general(a,b,(((0,),(0,)),((),())),preferred_element_type=F32)

def convolve(proj_ref, conv_ref, wide, parts):
    length = proj_ref.shape[0]
    heads, _, width = wide.shape
    rows = min(512, length)
    for h in range(heads):
        wide[h, 0:8] = jnp.zeros((8, width), F32)
        for c in range(length//rows):
            wide[h, 8+c*rows:8+(c+1)*rows] = proj_ref[c*rows:(c+1)*rows, h*width:(h+1)*width].astype(F32)
    def body(c, _):
        base = pl.multiple_of(c*rows, rows)
        for h in range(heads):
            x = wide[h, pl.ds(base, rows+8)]
            taps = conv_ref[h]
            mixed = taps[0:1]*x[8:] + taps[1:2]*x[7:7+rows] + taps[2:3]*x[6:6+rows]
            for p, ref in enumerate(parts):
                piece = mixed[:, p*HEAD_DIM:(p+1)*HEAD_DIM].astype(BF)
                if p == 0:
                    piece = piece * jnp.asarray(HEAD_DIM**-0.5, BF)
                ref[h, pl.ds(base, rows)] = piece
        return 0
    lax.fori_loop(0, length//rows, body, 0)

def mask_t(i, j, rows, prefix):
    kpos = j*rows + lax.broadcasted_iota(jnp.int32, (rows, 1), 0)
    qpos = i*rows + lax.broadcasted_iota(jnp.int32, (1, rows), 1)
    return (kpos <= qpos) | ((kpos < prefix) & (qpos < prefix))

def mask_n(i, j, rows, prefix):
    qpos = i*rows + lax.broadcasted_iota(jnp.int32, (rows, 1), 0)
    kpos = j*rows + lax.broadcasted_iota(jnp.int32, (1, rows), 1)
    return (kpos <= qpos) | ((kpos < prefix) & (qpos < prefix))

MESH = pl.DeviceIdType.MESH


def remote(src, dst, send, recv, peer):
    return pltpu.make_async_remote_copy(
        src_ref=src, dst_ref=dst, send_sem=send, recv_sem=recv, device_id=peer, device_id_type=MESH
    )


def greet(peers):
    barrier = pltpu.get_barrier_semaphore()
    for peer in peers:
        pl.semaphore_signal(barrier, inc=1, device_id=peer, device_id_type=MESH)
    pl.semaphore_wait(barrier, len(peers))


def split_shard():
    s = lax.axis_index("shard")
    return lax.axis_index("seq"), s // 2, s % 2, lax.axis_index("replica")


class Gather:
    def __init__(self, src, dst, sems, major=False):
        self.src, self.dst, self.major = src, dst, major
        self.sy, self.ry, self.sk, self.rk, self.local = sems
        self.ny = dst.shape[1 if major else 0] // 2
        self.chunks = dst.shape[0 if major else 1]
        self.z, self.y, self.c, self.x = split_shard()
        self.core = (self.z, 2 * self.y + 1 - self.c, self.x)

    def py(self, i):
        return (self.y + i) % self.ny

    def dy(self, i):
        return (self.z, 2 * self.py(i) + self.c, self.x)

    def peers(self):
        return [self.core] + [self.dy(i) for i in range(1, self.ny)]

    def slot(self, p, core, j):
        shard = 2 * p + core
        return self.dst.at[j, shard] if self.major else self.dst.at[shard, j]

    def own(self):
        shard = 2 * self.y + self.c
        dst = self.dst.at[:, shard] if self.major else self.dst.at[shard]
        return pltpu.make_async_copy(self.src, dst, self.local.at[0])

    def over_y(self, j, i):
        slot = self.slot(self.y, self.c, j)
        return remote(self.src.at[j], slot, self.sy.at[j, self.py(i)], self.ry.at[j, self.y], self.dy(i))

    def to_core(self, j):
        slot = self.slot(self.y, self.c, j)
        return remote(self.src.at[j], slot, self.sk.at[j, self.y], self.rk.at[j, self.y], self.core)

    def pass_on(self, j, i):
        ref = self.slot(self.py(i), self.c, j)
        return remote(ref, ref, self.sk.at[j, self.py(i)], self.rk.at[j, self.py(i)], self.core)

    def send(self, j):
        for i in range(1, self.ny):
            self.over_y(j, i).start()
        self.to_core(j).start()

    def start(self):
        for j in range(self.chunks):
            self.send(j)
        self.own().start()

    def relay(self, j):
        for i in range(1, self.ny):
            ref = self.slot(self.py(i), self.c, j)
            remote(ref, ref, self.sy.at[j, self.py(i)], self.ry.at[j, self.py(i)], self.dy(i)).wait_recv()
            self.pass_on(j, i).start()

    def arrive(self, j):
        for i in range(self.ny):
            ref = self.slot(self.py(i), 1 - self.c, j)
            remote(ref, ref, self.sk.at[j, self.py(i)], self.rk.at[j, self.py(i)], self.core).wait_recv()

    def sent(self, j):
        self.to_core(j).wait_send()
        for i in range(1, self.ny):
            self.over_y(j, i).wait_send()
            self.pass_on(j, i).wait_send()

    def finish(self):
        self.own().wait()
        for j in range(self.chunks):
            self.arrive(j)
            self.sent(j)

    @staticmethod
    def sems(shards, chunks):
        return [pltpu.SemaphoreType.DMA((chunks, shards // 2))] * 4 + [pltpu.SemaphoreType.DMA((1,))]


def gather_kernel(
    tok_ref, small_ref, qkv_ref, out_ref, up_ref,
    normed_ref, proj_ref, small_all, qkv_all, out_all, up_all,
    toks, weight_s, wsem, sl, sr, rl, rr, *sems,
):
    blocks, rows, width = toks.shape
    _, shards, depth, columns = qkv_all.shape
    small, qkv, out, up = (
        Gather(src, dst, sems[5 * i : 5 * i + 5], major=i == 1)
        for i, (src, dst) in enumerate(
            ((small_ref, small_all), (qkv_ref, qkv_all), (out_ref, out_all), (up_ref, up_all))
        )
    )
    z, y, c, x = split_shard()
    shard = 2 * y + c
    left, right = (z - 1, shard, x), (z + 1, shard, x)
    has_left, has_right = z > 0, z < blocks - 1
    greet(small.peers() + [((z + i) % blocks, shard, x) for i in range(1, blocks)])

    def go_left(b, src):
        return remote(src, toks.at[b], sl.at[b], rr.at[b], left)

    def go_right(b, src):
        return remote(src, toks.at[b], sr.at[b], rl.at[b], right)

    small.start()
    qkv.send(z)
    qkv.own().start()

    @pl.when(has_left)
    def _():
        go_left(z, tok_ref).start()

    @pl.when(has_right)
    def _():
        go_right(z, tok_ref).start()

    out.start()
    up.start()
    for i in range(1, blocks):
        qkv.send((z + i) % blocks)
    small.relay(0)
    qkv.relay(z)
    small.finish()
    qkv.own().wait()
    qkv.arrive(z)
    gain = jnp.concatenate([small_all[s, 0, 0:1, :depth] for s in range(shards)], axis=1).astype(F32)
    fetch = pltpu.make_async_copy(qkv_all.at[z], weight_s, wsem.at[0])
    fetch.start()
    fetch.wait()
    weight = weight_s[...].reshape(shards * depth, columns)

    def project(b, values):
        at = pl.ds(pl.multiple_of(b * rows, rows), rows)
        values = values.astype(F32)
        scale = lax.rsqrt(jnp.mean(values * values, axis=-1, keepdims=True) + 1e-06)
        normed = values * scale * gain
        proj_ref[at] = jnp.dot(normed.astype(BF), weight, preferred_element_type=F32).astype(BF)
        normed_ref[:, at] = jnp.transpose(normed).astype(BF)

    project(z, tok_ref[...])
    for d in range(1, blocks):
        before, after = z - d, z + d

        @pl.when(before >= 0)
        def _():
            go_right(before, toks.at[before]).wait_recv()

            @pl.when(has_right)
            def _():
                go_right(before, toks.at[before]).start()

        @pl.when(after < blocks)
        def _():
            go_left(after, toks.at[after]).wait_recv()

            @pl.when(has_left)
            def _():
                go_left(after, toks.at[after]).start()

        @pl.when(before >= 0)
        def _():
            project(before, toks[before])

        @pl.when(after < blocks)
        def _():
            project(after, toks[after])

        if d == 1:
            out.relay(0)
        last = up.chunks * d // (blocks - 1)
        for j in range(up.chunks * (d - 1) // (blocks - 1), last):
            up.relay(j)

    for i in range(1, blocks):
        qkv.relay((z + i) % blocks)
    out.finish()
    up.finish()
    for i in range(1, blocks):
        qkv.arrive((z + i) % blocks)
    for j in range(blocks):
        qkv.sent(j)

    def sent(b, _):
        @pl.when((b <= z) & has_right)
        def _():
            go_right(b, toks.at[b]).wait_send()

        @pl.when((b >= z) & has_left)
        def _():
            go_left(b, toks.at[b]).wait_send()

        return 0

    lax.fori_loop(0, blocks, sent, 0)


def gather_all(tokens, small, qkv, out, up, blocks, shards):
    rows, width = tokens.shape
    vm = pl.BlockSpec(memory_space=pltpu.VMEM)
    hbm = pl.BlockSpec(memory_space=pl.ANY)
    cut = 4
    arrays = [
        small[None],
        qkv,
        out[None],
        up.reshape(cut, up.shape[0] // cut, up.shape[1]),
    ]
    dma = pltpu.SemaphoreType.DMA
    sems = [dma((blocks,))] * 4
    for array in arrays:
        sems += Gather.sems(shards, array.shape[0])
    return pl.pallas_call(
        gather_kernel,
        out_shape=[
            jax.ShapeDtypeStruct((width, blocks * rows), BF),
            jax.ShapeDtypeStruct((blocks * rows, qkv.shape[2]), BF),
        ]
        + [
            jax.ShapeDtypeStruct(
                (blocks, shards) + array.shape[1:] if i == 1 else (shards,) + array.shape, BF
            )
            for i, array in enumerate(arrays)
        ],
        in_specs=[vm] * 5,
        out_specs=[vm] * 3 + [hbm] * 3,
        scratch_shapes=[pltpu.VMEM((blocks, rows, width), BF), pltpu.VMEM((shards,) + qkv.shape[1:], BF), dma((1,))]
        + sems,
        compiler_params=pltpu.CompilerParams(
            vmem_limit_bytes=60 * 1024 * 1024, collective_id=4, has_side_effects=True
        ),
        name="gather_all",
    )(tokens, *arrays)


def fwd_kernel(prefix_ref, proj_ref, conv_ref, down_ref, own_ref, lse_ref, rows_ref, down_all, wide, qs, ks, vs, m_s, l_s, acc_s, o_s, r_s, send, recv, *sems):
    heads = qs.shape[0]
    length = proj_ref.shape[0]
    blocks = own_ref.shape[1]
    rows = length // blocks
    prefix = prefix_ref[0]
    z, s_at, x = lax.axis_index("seq"), lax.axis_index("shard"), lax.axis_index("replica")

    def block_copy(h, i, at):
        return remote(o_s.at[h, i], r_s.at[at * heads + h], send.at[h, i], recv.at[h, at], (i, s_at, x))

    down = Gather(down_ref, down_all, sems)
    greet([((z + i) % blocks, s_at, x) for i in range(1, blocks)] + down.peers())
    down.start()
    convolve(proj_ref, conv_ref, wide, (qs, ks, vs))
    def head(h, _):
        for j in range(down.chunks):
            @pl.when(h == 1 + (j + 1) // 2)
            def _():
                down.relay(j)
        def qblock(i, _):
            q = qs[h, pl.ds(pl.multiple_of(i*rows, rows), rows)]
            m_s[...] = jnp.full((1, rows), NEG, F32)
            l_s[...] = jnp.zeros((1, rows), F32)
            acc_s[...] = jnp.zeros((HEAD_DIM, rows), F32)
            def step(j, masked):
                at = pl.ds(pl.multiple_of(j*rows, rows), rows)
                s = nt(ks[h, at], q)
                if masked:
                    s = jnp.where(mask_t(i, j, rows, prefix), s, NEG)
                m_old = m_s[...]
                m_new = jnp.maximum(m_old, jnp.max(s, axis=0, keepdims=True))
                p = jnp.exp(s - m_new)
                a = jnp.exp(m_old - m_new)
                m_s[...] = m_new
                l_s[...] = a*l_s[...] + jnp.sum(p, axis=0, keepdims=True)
                acc_s[...] = a*acc_s[...] + tn(vs[h, at], p.astype(BF))
                return 0
            lax.fori_loop(0, i, lambda j, _: step(j, False), 0)
            lax.fori_loop(i, jnp.maximum(i+1, blocks//2), lambda j, _: step(j, True), 0)
            l = l_s[...]
            done = (acc_s[...]/l).astype(BF)
            o_s[h, i] = done
            own_ref[h, i] = done
            @pl.when(i != z)
            def _():
                block_copy(h, i, z).start()
            lse = m_s[...] + jnp.log(l)
            lse_ref[h, :, pl.ds(pl.multiple_of(i*rows, rows), rows)] = jnp.broadcast_to(lse, (8, rows))
            return 0
        lax.fori_loop(0, blocks, qblock, 0)
        r_s[z * heads + h] = o_s[h, z]
        return 0
    lax.fori_loop(0, heads, head, 0)
    for j in range(down.chunks):
        if 1 + (j + 1) // 2 >= heads:
            down.relay(j)
    down.finish()
    def finish(h, _):
        for i in range(1, blocks):
            there = (z + i) % blocks
            block_copy(h, there, there).wait_recv()
            block_copy(h, there, z).wait_send()
        return 0
    lax.fori_loop(0, heads, finish, 0)
    rows_ref[...] = r_s[...]

def attention_fwd(prefix, proj, conv, down, blocks, shards):
    length, width = proj.shape
    heads = width//(3*HEAD_DIM)
    rows = length // blocks
    vm = pl.BlockSpec(memory_space=pltpu.VMEM)
    own = (heads, blocks, HEAD_DIM, rows)
    every = (heads * blocks, HEAD_DIM, rows)
    return pl.pallas_call(
        fwd_kernel,
        out_shape=(jax.ShapeDtypeStruct(own, BF), jax.ShapeDtypeStruct((heads, 8, length), F32), jax.ShapeDtypeStruct(every, BF),
            jax.ShapeDtypeStruct((shards,) + down.shape, BF)),
        in_specs=[pl.BlockSpec(memory_space=pltpu.SMEM), vm, vm, vm],
        out_specs=(vm, vm, vm, pl.BlockSpec(memory_space=pl.ANY)),
        scratch_shapes=[pltpu.VMEM((heads, 8+length, 3*HEAD_DIM), F32)] + [pltpu.VMEM((heads, length, HEAD_DIM), BF)]*3 + [
            pltpu.VMEM((1,rows),F32), pltpu.VMEM((1,rows),F32), pltpu.VMEM((HEAD_DIM,rows),F32), pltpu.VMEM(own,BF), pltpu.VMEM(every,BF),
            pltpu.SemaphoreType.DMA((heads, blocks)), pltpu.SemaphoreType.DMA((heads, blocks))] + Gather.sems(shards, down.shape[0]),
        compiler_params=pltpu.CompilerParams(vmem_limit_bytes=60*1024*1024, collective_id=2, has_side_effects=True),
        cost_estimate=pl.CostEstimate(flops=4*heads*length*length*HEAD_DIM, bytes_accessed=length*width*2, transcendentals=heads*length*length),
        name="attention_fwd",
    )(prefix, proj, conv, down)

class Sums:
    def __init__(self, parts, out_ref, bufs, sems, nz):
        self.parts, self.out = parts, out_ref
        self.a, self.b, self.c, self.near, self.far = bufs
        self.sa, self.ra, self.sb, self.rb, self.sc, self.rc, self.sz, self.rz, self.sf, self.rf = sems
        self.chunks, self.ny = self.a.shape[:2]
        self.nx = self.c.shape[1]
        self.nz = nz
        self.half = self.c.shape[2]
        self.piece = self.half // nz
        self.me = split_shard()
        z, y, c, x = self.me
        self.core = (z, 2 * y + 1 - c, x)
        self.low, self.high = z % 2, z // 2
        self.one = (z + 1 - 2 * self.low, 2 * y + c, x)
        self.two = (z + 2 - 4 * self.high, 2 * y + c, x)

    def py(self, i):
        return (self.me[1] + i) % self.ny

    def px(self, i):
        return (self.me[3] + i) % self.nx

    def pz(self, i):
        return (self.me[0] + i) % self.nz

    def dy(self, i):
        z, y, c, x = self.me
        return (z, 2 * self.py(i) + c, x)

    def dx(self, i):
        z, y, c, x = self.me
        return (z, 2 * y + c, self.px(i))

    def dz(self, i):
        z, y, c, x = self.me
        return (self.pz(i), 2 * y + c, x)

    def peers(self):
        out = [self.core] + [self.dy(i) for i in range(1, self.ny)]
        out += [self.dx(i) for i in range(1, self.nx)]
        return out + [self.dz(i) for i in range(1, self.nz)]

    def copy_a(self, k, src):
        return remote(src, self.a.at[k], self.sa.at[k], self.ra.at[k], self.core)

    def start(self):
        c = self.me[2]
        for ref, first, count in self.parts:
            for j in range(count):
                src = ref.at[:, 1 - c, j]
                self.copy_a(first + j, src).start()

    def copy_b(self, k, i, there):
        slot = self.ny - i - 1 if there else i - 1
        return remote(self.a.at[k, self.py(i)], self.b.at[k, slot], self.sb.at[k, i - 1], self.rb.at[k, slot], self.dy(i))

    def stage_b(self, k):
        c = self.me[2]
        self.copy_a(k, self.a.at[k]).wait_recv()
        for i in list(range(1, self.ny)) + [0]:
            p = self.py(i)
            for ref, first, count in self.parts:
                @pl.when((k >= first) & (k < first + count))
                def _():
                    j = jnp.clip(k - first, 0, count - 1)
                    self.a[k, p] = (self.a[k, p].astype(F32) + ref[p, c, j].astype(F32)).astype(BF)
            if i:
                self.copy_b(k, i, True).start()

    def copy_c(self, k, i, there):
        slot = self.me[3] if there else self.px(i)
        src = self.a.at[k, self.me[1], pl.ds(self.px(i) * self.half, self.half)]
        return remote(src, self.c.at[k, slot], self.sc.at[k, self.px(i)], self.rc.at[k, slot], self.dx(i))

    def stage_c(self, k):
        y = self.me[1]
        total = self.a[k, y].astype(F32)
        for i in range(1, self.ny):
            self.copy_b(k, i, False).wait_recv()
            total = total + self.b[k, i - 1].astype(F32)
        for i in range(1, self.ny):
            self.copy_b(k, i, True).wait_send()
        self.a[k, y] = total.astype(BF)
        for i in range(1, self.nx):
            self.copy_c(k, i, True).start()

    def pieces(self, low, high, count):
        return pl.ds(self.me[3] * self.half + (2 * low + high) * self.piece, count * self.piece)

    def copy_z(self, k, stage):
        if stage == 0:
            src, dst, peer = self.a.at[k, self.me[1], self.pieces(1 - self.low, 0, 2)], self.near.at[k], self.one
        elif stage == 1:
            src, dst, peer = self.a.at[k, self.me[1], self.pieces(self.low, 1 - self.high, 1)], self.far.at[k], self.two
        elif stage == 2:
            src = dst = self.out.at[k, self.pieces(self.low, self.high, 1)]
            peer = self.two
        else:
            src = dst = self.out.at[k, self.pieces(self.low, 0, 2)]
            peer = self.one
        return remote(src, dst, self.sz.at[k, stage], self.rz.at[k, stage], peer)

    def stage_d(self, k):
        z, y, c, x = self.me
        mine = pl.ds(x * self.half, self.half)
        total = self.a[k, y, mine].astype(F32)
        for i in range(1, self.nx):
            self.copy_c(k, i, False).wait_recv()
            total = total + self.c[k, self.px(i)].astype(F32)
        for i in range(1, self.nx):
            self.copy_c(k, i, True).wait_send()
        self.a[k, y, mine] = total.astype(BF)
        self.copy_z(k, 0).start()

    def stage_near(self, k):
        y = self.me[1]
        self.copy_z(k, 0).wait_recv()
        self.copy_z(k, 0).wait_send()
        mine = self.pieces(self.low, 0, 2)
        self.a[k, y, mine] = (self.a[k, y, mine].astype(F32) + self.near[k].astype(F32)).astype(BF)
        self.copy_z(k, 1).start()

    def stage_far(self, k):
        self.copy_z(k, 1).wait_recv()
        mine = self.pieces(self.low, self.high, 1)
        self.out[k, mine] = (self.a[k, self.me[1], mine].astype(F32) + self.far[k].astype(F32)).astype(BF)
        self.copy_z(k, 2).start()

    def stage_back(self, k):
        ref = self.out.at[k, self.pieces(self.low, 1 - self.high, 1)]
        remote(ref, ref, self.sz.at[k, 2], self.rz.at[k, 2], self.two).wait_recv()
        self.copy_z(k, 3).start()

    def copy_f(self, k, i, there):
        slot = self.me[3] if there else self.px(i)
        ref = self.out.at[k, pl.ds(slot * self.half, self.half)]
        return remote(ref, ref, self.sf.at[k, self.px(i)], self.rf.at[k, slot], self.dx(i))

    def stage_f(self, k):
        ref = self.out.at[k, self.pieces(1 - self.low, 0, 2)]
        remote(ref, ref, self.sz.at[k, 3], self.rz.at[k, 3], self.one).wait_recv()
        for i in range(1, self.nx):
            self.copy_f(k, i, True).start()

    LAGS = (0, 1, 2, 3, 4, 5)

    def step(self, t):
        stages = (self.stage_c, self.stage_d, self.stage_near, self.stage_far, self.stage_back, self.stage_f)
        for lag, stage in zip(self.LAGS, stages):
            @pl.when((t >= lag) & (t < self.chunks + lag))
            def _():
                stage(t - lag)

    def finish(self):
        def body(k, _):
            for i in range(1, self.nx):
                self.copy_f(k, i, False).wait_recv()
            self.copy_a(k, self.a.at[k]).wait_send()
            for i in range(1, self.nx):
                self.copy_f(k, i, True).wait_send()
            for stage in range(1, 4):
                self.copy_z(k, stage).wait_send()
            return 0

        lax.fori_loop(0, self.chunks, body, 0)

    @staticmethod
    def sems(chunks, ny, nx):
        out = [pltpu.SemaphoreType.DMA((chunks,))] * 2
        for n in (ny - 1, nx, 4, nx):
            out += [pltpu.SemaphoreType.DMA((chunks, n))] * 2
        return out


class OwnSums:
    def __init__(self, sums, part, out, bufs, sems):
        self.s, self.part, self.out = sums, part, out
        self.a, self.b, self.c = bufs
        self.sa, self.ra, self.sb, self.rb, self.sc, self.rc, self.se, self.re, self.sf, self.rf = sems
        self.half = self.c.shape[2]

    def copy_a(self, h):
        return remote(self.part.at[h, :, 1 - self.s.me[2]], self.a.at[h], self.sa.at[h], self.ra.at[h], self.s.core)

    def copy_b(self, h, i, there):
        s = self.s
        slot = s.ny - i - 1 if there else i - 1
        return remote(self.a.at[h, s.py(i)], self.b.at[h, slot], self.sb.at[h, i - 1], self.rb.at[h, slot], s.dy(i))

    def copy_c(self, h, i, there):
        s = self.s
        slot = s.me[3] if there else s.px(i)
        src = self.a.at[h, s.me[1], pl.ds(s.px(i) * self.half, self.half)]
        return remote(src, self.c.at[h, slot], self.sc.at[h, s.px(i)], self.rc.at[h, slot], s.dx(i))

    def copy_e(self, h, i, there):
        s = self.s
        slot = s.me[0] if there else s.pz(i)
        ref = self.out.at[h, slot, pl.ds(s.me[3] * self.half, self.half)]
        return remote(ref, ref, self.se.at[h, s.pz(i)], self.re.at[h, slot], s.dz(i))

    def copy_f(self, h, i, there):
        s = self.s
        slot = s.me[3] if there else s.px(i)
        ref = self.out.at[h, :, pl.ds(slot * self.half, self.half)]
        return remote(ref, ref, self.sf.at[h, s.px(i)], self.rf.at[h, slot], s.dx(i))

    def stage_b(self, h):
        s = self.s
        self.copy_a(h).wait_recv()
        for i in list(range(1, s.ny)) + [0]:
            p = s.py(i)
            self.a[h, p] = (self.a[h, p].astype(F32) + self.part[h, p, s.me[2]].astype(F32)).astype(BF)
            if i:
                self.copy_b(h, i, True).start()

    def stage_c(self, h):
        s = self.s
        total = self.a[h, s.me[1]].astype(F32)
        for i in range(1, s.ny):
            self.copy_b(h, i, False).wait_recv()
            total = total + self.b[h, i - 1].astype(F32)
        self.a[h, s.me[1]] = total.astype(BF)
        for i in range(1, s.nx):
            self.copy_c(h, i, True).start()

    def stage_e(self, h):
        s = self.s
        mine = pl.ds(s.me[3] * self.half, self.half)
        total = self.a[h, s.me[1], mine].astype(F32)
        for i in range(1, s.nx):
            self.copy_c(h, i, False).wait_recv()
            total = total + self.c[h, s.px(i)].astype(F32)
        self.out[h, s.me[0], mine] = total.astype(BF)
        for i in range(1, s.nz):
            self.copy_e(h, i, True).start()

    def stage_f(self, h):
        s = self.s
        for i in range(1, s.nz):
            self.copy_e(h, i, False).wait_recv()
        for i in range(1, s.nx):
            self.copy_f(h, i, True).start()

    def stages(self):
        return (self.stage_b, self.stage_c, self.stage_e, self.stage_f)

    def finish(self, h):
        s = self.s
        self.copy_a(h).wait_send()
        for i in range(1, s.ny):
            self.copy_b(h, i, True).wait_send()
        for i in range(1, s.nx):
            self.copy_c(h, i, True).wait_send()
            self.copy_f(h, i, False).wait_recv()
            self.copy_f(h, i, True).wait_send()
        for i in range(1, s.nz):
            self.copy_e(h, i, True).wait_send()

    @staticmethod
    def sems(heads, ny, nx, nz):
        out = [pltpu.SemaphoreType.DMA((heads,))] * 2
        for n in (ny - 1, nx, nz, nx):
            out += [pltpu.SemaphoreType.DMA((heads, n))] * 2
        return out


def bwd_kernel(counts, *refs):
    refs = list(refs)

    def take(n):
        out = refs[:n]
        del refs[:n]
        return out

    prefix_ref, proj_ref, conv_ref, do_ref, o_ref, lse_ref, normed_ref = take(7)
    part_refs = take(len(counts))
    gp_ref, sum_ref, own_ref = take(3)
    wide, qs, ks, vs, dos, delta, dq, dk, dv, gk, gv, gwide, gp_s, gpt, own_part = take(15)
    send, recv, gsend, grecv = take(4)
    bufs = take(5)
    sems = take(10)
    own_bufs = take(3)
    own_sems = take(10)
    heads, length, _ = qs.shape
    width = gwide.shape[1]
    blocks = dos.shape[1]
    rows = length//blocks
    prefix = prefix_ref[0]
    parts = []
    first = 0
    for ref, count in zip(part_refs, counts):
        parts.append((ref, first, count))
        first += count
    sums = Sums(parts, sum_ref, bufs, sems, blocks)
    own = OwnSums(sums, own_part, own_ref, own_bufs, own_sems)
    z, y, c, x = sums.me
    greet(sums.peers())

    def block_copy(h, i, at):
        return remote(do_ref.at[i * heads + h], dos.at[h, at], send.at[h, i], recv.at[h, at], (i, 2 * y + c, x))

    for h in range(heads):
        for i in range(1, blocks):
            block_copy(h, (z + i) % blocks, z).start()
        dos[h, z] = do_ref[z * heads + h]
    sums.start()

    def gp_copy(h, i, at):
        return remote(gpt.at[h, i], gp_ref.at[at * heads + h], gsend.at[h, i], grecv.at[h, at], (i, 2 * y + c, x))

    ahead = min(0, sums.chunks)
    for k in range(ahead):
        sums.stage_b(k)
    convolve(proj_ref, conv_ref, wide, (qs, ks, vs))

    def head(h, _):
        for i in range(1, blocks):
            there = (z + i) % blocks
            block_copy(h, there, there).wait_recv()
        for i in range(blocks):
            prod = dos[h, i].astype(F32) * o_ref[h, i].astype(F32)
            delta[i] = jnp.broadcast_to(jnp.sum(prod, axis=0, keepdims=True), (8, rows))
        dq[...] = jnp.zeros(dq.shape, F32)
        def kblock(j, _):
            t = h*blocks + j
            @pl.when(t + ahead < sums.chunks)
            def _():
                sums.stage_b(t + ahead)
            @pl.when((t > 0) & (t != 3))
            def _():
                sums.step(jnp.where(t < 3, t - 1, t - 2))
            for n, stage in enumerate(own.stages()[:3], 1):
                @pl.when((h > 0) & (j == n))
                def _():
                    stage(h - 1)
            kat = pl.ds(pl.multiple_of(j*rows, rows), rows)
            k = ks[h, kat]; v = vs[h, kat]
            dk[...] = jnp.zeros(dk.shape, F32)
            dv[...] = jnp.zeros(dv.shape, F32)
            def step(i, masked):
                qat = pl.ds(pl.multiple_of(i*rows, rows), rows)
                q = qs[h, qat]; do = dos[h, i]
                s = nt(k, q)
                p = jnp.exp(s - lse_ref[h, 0:1, qat])
                if masked:
                    p = jnp.where(mask_t(i, j, rows, prefix), p, 0.0)
                dv[...] += nt(p.astype(BF), do)
                dp = jnp.dot(v, do, preferred_element_type=F32)
                ds = (p*(dp - delta[i, 0:1])).astype(BF)
                dk[...] += jnp.dot(ds, q, preferred_element_type=F32)
                dq[qat] += tn(ds, k)
                return 0
            lax.fori_loop(j+1, blocks, lambda i, _: step(i, False), 0)
            lax.fori_loop(jnp.where(j < blocks//2, 0, j), j+1, lambda i, _: step(i, True), 0)
            gk[kat] = dk[...].astype(BF)
            gv[kat] = dv[...].astype(BF)
            return 0
        lax.fori_loop(0, blocks, kblock, 0)
        def fill(c, _):
            at = pl.ds(pl.multiple_of(c*rows, rows), rows)
            gq = (dq[at]*(HEAD_DIM**-0.5)).astype(BF)
            gwide[at] = jnp.concatenate([gq, gk[at], gv[at]], axis=1).astype(F32)
            return 0
        lax.fori_loop(0, blocks, fill, 0)
        taps = conv_ref[h]
        def out(i, total):
            base = pl.multiple_of(i*rows, rows)
            g = gwide[pl.ds(base, rows+8)]
            w = wide[h, pl.ds(base, rows+8)]
            g0 = g[:rows]
            gp = taps[0:1]*g0 + taps[1:2]*g[1:rows+1] + taps[2:3]*g[2:rows+2]
            gp_s[pl.ds(base, rows)] = gp.astype(BF)
            gpt[h, i] = jnp.transpose(gp).astype(BF)
            add = [jnp.sum(g0*w[8-t:8-t+rows], axis=0, keepdims=True) for t in range(3)]
            return tuple(a+b for a, b in zip(total, add))
        total = lax.fori_loop(0, blocks, out, tuple(jnp.zeros((1, width), F32) for _ in range(3)))
        @pl.when(h < heads - 1)
        def _():
            for i in range(1, blocks):
                gp_copy(h, (z + i) % blocks, z).start()
        gp_ref[z * heads + h] = gpt[h, z]
        grad = jnp.dot(normed_ref[...], gp_s[...], preferred_element_type=F32).astype(BF)
        shape = own_part.shape[1:]
        mine = grad.shape[0] // (16 * shape[0] * shape[1])
        grad = grad.reshape(shape[0] * shape[1], 2, 8 * mine, width)
        grad = jnp.concatenate([grad[:, 0], grad[:, 1]], axis=2)
        own_part[h, :, :, 0:mine] = grad.reshape(shape[0], shape[1], mine, 8, 2 * width)
        extra = jnp.concatenate(list(total) + [jnp.zeros((5, width), F32)], axis=0)
        extra = jnp.concatenate([extra, jnp.zeros((8, width), F32)], axis=1).astype(BF)
        own_part[h, :, :, mine] = jnp.broadcast_to(extra, shape[:2] + (8, 2 * width))
        for spare in range(mine + 1, shape[2]):
            own_part[h, :, :, spare] = jnp.zeros(shape[:2] + (8, 2 * width), BF)
        own.copy_a(h).start()
        return 0
    gwide[length:length+8] = jnp.zeros((8, width), F32)
    lax.fori_loop(0, heads, head, 0)
    steps = heads*blocks
    turns = steps - 2
    def rest(t, _):
        sums.stage_b(t)
        return 0
    lax.fori_loop(steps + ahead, sums.chunks, rest, 0)
    for n, stage in enumerate(own.stages()):
        sums.step(turns + n)
        stage(heads - 1)
    for n in range(1, blocks):
        gp_copy(heads - 1, (z + n) % blocks, z).start()
    def forward(h, _):
        own.stage_f(h)
        return 0
    lax.fori_loop(0, heads - 1, forward, 0)
    count = len(own.stages())
    for n in range(count, blocks):
        gp_copy(heads - 1, (z + n) % blocks, z).start()
    def tail(t, _):
        sums.step(t)
        return 0
    lax.fori_loop(turns + count, max(sums.chunks + sums.LAGS[-1], turns + count), tail, 0)
    sums.finish()
    def done(h, _):
        own.finish(h)
        for i in range(1, blocks):
            there = (z + i) % blocks
            block_copy(h, there, z).wait_send()
            gp_copy(h, there, there).wait_recv()
            gp_copy(h, there, z).wait_send()
        return 0
    lax.fori_loop(0, heads, done, 0)

def attention_bwd(prefix, proj, conv, do, o, lse, normed, parts, shape):
    length = proj.shape[0]
    heads, blocks = o.shape[:2]
    width = 3 * HEAD_DIM
    rows = length // blocks
    counts = tuple(part.shape[2] for part in parts)
    ny, _, _, units = parts[0].shape[:4]
    unit = parts[0].shape[4:]
    nx = shape["replica"]
    chunks = sum(counts)
    half = units // nx
    own_units = -(-(normed.shape[0] // (32 * ny) + 1) // nx) * nx
    own_unit = (8, 2 * width)
    vm = pl.BlockSpec(memory_space=pltpu.VMEM)
    dma = pltpu.SemaphoreType.DMA
    per = pltpu.VMEM((heads, length, HEAD_DIM), BF)
    return pl.pallas_call(
        functools.partial(bwd_kernel, counts),
        out_shape=(
            jax.ShapeDtypeStruct((heads * blocks, width, rows), BF),
            jax.ShapeDtypeStruct((chunks, units) + unit, BF),
            jax.ShapeDtypeStruct((heads, blocks, own_units) + own_unit, BF),
        ),
        in_specs=[pl.BlockSpec(memory_space=pltpu.SMEM)] + [vm]*(6 + len(parts)),
        out_specs=(vm, vm, vm),
        scratch_shapes=[pltpu.VMEM((heads, 8+length, width), F32), per, per, per, pltpu.VMEM(o.shape, BF), pltpu.VMEM((blocks, 8, rows), F32),
            pltpu.VMEM((length, HEAD_DIM), F32), pltpu.VMEM((rows, HEAD_DIM), F32), pltpu.VMEM((rows, HEAD_DIM), F32),
            pltpu.VMEM((length, HEAD_DIM), BF), pltpu.VMEM((length, HEAD_DIM), BF),
            pltpu.VMEM((length+8, width), F32), pltpu.VMEM((length, width), BF), pltpu.VMEM((heads, blocks, width, rows), BF),
            pltpu.VMEM((heads, ny, 2, own_units) + own_unit, BF)]
            + [dma((heads, blocks))] * 4
            + [pltpu.VMEM((chunks, ny, units) + unit, BF), pltpu.VMEM((chunks, ny - 1, units) + unit, BF),
            pltpu.VMEM((chunks, nx, half) + unit, BF), pltpu.VMEM((chunks, half // 2) + unit, BF), pltpu.VMEM((chunks, half // 4) + unit, BF)]
            + Sums.sems(chunks, ny, nx)
            + [pltpu.VMEM((heads, ny, own_units) + own_unit, BF), pltpu.VMEM((heads, ny - 1, own_units) + own_unit, BF),
            pltpu.VMEM((heads, nx, own_units // nx) + own_unit, BF)]
            + OwnSums.sems(heads, ny, nx, blocks),
        compiler_params=pltpu.CompilerParams(vmem_limit_bytes=67043328, collective_id=3, has_side_effects=True),
        cost_estimate=pl.CostEstimate(flops=10*heads*length*length*HEAD_DIM, bytes_accessed=length*width*4, transcendentals=heads*length*length),
        name="attention_bwd",
    )(prefix, proj, conv, do, o, lse, normed, *parts)


def finish_kernel(
    gp_ref, sum_ref, own_ref, wq_ref, tok_ref, gh_ref, small_all, w_qkv_ref, w_up_ref, small_ref,
    gin_out, qkv_out, out_out, up_out, down_out, conv_ref, ggain_ref,
    wq, tok, gh, w_qkv, w_up, gin, qkv, out, up, down, isem, osem,
):
    depth = w_qkv.shape[0]
    width = tok.shape[1]
    heads, blocks = own_ref.shape[:2]
    mine = depth // 8
    loads = [
        pltpu.make_async_copy(src, dst, isem.at[i])
        for i, (src, dst) in enumerate(
            ((wq_ref, wq), (tok_ref, tok), (gh_ref, gh), (w_up_ref, w_up), (w_qkv_ref, w_qkv))
        )
    ]
    for load in loads:
        load.start()
    stores = [
        pltpu.make_async_copy(src, dst, osem.at[i])
        for i, (src, dst) in enumerate(
            ((down, down_out), (out, out_out), (up, up_out), (qkv, qkv_out), (gin, gin_out))
        )
    ]
    ups = w_up.shape[1] // width
    downs = down.shape[0] // depth

    def rows_of(first, count):
        return sum_ref[first * mine : (first + count) * mine].reshape(count * depth, width).astype(F32)

    for i in range(downs):
        down[i * depth : (i + 1) * depth] = rows_of(ups + i, 1)
    stores[0].start()
    out[...] = rows_of(ups + downs, 1)
    stores[1].start()
    loads[3].wait()
    total = jnp.zeros((depth, 1), F32)
    for i in range(ups):
        at = slice(i * width, (i + 1) * width)
        grad = rows_of(i, 1)
        up[:, at] = grad
        total = total + jnp.sum(grad * w_up[:, at].astype(F32), axis=1, keepdims=True)
    stores[2].start()
    lanes = 3 * HEAD_DIM

    def grad_of(h, j):
        pair = own_ref[h, j, : mine // 2].reshape(depth // 2, 2 * lanes)
        return jnp.concatenate([pair[:, :lanes], pair[:, lanes:]], axis=0)

    grads = [grad_of(h, j) for j in range(blocks) for h in range(heads)]
    taps = [own_ref[h, j, mine // 2] for j in range(blocks) for h in range(heads)]

    def merge(pieces, p):
        return jnp.concatenate([piece[:, p * HEAD_DIM : (p + 1) * HEAD_DIM] for piece in pieces], axis=1)

    loads[4].wait()
    attn = jnp.zeros((depth, 1), F32)
    for p in range(3):
        at = slice(p * width, (p + 1) * width)
        grad = merge(grads, p).astype(F32)
        qkv[:, at] = grad
        attn = attn + jnp.sum(grad * w_qkv[:, at].astype(F32), axis=1, keepdims=True)
        conv_ref[:, at] = merge(taps, p).astype(F32)
    stores[3].start()
    columns = jnp.concatenate([jnp.broadcast_to(attn, (depth, 64)), jnp.broadcast_to(total, (depth, 64))], axis=1)
    both = jnp.transpose(columns)
    gains = small_ref[...].astype(F32)[0:2, :depth]
    ggain_ref[0:1] = both[0:1] / gains[0:1]
    ggain_ref[1:2] = both[64:65] / gains[1:2]
    for load in loads[:3]:
        load.wait()
    e1 = jnp.zeros(gh.shape, F32)
    for j in range(blocks):
        e1 = e1 + lax.dot_general(gp_ref[j], wq[j], (((0,), (1,)), ((), ())), preferred_element_type=F32)
    x = tok[...].astype(F32)
    scale = lax.rsqrt(jnp.mean(x * x, axis=-1, keepdims=True) + 1e-06)
    gone = jnp.concatenate([small_all[s, 0, 0:1, :depth] for s in range(small_all.shape[0])], axis=1)
    weighted = e1 * gone.astype(F32)
    back = scale * weighted - x * scale**3 * jnp.mean(weighted * x, axis=-1, keepdims=True)
    gin[...] = (gh[...] + back).astype(BF)
    stores[4].start()
    for store in stores:
        store.wait()


def finish(gp, sums, own_sums, wq, tok, gh, small_all, w_qkv, w_up, small, ff):
    depth, width = w_qkv.shape[0], tok.shape[1]
    vm = pl.BlockSpec(memory_space=pltpu.VMEM)
    hbm = pl.BlockSpec(memory_space=pl.ANY)
    dma = pltpu.SemaphoreType.DMA
    outs = [
        (tok.shape, BF),
        (w_qkv.shape, F32),
        ((depth, width), F32),
        (w_up.shape, F32),
        ((ff, width), F32),
    ]
    flat = [((8, w_qkv.shape[1]), F32), ((2, depth), F32)]
    kept = [(a.shape, a.dtype) for a in (wq, tok, gh, w_qkv, w_up)]
    return pl.pallas_call(
        finish_kernel,
        out_shape=[jax.ShapeDtypeStruct(*o) for o in outs + flat],
        in_specs=[vm] * 3 + [hbm] * 3 + [vm] + [hbm] * 2 + [vm],
        out_specs=[hbm] * 5 + [vm] * 2,
        scratch_shapes=[pltpu.VMEM(*o) for o in kept + outs] + [dma((5,)), dma((5,))],
        compiler_params=pltpu.CompilerParams(vmem_limit_bytes=60 * 1024 * 1024),
        name="finish",
    )(gp, sums, own_sums, wq, tok, gh, small_all, w_qkv, w_up, small)


def rms_scale(values):
    return lax.rsqrt(jnp.mean(values * values, axis=-1, keepdims=True) + 1e-06)


def norm_back(values, scale_rows, gain, upstream):
    weighted = upstream * gain
    grad_values = scale_rows * weighted - values * scale_rows**3 * jnp.mean(
        weighted * values, axis=-1, keepdims=True
    )
    return grad_values


def dot(a, b):
    return jnp.dot(a, b, preferred_element_type=F32)


def per_device(
    tokens, prefix_len, w_qkv, w_out, w_up, w_down, conv_w, gain_attn, gain_ffn, cotangent
):
    blocks = lax.axis_size("seq")
    me = lax.axis_index("seq")
    rows, width = tokens.shape[1:]
    own = HEADS // blocks * HEAD_DIM
    depth = w_qkv.shape[0]

    shards, copies = lax.axis_size("shard"), lax.axis_size("replica")
    heads = HEADS // blocks
    columns = w_qkv.reshape(depth, 3, blocks, heads, HEAD_DIM).transpose(2, 0, 3, 1, 4)
    gains = jnp.pad(jnp.stack([gain_attn, gain_ffn]), ((0, 0), (0, conv_w.shape[1] - depth)))
    small = jnp.pad(jnp.concatenate([gains, conv_w]), ((0, 3), (0, 0)))
    normed_all, projected, small_all, full_qkv, full_out, full_up = gather_all(
        tokens[0], small, columns.reshape(blocks, depth, 3 * own), w_out, w_up, blocks, shards
    )
    full_qkv = full_qkv.reshape(blocks, width, 3 * own)
    full_out = full_out.reshape(width, width)
    full_up = full_up.reshape(width, -1)
    full_gtwo = small_all[:, 0, 1, :depth].reshape(width).astype(F32)
    full_conv = small_all[:, 0, 2:5].transpose(1, 0, 2)
    own_conv = lax.dynamic_index_in_dim(full_conv.reshape(3, 3, blocks, heads, HEAD_DIM), me, 2, False)
    own_conv = own_conv.transpose(2, 0, 1, 3).reshape(heads, 3, 3 * HEAD_DIM).astype(F32)
    attended_own, logsum, attended, full_down = attention_fwd(
        prefix_len, projected, own_conv, w_down.reshape(-1, depth, width), blocks, shards
    )
    full_down = full_down.reshape(-1, width)
    attended = attended.reshape(width, rows)

    inputs = tokens[0].astype(F32)
    hidden = inputs + tn(attended, full_out)
    scale_two = rms_scale(hidden)
    normed_two_b = (hidden * scale_two * full_gtwo).astype(BF)
    positive = jnp.maximum(dot(normed_two_b, full_up), 0.0)
    active_b = (positive * positive).astype(BF)
    output = hidden + dot(active_b, full_down)

    incoming = cotangent[0]
    grad_upper_b = (dot(incoming, full_down.T) * 2.0 * positive).astype(BF)
    grad_normed_two = dot(grad_upper_b, full_up.T)
    grad_hidden = incoming.astype(F32) + norm_back(hidden, scale_two, full_gtwo, grad_normed_two)
    grad_hidden_b = grad_hidden.astype(BF)
    grad_attended = nt(full_out, grad_hidden_b).astype(BF)

    mine = depth // 8

    def cut(grad):
        return grad.astype(BF).reshape(shards // 2, 2, -1, mine, 8, width)

    parts = [
        cut(dot(normed_two_b.T, grad_upper_b[:, i * width : (i + 1) * width]))
        for i in range(grad_upper_b.shape[1] // width)
    ]
    parts += [cut(dot(active_b.T, incoming)), cut(dot(attended, grad_hidden_b))]
    pieces = sum(part.shape[2] for part in parts)
    if mine % (copies * blocks):
        units = -(-pieces * mine // (copies * blocks)) * copies * blocks
        joined = [part.reshape(shards // 2, 2, -1, 8, width) for part in parts]
        joined.append(jnp.zeros((shards // 2, 2, units - pieces * mine, 8, width), BF))
        joined = jnp.concatenate(joined, axis=2)
        parts = [joined.reshape(shards // 2, 2, -1, copies * blocks, 8, width)]

    grad_projected, sums, own_sums = attention_bwd(
        prefix_len, projected, own_conv, grad_attended.reshape(HEADS, HEAD_DIM, rows),
        attended_own, logsum, normed_all, parts, {"replica": copies},
    )
    grad_projected = grad_projected.reshape(blocks, 3 * own, rows)
    sums = sums.reshape(-1, 8, width)
    grad_input, total_qkv, total_out, total_up, total_down, total_conv, grad_gains = finish(
        grad_projected, sums, own_sums, full_qkv, tokens[0], grad_hidden, small_all,
        w_qkv, w_up, small, w_down.shape[0],
    )
    at = lax.axis_index("shard")
    return (
        output[None].astype(BF),
        grad_input[None],
        total_qkv,
        total_out,
        total_up,
        total_down,
        lax.dynamic_slice_in_dim(total_conv[:3], at * conv_w.shape[1], conv_w.shape[1], 1),
        grad_gains[0],
        grad_gains[1],
    )


def solution(mesh):
    placed = (
        P(("shard", "replica"), "seq", None),
        P(("shard", "replica")),
        P("shard", None),
        P("shard", None),
        P("shard", None),
        P("shard", None),
        P(None, "shard"),
        P("shard"),
        P("shard"),
        P(("shard", "replica"), "seq", None),
    )
    return jax.shard_map(
        per_device,
        mesh=mesh,
        in_specs=placed,
        out_specs=(
            P(("shard", "replica"), "seq", None),
            P(("shard", "replica"), "seq", None),
            P("shard", None),
            P("shard", None),
            P("shard", None),
            P("shard", None),
            P(None, "shard"),
            P("shard"),
            P("shard"),
        ),
        check_vma=False,
    )
```
